256 devices in a mesh: gz: 8 (over x, core), gx: 4 (over y), gy: 8 (over z).
Axes of the slice: x: 4, y: 4, z: 8, core: 2. Of those that a mesh axis runs over, the one named last changes fastest.
Arguments:
- right_side: float32 [64, 3, 64, 1024], P('gz', None, 'gy', 'gx'), may hold values from -6 to 6
- start_field: float32 [64, 3, 64, 1024], P('gz', None, 'gy', 'gx'), may hold values from -6 to 6
- layer_material: int32 [64], P('gz'), may hold values from 0 to 7
- stiffness: float32 [8, 3, 3, 3], replicated, may hold values from -0.2 to 8, as said below
- line_factors: float32 [8, 3, 3, 3], replicated, may hold values from -0.05 to 1
Outputs:
- solution_field: float32 [64, 3, 64, 1024], P('gz', None, 'gy', 'gx')
- final_residual: float32 [64, 3, 64, 1024], P('gz', None, 'gy', 'gx')
The draws below stay inside these ranges and needn't reach their ends.
Inputs may be any that keep to these rules, and one draw needn't show every extreme that they name: `stiffness`: diagonal blocks dominate each row over the lateral and vertical couplings of the stencil.
All inputs are finite; a program needn't handle non-finite values.
Results may differ from the reference program's by a relative error of at most 0.0001.
Values sent between devices are 32-bit elements; how exact they have to be, the bound alone decides.
No kernel may reach another device: no remote copies, remote signals or barrier semaphores. Data moves between devices by JAX's collectives and lax.ppermute only.
A program may use at most 64 MiB of HBM per device.

```python
import jax
import jax.numpy as jnp
from jax import lax

MATS = 8
SWEEPS = 3
NZ = 64
NY = 64
NX = 1024


def symmetric_noise(key, scale):
    noise = jax.random.uniform(key, (MATS, 3, 3), jnp.float32, -1.0, 1.0)
    both = 0.5 * (noise + jnp.swapaxes(noise, 1, 2))
    return scale * both * (1.0 - jnp.eye(3, dtype=jnp.float32))


def draw_stiffness(key, part):
    keys = jax.random.split(jax.random.fold_in(key, 11), 6)
    eye = jnp.eye(3, dtype=jnp.float32)
    lateral_rate = jax.random.uniform(keys[0], (MATS, 3), jnp.float32, 0.1, 0.3)
    vertical_rate = jax.random.uniform(keys[1], (MATS, 3), jnp.float32, 0.5, 1.5)
    margin = jax.random.uniform(keys[2], (MATS, 3), jnp.float32, 0.3, 1.0)
    lateral_off = symmetric_noise(keys[3], 0.03)
    vertical_off = symmetric_noise(keys[4], 0.1)
    diagonal_off = symmetric_noise(keys[5], 0.2)
    lateral_block = eye * lateral_rate[:, :, None] + lateral_off
    vertical_block = eye * vertical_rate[:, :, None] + vertical_off
    diagonal_value = 4.0 * lateral_rate + 2.0 * vertical_rate + margin
    diagonal_value = diagonal_value + 4.0 * jnp.sum(jnp.abs(lateral_off), axis=2)
    diagonal_value = diagonal_value + 2.0 * jnp.sum(jnp.abs(vertical_off), axis=2)
    diagonal_value = diagonal_value + jnp.sum(jnp.abs(diagonal_off), axis=2)
    diagonal_block = eye * diagonal_value[:, :, None] + diagonal_off
    return jnp.stack([diagonal_block, lateral_block, vertical_block], axis=1)


def draw_line_factors(key, part):
    keys = jax.random.split(jax.random.fold_in(key, 23), 8)
    eye = jnp.eye(3, dtype=jnp.float32)
    fast_comp = jax.random.randint(keys[0], (), 0, 3)
    quick_mask = jnp.arange(3)[None, :] == fast_comp

    def rates(first_key, second_key):
        slow = 1.0 - jnp.exp(jax.random.uniform(first_key, (MATS, 3), jnp.float32, jnp.log(1.0 / NZ), jnp.log(3.0 / NZ)))
        quick = 1.0 - jax.random.uniform(second_key, (MATS, 3), jnp.float32, 0.03, 0.08)
        return jnp.where(quick_mask, quick, slow)
    forward_rate = rates(keys[1], keys[2])
    backward_rate = rates(keys[3], keys[4])

    def multiplier(rate, sub_key):
        root = jnp.sqrt(1.0 - rate)
        coupling = 0.1 * root[:, :, None] * symmetric_noise(sub_key, 1.0) * root[:, None, :]
        return eye * rate[:, :, None] + coupling
    forward_block = multiplier(forward_rate, keys[5])
    backward_block = multiplier(backward_rate, keys[6])
    gain = 1.5 * (1.0 - forward_rate) * (1.0 - backward_rate)
    pivot_block = gain[:, :, None] * (eye + symmetric_noise(keys[7], 0.1))
    return jnp.stack([pivot_block, forward_block, backward_block], axis=1)


def touch_ends(values, stream_key, smallest, high):
    longest = values.shape.index(max(values.shape))
    spots = []
    for shift in (0, 1):
        where = [jax.random.randint(jax.random.fold_in(stream_key, axis), (), 0, length) for axis, length in enumerate(values.shape)]
        where[longest] = (where[longest] + shift) % values.shape[longest]
        spots.append(tuple(where))
    return values.at[spots[0]].set(smallest).at[spots[1]].set(high)


def levels(key, dims, shards, low, top_value):
    factor_of = 1.0
    for axis_at, parts in shards:
        steps = jax.random.uniform(jax.random.fold_in(jax.random.fold_in(key, 6), axis_at), (parts,), jnp.float32, low / len(shards), top_value / len(shards))
        factor_of = factor_of * jnp.repeat(jnp.exp(steps), dims[axis_at] // parts).reshape((-1,) + (1,) * (len(dims) - 1 - axis_at))
    return factor_of


def scatter_about(key, extent, spread, bound, cuts=(), kind=jnp.bfloat16):
    level = levels(key, extent, cuts, -0.22, 0.18) if cuts else 1.0
    drawn = jax.random.normal(key, extent, jnp.float32) * spread * level
    return jnp.minimum(jnp.maximum(drawn, -bound), bound).astype(kind)


def setup_inputs(seed: int = 0) -> dict:
    seeds = jax.random.split(jax.random.key(seed), 6)
    right_side = scatter_about(seeds[0], (NZ, 3, NY, NX), 1.0, 6.0, ((0, 8), (2, 8), (3, 4)), jnp.float32)
    start_field = scatter_about(seeds[1], (NZ, 3, NY, NX), 1.0, 6.0, ((0, 8), (2, 8), (3, 4)), jnp.float32)
    layer_material = touch_ends(jax.random.randint(seeds[2], (NZ,), 0, MATS), jax.random.fold_in(seeds[2], 1), 0, MATS - 1).astype(jnp.int32)
    stiffness = draw_stiffness(jax.random.fold_in(seeds[5], 71), 0)
    line_factors = draw_line_factors(jax.random.fold_in(seeds[5], 71), 0)
    return dict(right_side=right_side, start_field=start_field, layer_material=layer_material, stiffness=stiffness, line_factors=line_factors)


def apply_block(blocks, field):
    columns = []
    for row_index in range(3):
        summed = blocks[..., row_index, 0, None, None] * field[..., 0, :, :]
        for col_index in (1, 2):
            summed = summed + blocks[..., row_index, col_index, None, None] * field[..., col_index, :, :]
        columns.append(summed)
    return jnp.stack(columns, axis=-3)


def operate(field, diag_block, lateral_block, vertical_block):
    padded = jnp.pad(field, ((1, 1), (0, 0), (1, 1), (1, 1)))
    lateral = padded[1:-1, :, 1:-1, 2:] + padded[1:-1, :, 1:-1, :-2]
    lateral = lateral + padded[1:-1, :, 2:, 1:-1] + padded[1:-1, :, :-2, 1:-1]
    vertical = padded[2:, :, 1:-1, 1:-1] + padded[:-2, :, 1:-1, 1:-1]
    return apply_block(diag_block, field) - apply_block(lateral_block, lateral) - apply_block(vertical_block, vertical)


def line_solve(resid, factor_blocks):
    weighted = apply_block(factor_blocks[:, 0], resid)

    def advance(carry, item):
        multiplier, source = item
        nxt = source + apply_block(multiplier, carry)
        return nxt, nxt

    start = jnp.zeros(resid.shape[1:], jnp.float32)
    _, upward = lax.scan(advance, start, (factor_blocks[:, 1], weighted))
    _, downward = lax.scan(advance, start, (factor_blocks[:, 2], upward), reverse=True)
    return downward


def reference(right_side, start_field, layer_material, stiffness, line_factors):
    fine_sten = stiffness[layer_material]
    coarse_ids = layer_material[0::2]
    coarse_sten = stiffness[coarse_ids]
    fine_fac = line_factors[layer_material]
    coarse_fac = line_factors[coarse_ids]
    fine_args = (fine_sten[:, 0], fine_sten[:, 1], fine_sten[:, 2])
    coarse_args = (coarse_sten[:, 0], coarse_sten[:, 1], 0.25 * coarse_sten[:, 2])
    field = start_field
    for counter in range(SWEEPS):
        field = field + line_solve(right_side - operate(field, *fine_args), fine_fac)
    resid = right_side - operate(field, *fine_args)
    paired = resid.reshape(resid.shape[0] // 2, 2, 3, resid.shape[2], resid.shape[3])
    coarse_rhs = paired[:, 0] + paired[:, 1]
    correction = line_solve(coarse_rhs, coarse_fac)
    for counter in range(SWEEPS - 1):
        correction = correction + line_solve(coarse_rhs - operate(correction, *coarse_args), coarse_fac)
    solution_field = field + jnp.repeat(correction, 2, axis=0)
    final_residual = right_side - operate(solution_field, *fine_args)
    return solution_field, final_residual
```

```python
import jax
import jax.numpy as jnp
from jax import lax
from jax.experimental import pallas as pl
from jax.experimental.pallas import tpu as pltpu
from jax.sharding import PartitionSpec as P

F32 = jnp.float32
BF16 = jnp.bfloat16
HALO = 7
XH = 8
XT = 32
XW = XT + 2 * XH
YT = 8
YW = YT + 2 * HALO
NZ = 64
NC = NZ // 2
VMEM = pl.BlockSpec(memory_space=pltpu.VMEM)
SMEM = pl.BlockSpec(memory_space=pltpu.SMEM)


def params():
    return pltpu.CompilerParams(vmem_limit_bytes=40 * 1024 * 1024)


def swap_blocks(tile):
    sub = lax.broadcasted_iota(jnp.int32, tile.shape, 1)
    blk = lax.broadcasted_iota(jnp.int32, tile.shape, 2) // 32
    for bit in (1, 2, 4):
        up = pltpu.roll(pltpu.roll(tile, 8 - bit, axis=1), 32 * bit, axis=2)
        down = pltpu.roll(pltpu.roll(tile, bit, axis=1), 256 - 32 * bit, axis=2)
        in_sub = (sub & bit) != 0
        in_blk = (blk & bit) != 0
        tile = jnp.where(in_sub == in_blk, tile, jnp.where(in_blk, up, down))
    return tile


def pack_kernel(load_ref, start_ref, out_ref):
    for f, ref in enumerate((load_ref, start_ref)):
        for c in range(3):
            tile = swap_blocks(ref[:, c])
            for z in range(8):
                for h in range(2):
                    at = h * 48 + f * 24 + c * 8 + z
                    out_ref[pl.ds(at, 8, stride=96), :] = tile[z, :, h * 128 : h * 128 + 128]


def unpack_kernel(got_ref, start_ref, field_ref, resid_ref):
    for f, ref in enumerate((field_ref, resid_ref)):
        for c in range(3):
            halves = []
            for h in range(2):
                at = h * 48 + f * 24 + c * 8
                rows = [got_ref[pl.ds(at + z, 8, stride=96), :] for z in range(8)]
                halves.append(jnp.stack(rows, axis=0))
            tile = swap_blocks(jnp.concatenate(halves, axis=2))
            if f == 0:
                tile = tile + start_ref[:, c]
            ref[:, c] = tile


def turn_kernel(got_ref, own_ref, low_ref, high_ref):
    halves = []
    for h in range(2):
        rows = [got_ref[g, h * 48 + q * 8 : h * 48 + q * 8 + 8] for q in range(6) for g in range(8)]
        halves.append(jnp.transpose(jnp.concatenate(rows, axis=0)))
    turned = jnp.concatenate(halves, axis=0).reshape(YT, XT, 384)
    own_ref[...] = turned
    low_ref[...] = turned[:HALO]
    high_ref[...] = turned[YT - HALO :]


def sides_kernel(own_ref, above_ref, below_ref, left_ref, right_ref):
    for ref, cols in ((left_ref, slice(0, XH)), (right_ref, slice(XT - XH, XT))):
        ref[0:HALO] = above_ref[:, cols]
        ref[HALO : HALO + YT] = own_ref[:, cols]
        ref[HALO + YT :] = below_ref[:, cols]


def split(value):
    high = value.astype(BF16)
    return high, (value - high.astype(F32)).astype(BF16)


def line_rows(mats_ref, factor_ref, dst_ref, layers, step):
    lane = lax.broadcasted_iota(jnp.int32, (1, 3 * layers), 1)

    def up(z, state):
        base = mats_ref[z * step] * 27
        new = []
        for i in range(3):
            row = jnp.zeros((1, 3 * layers), F32)
            for j in range(3):
                row = jnp.where(lane == j * layers + z, factor_ref[base + i * 3 + j], row)
            for j in range(3):
                row = row + factor_ref[base + 9 + i * 3 + j] * state[j]
            dst_ref[pl.ds(i * layers + z, 1), :] = row
            new.append(row)
        return tuple(new)

    def down(t, state):
        z = layers - 1 - t
        base = mats_ref[z * step] * 27
        new = []
        for i in range(3):
            row = dst_ref[pl.ds(i * layers + z, 1), :]
            for j in range(3):
                row = row + factor_ref[base + 18 + i * 3 + j] * state[j]
            dst_ref[pl.ds(i * layers + z, 1), :] = row
            new.append(row)
        return tuple(new)

    zero = tuple(jnp.zeros((1, 3 * layers), F32) for _ in range(3))
    lax.fori_loop(0, layers, up, zero, unroll=8)
    lax.fori_loop(0, layers, down, zero, unroll=8)


def couple(sten, which, blocks):
    out = []
    for i in range(3):
        total = None
        for j in range(3):
            at = which * 9 + i * 3 + j
            term = sten[:, at : at + 1] * blocks[j]
            total = term if total is None else total + term
        out.append(total)
    return out


def above_below(block):
    row = lax.broadcasted_iota(jnp.int32, block.shape, 0)
    n = block.shape[0]
    low = jnp.where(row == 0, 0.0, pltpu.roll(block, 1, axis=0))
    high = jnp.where(row == n - 1, 0.0, pltpu.roll(block, n - 1, axis=0))
    return low + high


def store_split(ref, at, rows):
    value = jnp.transpose(jnp.concatenate(rows, axis=0))
    high, low = split(value)
    ref[0, :, at : at + value.shape[1]] = high
    ref[1, :, at : at + value.shape[1]] = low


def setup_kernel(
    mats_ref, factor_ref, sten_ref, fine_ref, coarse_ref, first_ref, line_ref, cline_ref
):
    sten = sten_ref[...]
    line_rows(mats_ref, factor_ref, line_ref, NZ, 1)
    line_rows(mats_ref, factor_ref, cline_ref, NC, 2)

    row = lax.broadcasted_iota(jnp.int32, (NZ, 256), 0)
    lane = lax.broadcasted_iota(jnp.int32, (NZ, 256), 1)
    comp = lane // NZ - 1
    layer = lane % NZ
    same = (row == layer) & (comp >= 0)
    near = ((row == layer + 1) | (row == layer - 1)) & (comp >= 0)

    def picked(which, i):
        at = which * 9 + i * 3
        return jnp.where(
            comp == 0,
            sten[:, at : at + 1],
            jnp.where(comp == 1, sten[:, at + 1 : at + 2], sten[:, at + 2 : at + 3]),
        )

    store_split(
        first_ref,
        0,
        [jnp.where(same, picked(0, i), jnp.where(near, -picked(2, i), 0.0)) for i in range(3)],
    )
    store_split(first_ref, 256, [jnp.where(same, picked(1, i), 0.0) for i in range(3)])

    def level(sten_part, scale, ref, layers):
        blocks = [ref[i * layers : (i + 1) * layers, :] for i in range(3)]
        lateral = couple(sten_part, 1, blocks)
        diag = couple(sten_part, 0, blocks)
        vert = couple(sten_part, 2, [above_below(block) for block in blocks])
        if scale is not None:
            vert = [scale * part for part in vert]
        wide = blocks[0].shape
        r = lax.broadcasted_iota(jnp.int32, wide, 0)
        q = lax.broadcasted_iota(jnp.int32, wide, 1)
        kept = [
            jnp.where(q == r + i * layers, 1.0, 0.0) - (diag[i] - vert[i]) for i in range(3)
        ]
        return blocks, kept, lateral

    blocks, kept, lateral = level(sten, None, line_ref, NZ)
    store_split(fine_ref, 0, blocks)
    store_split(fine_ref, 256, kept)
    store_split(fine_ref, 512, lateral)

    def exact(a, b):
        return jnp.dot(a, b, precision=lax.Precision.HIGHEST, preferred_element_type=F32)

    layer_at = lax.broadcasted_iota(jnp.int32, (NC, NZ), 1) // 2
    pairs = (lax.broadcasted_iota(jnp.int32, (NC, NZ), 0) == layer_at).astype(F32)
    layer_at = lax.broadcasted_iota(jnp.int32, (NZ, NC), 0) // 2
    repeats = (lax.broadcasted_iota(jnp.int32, (NZ, NC), 1) == layer_at).astype(F32)

    def paired(part):
        return [exact(pairs, block) for block in part]

    store_split(fine_ref, 768, paired(kept))
    store_split(fine_ref, 896, paired(lateral))

    coarse_sten = sten_ref[pl.ds(0, NC, stride=2), :]
    cblocks, ckept, clateral = level(coarse_sten, 0.25, cline_ref, NC)
    store_split(coarse_ref, 0, ckept)
    store_split(coarse_ref, 128, clateral)
    spread = [exact(repeats, block) for block in cblocks]
    diag = couple(sten, 0, spread)
    vert = couple(sten, 2, [above_below(block) for block in spread])
    store_split(coarse_ref, 256, spread)
    store_split(coarse_ref, 512, [d - v for d, v in zip(diag, vert)])
    store_split(coarse_ref, 768, couple(sten, 1, spread))


def cycle_kernel(
    own_ref,
    above_ref,
    below_ref,
    left_ref,
    right_ref,
    fine_ref,
    coarse_ref,
    first_ref,
    out_ref,
    x_ref,
    r_ref,
    keep_ref,
    side_ref,
    sum_ref,
    rc_ref,
    ckeep_ref,
    cside_ref,
    csum_ref,
):
    gz, gx, gy = (lax.axis_index(axis) for axis in ("gz", "gx", "gy"))
    at_left = (gx == 0) & (gz == 0)
    at_right = (gx == lax.axis_size("gx") - 1) & (gz == lax.axis_size("gz") - 1)
    at_top = gy == 0
    at_bottom = gy == lax.axis_size("gy") - 1

    x_ref[:, 0:XH] = left_ref[...]
    x_ref[:, XH + XT :] = right_ref[...]
    x_ref[0:HALO, XH : XH + XT] = above_ref[...]
    x_ref[HALO : HALO + YT, XH : XH + XT] = own_ref[...]
    x_ref[HALO + YT :, XH : XH + XT] = below_ref[...]

    def product(halves, w_ref, at, width):
        high, low = halves
        wh = w_ref[0, :, at : at + width]
        wl = w_ref[1, :, at : at + width]

        def dot(a, b):
            return jnp.dot(a, b, preferred_element_type=F32)

        return dot(high, wh) + (dot(high, wl) + dot(low, wh))

    def chunks(lo, hi, size):
        return [(y, min(y + size, hi)) for y in range(lo, hi, size)]

    def apply(src, lanes, lo, hi, w_ref, jobs, size=4):
        for a, b in chunks(lo, hi, size):
            value = src[a:b, :, lanes].reshape((b - a) * XW, -1)
            halves = split(value)
            for at, width, dst in jobs:
                dst[a:b] = product(halves, w_ref, at, width).reshape(b - a, XW, width)

    def spread(side, y):
        mid = side[y]
        return (side[y - 1] + side[y + 1]) + (
            pltpu.roll(mid, 1, axis=0) + pltpu.roll(mid, XW - 1, axis=0)
        )

    def clear(ref, lo, hi):
        width = ref.shape[2]

        @pl.when(at_left)
        def _():
            ref[lo:hi, 0:XH] = jnp.zeros((hi - lo, XH, width), F32)

        @pl.when(at_right)
        def _():
            ref[lo:hi, XH + XT :] = jnp.zeros((hi - lo, XH, width), F32)

        if lo < HALO:

            @pl.when(at_top)
            def _():
                ref[lo:HALO] = jnp.zeros((HALO - lo, XW, width), F32)

        if hi > HALO + YT:

            @pl.when(at_bottom)
            def _():
                ref[HALO + YT : hi] = jnp.zeros((hi - HALO - YT, XW, width), F32)

    own = slice(HALO, HALO + YT)
    inner = slice(XH, XH + XT)
    every = slice(None)

    apply(
        x_ref, slice(128, 384), 0, YW, first_ref, [(0, 192, keep_ref), (256, 192, side_ref)]
    )
    for y in range(1, YW - 1):
        r_ref[y] = (x_ref[y, :, 0:192] - keep_ref[y]) + spread(side_ref, y)
    clear(r_ref, 1, YW - 1)
    sum_ref[...] = r_ref[own, inner]

    for sweep in (1, 2):
        lo, hi = sweep, YW - sweep
        apply(r_ref, every, lo, hi, fine_ref, [(256, 192, keep_ref), (512, 192, side_ref)])
        for y in range(lo + 1, hi - 1):
            r_ref[y] = keep_ref[y] + spread(side_ref, y)
        clear(r_ref, lo + 1, hi - 1)
        sum_ref[...] += r_ref[own, inner]

    apply(r_ref, every, 3, YW - 3, fine_ref, [(768, 96, ckeep_ref), (896, 96, cside_ref)])
    apply(
        r_ref, every, HALO - 1, HALO + YT + 1, fine_ref, [(256, 192, keep_ref), (512, 192, side_ref)], 5
    )
    for y in range(4, YW - 4):
        rc_ref[y] = ckeep_ref[y] + spread(cside_ref, y)
    clear(rc_ref, 4, YW - 4)
    for y in range(HALO, HALO + YT):
        r_ref[y] = keep_ref[y] + spread(side_ref, y)
    csum_ref[HALO - 1 : HALO + YT + 1] = rc_ref[HALO - 1 : HALO + YT + 1]

    for sweep in (4, 5):
        lo, hi = sweep, YW - sweep
        apply(rc_ref, every, lo, hi, coarse_ref, [(0, 96, ckeep_ref), (128, 96, cside_ref)], 5)
        for y in range(lo + 1, hi - 1):
            rc_ref[y] = ckeep_ref[y] + spread(cside_ref, y)
        clear(rc_ref, lo + 1, hi - 1)
        csum_ref[HALO - 1 : HALO + YT + 1] += rc_ref[HALO - 1 : HALO + YT + 1]

    apply(
        csum_ref,
        every,
        HALO - 1,
        HALO + YT + 1,
        coarse_ref,
        [(512, 192, keep_ref), (768, 192, side_ref)],
        5,
    )
    resid = []
    for y in range(HALO, HALO + YT):
        resid.append(((r_ref[y] - keep_ref[y]) + spread(side_ref, y))[inner])
    resid = jnp.concatenate(resid, axis=0)
    change = product(split(sum_ref[...].reshape(YT * XT, 192)), fine_ref, 0, 192)
    change = change + product(
        split(csum_ref[own, inner].reshape(YT * XT, 96)), coarse_ref, 256, 192
    )
    for f, value in enumerate((change, resid)):
        turned = jnp.transpose(value)
        for c in range(3):
            for g in range(8):
                rows = turned[c * NZ + g * 8 : c * NZ + g * 8 + 8]
                for h in range(2):
                    at = h * 48 + f * 24 + c * 8
                    out_ref[g, at : at + 8, :] = rows[:, h * 128 : h * 128 + 128]


def shape(*dims, dtype=F32):
    return jax.ShapeDtypeStruct(dims, dtype)


def on_device(right_side, start_field, layer_material, stiffness, line_factors):
    size_y = lax.axis_size("gy")
    mats = lax.all_gather(layer_material, "gz", axis=0, tiled=True)
    packed = pl.pallas_call(
        pack_kernel,
        out_shape=shape(768, 128),
        in_specs=[VMEM, VMEM],
        out_specs=VMEM,
        compiler_params=params(),
        name="pack",
    )(right_side, start_field)
    got = lax.all_to_all(packed.reshape(8, 96, 128), "gz", 0, 0, tiled=True)

    onehot = (mats[:, None] == jnp.arange(stiffness.shape[0])[None, :]).astype(F32)
    sten = jnp.sum(onehot[:, :, None] * stiffness.reshape(1, -1, 27), axis=1)
    sten = jnp.pad(sten, ((0, 0), (0, 128 - 27)))
    fine, coarse, first = pl.pallas_call(
        setup_kernel,
        out_shape=(
            shape(2, 192, 1024, dtype=BF16),
            shape(2, 96, 1024, dtype=BF16),
            shape(2, 256, 512, dtype=BF16),
        ),
        in_specs=[SMEM, SMEM, VMEM],
        out_specs=(VMEM, VMEM, VMEM),
        scratch_shapes=[
            pltpu.VMEM((192, 192), F32),
            pltpu.VMEM((96, 96), F32),
        ],
        compiler_params=params(),
        name="setup",
    )(mats, line_factors.reshape(-1), sten)

    own, low, high = pl.pallas_call(
        turn_kernel,
        out_shape=(shape(YT, XT, 384), shape(HALO, XT, 384), shape(HALO, XT, 384)),
        in_specs=[VMEM],
        out_specs=(VMEM, VMEM, VMEM),
        compiler_params=params(),
        name="turn",
    )(got)
    ahead = [(i, i + 1) for i in range(size_y - 1)]
    above = lax.ppermute(high, "gy", ahead)
    below = lax.ppermute(low, "gy", [(b, a) for a, b in ahead])
    to_left, to_right = pl.pallas_call(
        sides_kernel,
        out_shape=(shape(YW, XH, 384), shape(YW, XH, 384)),
        in_specs=[VMEM, VMEM, VMEM],
        out_specs=(VMEM, VMEM),
        compiler_params=params(),
        name="sides",
    )(own, above, below)
    count_x, count_z = lax.axis_size("gx"), lax.axis_size("gz")
    along = [(i % count_z) * count_x + i // count_z for i in range(count_x * count_z)]
    ahead = list(zip(along[:-1], along[1:]))
    left = lax.ppermute(to_right, ("gz", "gx"), ahead)
    right = lax.ppermute(to_left, ("gz", "gx"), [(b, a) for a, b in ahead])

    out = pl.pallas_call(
        cycle_kernel,
        out_shape=shape(8, 96, 128),
        in_specs=[VMEM] * 8,
        out_specs=VMEM,
        scratch_shapes=[
            pltpu.VMEM((YW, XW, 384), F32),
            pltpu.VMEM((YW, XW, 192), F32),
            pltpu.VMEM((YW, XW, 192), F32),
            pltpu.VMEM((YW, XW, 192), F32),
            pltpu.VMEM((YT, XT, 192), F32),
            pltpu.VMEM((YW, XW, 96), F32),
            pltpu.VMEM((YW, XW, 96), F32),
            pltpu.VMEM((YW, XW, 96), F32),
            pltpu.VMEM((YW, XW, 96), F32),
        ],
        compiler_params=params(),
        name="cycle",
    )(own, above, below, left, right, fine, coarse, first)
    back = lax.all_to_all(out, "gz", 0, 0, tiled=True)
    return pl.pallas_call(
        unpack_kernel,
        out_shape=(shape(8, 3, 8, 256), shape(8, 3, 8, 256)),
        in_specs=[VMEM, VMEM],
        out_specs=(VMEM, VMEM),
        compiler_params=params(),
        name="unpack",
    )(back.reshape(768, 128), start_field)


def solution(mesh):
    return jax.shard_map(
        on_device,
        mesh=mesh,
        in_specs=(P("gz", None, "gy", "gx"), P("gz", None, "gy", "gx"), P("gz"), P(), P()),
        out_specs=(P("gz", None, "gy", "gx"), P("gz", None, "gy", "gx")),
        check_vma=False,
    )
```

```python
import jax
import jax.numpy as jnp
from jax import lax
from jax.experimental import pallas as pl
from jax.experimental.pallas import tpu as pltpu
from jax.sharding import PartitionSpec as P

F32 = jnp.float32
BF16 = jnp.bfloat16
HALO = 7
XH = 8
XT = 32
XW = XT + 2 * XH
YT = 8
YW = YT + 2 * HALO
ROWS = 104
NZ = 64
NC = NZ // 2
VMEM = pl.BlockSpec(memory_space=pltpu.VMEM)
HBM = pl.BlockSpec(memory_space=pltpu.HBM)
SMEM = pl.BlockSpec(memory_space=pltpu.SMEM)


def params():
    return pltpu.CompilerParams(vmem_limit_bytes=40 * 1024 * 1024)


def swap_blocks(tile):
    sub = lax.broadcasted_iota(jnp.int32, tile.shape, 1)
    blk = lax.broadcasted_iota(jnp.int32, tile.shape, 2) // 32
    for bit in (1, 2, 4):
        up = pltpu.roll(pltpu.roll(tile, 8 - bit, axis=1), 32 * bit, axis=2)
        down = pltpu.roll(pltpu.roll(tile, bit, axis=1), 256 - 32 * bit, axis=2)
        in_sub = (sub & bit) != 0
        in_blk = (blk & bit) != 0
        tile = jnp.where(in_sub == in_blk, tile, jnp.where(in_blk, up, down))
    return tile


def fetches(pairs, sems):
    copies = [pltpu.make_async_copy(src, dst, sems.at[i]) for i, (src, dst) in enumerate(pairs)]
    for copy in copies:
        copy.start()
    return copies


def pack_kernel(load_hbm, start_hbm, mats_hbm, out_ref, in_ref, mats_ref, sems, mats_sem):
    mats_copy = pltpu.make_async_copy(mats_hbm, mats_ref, mats_sem)
    mats_copy.start()
    order = [(f, c) for f in range(2) for c in range(3)]
    copies = fetches(
        [((load_hbm, start_hbm)[f].at[:, c], in_ref.at[i]) for i, (f, c) in enumerate(order)], sems
    )
    for i, (f, c) in enumerate(order):
        copies[i].wait()
        tile = swap_blocks(in_ref[i])
        for z in range(8):
            for h in range(2):
                at = h * 48 + f * 24 + c * 8 + z
                out_ref[pl.ds(at, 8, stride=ROWS), :] = tile[z, :, h * 128 : h * 128 + 128]
    mats_copy.wait()
    lane = lax.broadcasted_iota(jnp.int32, (8, 128), 1)
    ids = jnp.zeros((8, 128), jnp.int32)
    for z in range(8):
        ids = jnp.where(lane == z, mats_ref[z], ids)
    for k in range(8):
        out_ref[k * ROWS + 96 : k * ROWS + 104, :] = ids.astype(F32)


def unpack_kernel(got_ref, start_ref, field_hbm, resid_hbm, out_ref, sems):
    copies = []
    for f, ref in enumerate((field_hbm, resid_hbm)):
        for c in range(3):
            halves = []
            for h in range(2):
                at = h * 48 + f * 24 + c * 8
                rows = [got_ref[pl.ds(at + z, 8, stride=96), :] for z in range(8)]
                halves.append(jnp.stack(rows, axis=0))
            tile = swap_blocks(jnp.concatenate(halves, axis=2))
            if f == 0:
                tile = tile + start_ref[:, c]
            i = f * 3 + c
            out_ref[i] = tile
            copy = pltpu.make_async_copy(out_ref.at[i], ref.at[:, c], sems.at[i])
            copy.start()
            copies.append(copy)
    for copy in copies:
        copy.wait()


def turn_kernel(got_ref, own_ref, low_ref, high_ref):
    halves = []
    for h in range(2):
        rows = [got_ref[g, h * 48 + q * 8 : h * 48 + q * 8 + 8] for q in range(6) for g in range(8)]
        halves.append(jnp.transpose(jnp.concatenate(rows, axis=0)))
    turned = jnp.concatenate(halves, axis=0).reshape(YT, XT, 384)
    own_ref[...] = turned
    low_ref[...] = turned[:HALO]
    high_ref[...] = turned[YT - HALO :]


def sides_kernel(own_ref, above_ref, below_ref, after_ref, left_ref, right_ref):
    for ref, cols in ((left_ref, slice(0, XH)), (right_ref, slice(XT - XH, XT))):
        ref[0:HALO] = above_ref[:, cols]
        ref[HALO : HALO + YT] = own_ref[:, cols]
        ref[HALO + YT :] = below_ref[:, cols]


def split(value):
    high = value.astype(BF16)
    return high, (value - high.astype(F32)).astype(BF16)


def line_rows(mats_ref, factor_ref, dst_ref, layers, step):
    lane = lax.broadcasted_iota(jnp.int32, (1, 3 * layers), 1)

    def up(z, state):
        base = mats_ref[z * step] * 27
        new = []
        for i in range(3):
            row = jnp.zeros((1, 3 * layers), F32)
            for j in range(3):
                row = jnp.where(lane == j * layers + z, factor_ref[base + i * 3 + j], row)
            for j in range(3):
                row = row + factor_ref[base + 9 + i * 3 + j] * state[j]
            dst_ref[pl.ds(i * layers + z, 1), :] = row
            new.append(row)
        return tuple(new)

    def down(t, state):
        z = layers - 1 - t
        base = mats_ref[z * step] * 27
        new = []
        for i in range(3):
            row = dst_ref[pl.ds(i * layers + z, 1), :]
            for j in range(3):
                row = row + factor_ref[base + 18 + i * 3 + j] * state[j]
            dst_ref[pl.ds(i * layers + z, 1), :] = row
            new.append(row)
        return tuple(new)

    zero = tuple(jnp.zeros((1, 3 * layers), F32) for _ in range(3))
    lax.fori_loop(0, layers, up, zero, unroll=8)
    lax.fori_loop(0, layers, down, zero, unroll=8)


def couple(sten, which, blocks):
    out = []
    for i in range(3):
        total = None
        for j in range(3):
            at = which * 9 + i * 3 + j
            term = sten[:, at : at + 1] * blocks[j]
            total = term if total is None else total + term
        out.append(total)
    return out


def above_below(block):
    row = lax.broadcasted_iota(jnp.int32, block.shape, 0)
    n = block.shape[0]
    low = jnp.where(row == 0, 0.0, pltpu.roll(block, 1, axis=0))
    high = jnp.where(row == n - 1, 0.0, pltpu.roll(block, n - 1, axis=0))
    return low + high


def store_split(ref, at, rows):
    value = jnp.transpose(jnp.concatenate(rows, axis=0))
    high, low = split(value)
    ref[0, :, at : at + value.shape[1]] = high
    ref[1, :, at : at + value.shape[1]] = low


def setup_kernel(
    mats_ref, factor_ref, sten_ref, fine_ref, coarse_ref, first_ref, line_ref, cline_ref
):
    sten = sten_ref[...]
    line_rows(mats_ref, factor_ref, line_ref, NZ, 1)
    line_rows(mats_ref, factor_ref, cline_ref, NC, 2)

    row = lax.broadcasted_iota(jnp.int32, (NZ, 256), 0)
    lane = lax.broadcasted_iota(jnp.int32, (NZ, 256), 1)
    comp = lane // NZ - 1
    layer = lane % NZ
    same = (row == layer) & (comp >= 0)
    near = ((row == layer + 1) | (row == layer - 1)) & (comp >= 0)

    def picked(which, i):
        at = which * 9 + i * 3
        return jnp.where(
            comp == 0,
            sten[:, at : at + 1],
            jnp.where(comp == 1, sten[:, at + 1 : at + 2], sten[:, at + 2 : at + 3]),
        )

    store_split(
        first_ref,
        0,
        [jnp.where(same, picked(0, i), jnp.where(near, -picked(2, i), 0.0)) for i in range(3)],
    )
    store_split(first_ref, 256, [jnp.where(same, picked(1, i), 0.0) for i in range(3)])

    def level(sten_part, scale, ref, layers):
        blocks = [ref[i * layers : (i + 1) * layers, :] for i in range(3)]
        lateral = couple(sten_part, 1, blocks)
        diag = couple(sten_part, 0, blocks)
        vert = couple(sten_part, 2, [above_below(block) for block in blocks])
        if scale is not None:
            vert = [scale * part for part in vert]
        wide = blocks[0].shape
        r = lax.broadcasted_iota(jnp.int32, wide, 0)
        q = lax.broadcasted_iota(jnp.int32, wide, 1)
        kept = [
            jnp.where(q == r + i * layers, 1.0, 0.0) - (diag[i] - vert[i]) for i in range(3)
        ]
        return blocks, kept, lateral

    blocks, kept, lateral = level(sten, None, line_ref, NZ)
    store_split(fine_ref, 0, blocks)
    store_split(fine_ref, 256, kept)
    store_split(fine_ref, 512, lateral)

    def exact(a, b):
        return jnp.dot(a, b, precision=lax.Precision.HIGHEST, preferred_element_type=F32)

    layer_at = lax.broadcasted_iota(jnp.int32, (NC, NZ), 1) // 2
    pairs = (lax.broadcasted_iota(jnp.int32, (NC, NZ), 0) == layer_at).astype(F32)
    layer_at = lax.broadcasted_iota(jnp.int32, (NZ, NC), 0) // 2
    repeats = (lax.broadcasted_iota(jnp.int32, (NZ, NC), 1) == layer_at).astype(F32)

    def paired(part):
        return [exact(pairs, block) for block in part]

    store_split(fine_ref, 768, paired(kept))
    store_split(fine_ref, 896, paired(lateral))

    coarse_sten = sten_ref[pl.ds(0, NC, stride=2), :]
    cblocks, ckept, clateral = level(coarse_sten, 0.25, cline_ref, NC)
    store_split(coarse_ref, 0, ckept)
    store_split(coarse_ref, 128, clateral)
    spread = [exact(repeats, block) for block in cblocks]
    diag = couple(sten, 0, spread)
    vert = couple(sten, 2, [above_below(block) for block in spread])
    store_split(coarse_ref, 256, spread)
    store_split(coarse_ref, 512, [d - v for d, v in zip(diag, vert)])
    store_split(coarse_ref, 768, couple(sten, 1, spread))


def cycle_kernel(
    own_ref,
    above_ref,
    below_ref,
    left_ref,
    right_ref,
    fine_ref,
    coarse_ref,
    first_ref,
    out_ref,
    x_ref,
    r_ref,
    keep_ref,
    side_ref,
    sum_ref,
    rc_ref,
    ckeep_ref,
    cside_ref,
    csum_ref,
):
    gz, gx, gy = (lax.axis_index(axis) for axis in ("gz", "gx", "gy"))
    at_left = (gx == 0) & (gz == 0)
    at_right = (gx == lax.axis_size("gx") - 1) & (gz == lax.axis_size("gz") - 1)
    at_top = gy == 0
    at_bottom = gy == lax.axis_size("gy") - 1

    x_ref[:, 0:XH] = left_ref[...]
    x_ref[:, XH + XT :] = right_ref[...]
    x_ref[0:HALO, XH : XH + XT] = above_ref[...]
    x_ref[HALO : HALO + YT, XH : XH + XT] = own_ref[...]
    x_ref[HALO + YT :, XH : XH + XT] = below_ref[...]

    def product(halves, w_ref, at, width):
        high, low = halves
        wh = w_ref[0, :, at : at + width]
        wl = w_ref[1, :, at : at + width]

        def dot(a, b):
            return jnp.dot(a, b, preferred_element_type=F32)

        return dot(high, wh) + (dot(high, wl) + dot(low, wh))

    def chunks(lo, hi, size):
        return [(y, min(y + size, hi)) for y in range(lo, hi, size)]

    def apply(src, lanes, lo, hi, w_ref, jobs, size=4):
        for a, b in chunks(lo, hi, size):
            value = src[a:b, :, lanes].reshape((b - a) * XW, -1)
            halves = split(value)
            for at, width, dst in jobs:
                dst[a:b] = product(halves, w_ref, at, width).reshape(b - a, XW, width)

    def spread(side, y):
        mid = side[y]
        return (side[y - 1] + side[y + 1]) + (
            pltpu.roll(mid, 1, axis=0) + pltpu.roll(mid, XW - 1, axis=0)
        )

    def clear(ref, lo, hi):
        width = ref.shape[2]

        @pl.when(at_left)
        def _():
            ref[lo:hi, 0:XH] = jnp.zeros((hi - lo, XH, width), F32)

        @pl.when(at_right)
        def _():
            ref[lo:hi, XH + XT :] = jnp.zeros((hi - lo, XH, width), F32)

        if lo < HALO:

            @pl.when(at_top)
            def _():
                ref[lo:HALO] = jnp.zeros((HALO - lo, XW, width), F32)

        if hi > HALO + YT:

            @pl.when(at_bottom)
            def _():
                ref[HALO + YT : hi] = jnp.zeros((hi - HALO - YT, XW, width), F32)

    own = slice(HALO, HALO + YT)
    inner = slice(XH, XH + XT)
    every = slice(None)

    apply(
        x_ref, slice(128, 384), 0, YW, first_ref, [(0, 192, keep_ref), (256, 192, side_ref)]
    )
    for y in range(1, YW - 1):
        r_ref[y] = (x_ref[y, :, 0:192] - keep_ref[y]) + spread(side_ref, y)
    clear(r_ref, 1, YW - 1)
    sum_ref[...] = r_ref[own, inner]

    for sweep in (1, 2):
        lo, hi = sweep, YW - sweep
        apply(r_ref, every, lo, hi, fine_ref, [(256, 192, keep_ref), (512, 192, side_ref)])
        for y in range(lo + 1, hi - 1):
            r_ref[y] = keep_ref[y] + spread(side_ref, y)
        clear(r_ref, lo + 1, hi - 1)
        sum_ref[...] += r_ref[own, inner]

    apply(r_ref, every, 3, YW - 3, fine_ref, [(768, 96, ckeep_ref), (896, 96, cside_ref)])
    apply(
        r_ref, every, HALO - 1, HALO + YT + 1, fine_ref, [(256, 192, keep_ref), (512, 192, side_ref)], 5
    )
    for y in range(4, YW - 4):
        rc_ref[y] = ckeep_ref[y] + spread(cside_ref, y)
    clear(rc_ref, 4, YW - 4)
    for y in range(HALO, HALO + YT):
        r_ref[y] = keep_ref[y] + spread(side_ref, y)
    csum_ref[HALO - 1 : HALO + YT + 1] = rc_ref[HALO - 1 : HALO + YT + 1]

    for sweep in (4, 5):
        lo, hi = sweep, YW - sweep
        apply(rc_ref, every, lo, hi, coarse_ref, [(0, 96, ckeep_ref), (128, 96, cside_ref)], 5)
        for y in range(lo + 1, hi - 1):
            rc_ref[y] = ckeep_ref[y] + spread(cside_ref, y)
        clear(rc_ref, lo + 1, hi - 1)
        csum_ref[HALO - 1 : HALO + YT + 1] += rc_ref[HALO - 1 : HALO + YT + 1]

    apply(
        csum_ref,
        every,
        HALO - 1,
        HALO + YT + 1,
        coarse_ref,
        [(512, 192, keep_ref), (768, 192, side_ref)],
        5,
    )
    resid = []
    for y in range(HALO, HALO + YT):
        resid.append(((r_ref[y] - keep_ref[y]) + spread(side_ref, y))[inner])
    resid = jnp.concatenate(resid, axis=0)
    change = product(split(sum_ref[...].reshape(YT * XT, 192)), fine_ref, 0, 192)
    change = change + product(
        split(csum_ref[own, inner].reshape(YT * XT, 96)), coarse_ref, 256, 192
    )
    for f, value in enumerate((change, resid)):
        turned = jnp.transpose(value)
        for c in range(3):
            for g in range(8):
                rows = turned[c * NZ + g * 8 : c * NZ + g * 8 + 8]
                for h in range(2):
                    at = h * 48 + f * 24 + c * 8
                    out_ref[g, at : at + 8, :] = rows[:, h * 128 : h * 128 + 128]


def shape(*dims, dtype=F32):
    return jax.ShapeDtypeStruct(dims, dtype)


def on_device(right_side, start_field, layer_material, stiffness, line_factors):
    size_y = lax.axis_size("gy")
    packed = pl.pallas_call(
        pack_kernel,
        out_shape=shape(8 * ROWS, 128),
        in_specs=[HBM, HBM, HBM],
        out_specs=VMEM,
        scratch_shapes=[
            pltpu.VMEM((6, 8, 8, 256), F32),
            pltpu.SMEM((8,), jnp.int32),
            pltpu.SemaphoreType.DMA((6,)),
            pltpu.SemaphoreType.DMA,
        ],
        compiler_params=params(),
        name="pack",
    )(right_side, start_field, layer_material)
    got = lax.all_to_all(packed.reshape(8, ROWS, 128), "gz", 0, 0, tiled=True)
    mats = got[:, 96, :8].reshape(-1).astype(jnp.int32)

    onehot = (mats[:, None] == jnp.arange(stiffness.shape[0])[None, :]).astype(F32)
    sten = jnp.sum(onehot[:, :, None] * stiffness.reshape(1, -1, 27), axis=1)
    sten = jnp.pad(sten, ((0, 0), (0, 128 - 27)))
    fine, coarse, first = pl.pallas_call(
        setup_kernel,
        out_shape=(
            shape(2, 192, 1024, dtype=BF16),
            shape(2, 96, 1024, dtype=BF16),
            shape(2, 256, 512, dtype=BF16),
        ),
        in_specs=[SMEM, SMEM, VMEM],
        out_specs=(VMEM, VMEM, VMEM),
        scratch_shapes=[
            pltpu.VMEM((192, 192), F32),
            pltpu.VMEM((96, 96), F32),
        ],
        compiler_params=params(),
        name="setup",
    )(mats, line_factors.reshape(-1), sten)

    own, low, high = pl.pallas_call(
        turn_kernel,
        out_shape=(shape(YT, XT, 384), shape(HALO, XT, 384), shape(HALO, XT, 384)),
        in_specs=[VMEM],
        out_specs=(VMEM, VMEM, VMEM),
        compiler_params=params(),
        name="turn",
    )(got)
    ahead = [(i, i + 1) for i in range(size_y - 1)]
    above = lax.ppermute(high, "gy", ahead)
    below = lax.ppermute(low, "gy", [(b, a) for a, b in ahead])
    to_left, to_right = pl.pallas_call(
        sides_kernel,
        out_shape=(shape(YW, XH, 384), shape(YW, XH, 384)),
        in_specs=[VMEM, VMEM, VMEM, pl.BlockSpec(memory_space=pl.ANY)],
        out_specs=(VMEM, VMEM),
        compiler_params=params(),
        name="sides",
    )(own, above, below, fine)
    count_x, count_z = lax.axis_size("gx"), lax.axis_size("gz")
    along = [(i % count_z) * count_x + i // count_z for i in range(count_x * count_z)]
    ahead = list(zip(along[:-1], along[1:]))
    left = lax.ppermute(to_right, ("gz", "gx"), ahead)
    right = lax.ppermute(to_left, ("gz", "gx"), [(b, a) for a, b in ahead])

    out = pl.pallas_call(
        cycle_kernel,
        out_shape=shape(8, 96, 128),
        in_specs=[VMEM] * 8,
        out_specs=VMEM,
        scratch_shapes=[
            pltpu.VMEM((YW, XW, 384), F32),
            pltpu.VMEM((YW, XW, 192), F32),
            pltpu.VMEM((YW, XW, 192), F32),
            pltpu.VMEM((YW, XW, 192), F32),
            pltpu.VMEM((YT, XT, 192), F32),
            pltpu.VMEM((YW, XW, 96), F32),
            pltpu.VMEM((YW, XW, 96), F32),
            pltpu.VMEM((YW, XW, 96), F32),
            pltpu.VMEM((YW, XW, 96), F32),
        ],
        compiler_params=params(),
        name="cycle",
    )(own, above, below, left, right, fine, coarse, first)
    back = lax.all_to_all(out, "gz", 0, 0, tiled=True)
    return pl.pallas_call(
        unpack_kernel,
        out_shape=(shape(8, 3, 8, 256), shape(8, 3, 8, 256)),
        in_specs=[VMEM, VMEM],
        out_specs=(HBM, HBM),
        scratch_shapes=[pltpu.VMEM((6, 8, 8, 256), F32), pltpu.SemaphoreType.DMA((6,))],
        compiler_params=params(),
        name="unpack",
    )(back.reshape(768, 128), start_field)


def solution(mesh):
    return jax.shard_map(
        on_device,
        mesh=mesh,
        in_specs=(P("gz", None, "gy", "gx"), P("gz", None, "gy", "gx"), P("gz"), P(), P()),
        out_specs=(P("gz", None, "gy", "gx"), P("gz", None, "gy", "gx")),
        check_vma=False,
    )
```

```python
import jax
import jax.numpy as jnp
from jax import lax
from jax.experimental import pallas as pl
from jax.experimental.pallas import tpu as pltpu
from jax.sharding import PartitionSpec as P

F32 = jnp.float32
BF16 = jnp.bfloat16
HALO = 7
XH = 8
XT = 32
XW = XT + 2 * XH
YT = 8
YW = YT + 2 * HALO
ROWS = 104
NZ = 64
NC = NZ // 2
VMEM = pl.BlockSpec(memory_space=pltpu.VMEM)
HBM = pl.BlockSpec(memory_space=pltpu.HBM)
SMEM = pl.BlockSpec(memory_space=pltpu.SMEM)


def params(mib=40):
    return pltpu.CompilerParams(vmem_limit_bytes=mib * 1024 * 1024)


def swap_blocks(tile):
    sub = lax.broadcasted_iota(jnp.int32, tile.shape, 1)
    blk = lax.broadcasted_iota(jnp.int32, tile.shape, 2) // 32
    for bit in (1, 2, 4):
        up = pltpu.roll(pltpu.roll(tile, 8 - bit, axis=1), 32 * bit, axis=2)
        down = pltpu.roll(pltpu.roll(tile, bit, axis=1), 256 - 32 * bit, axis=2)
        in_sub = (sub & bit) != 0
        in_blk = (blk & bit) != 0
        tile = jnp.where(in_sub == in_blk, tile, jnp.where(in_blk, up, down))
    return tile


def fetches(pairs, sems):
    copies = [pltpu.make_async_copy(src, dst, sems.at[i]) for i, (src, dst) in enumerate(pairs)]
    for copy in copies:
        copy.start()
    return copies


def pack_kernel(load_hbm, start_hbm, mats_hbm, out_ref, in_ref, mats_ref, sems, mats_sem):
    mats_copy = pltpu.make_async_copy(mats_hbm, mats_ref, mats_sem)
    mats_copy.start()
    order = [(f, c) for f in range(2) for c in range(3)]
    copies = fetches(
        [((load_hbm, start_hbm)[f].at[:, c], in_ref.at[i]) for i, (f, c) in enumerate(order)], sems
    )
    for i, (f, c) in enumerate(order):
        copies[i].wait()
        tile = swap_blocks(in_ref[i])
        for z in range(8):
            for h in range(2):
                at = h * 48 + f * 24 + c * 8 + z
                out_ref[pl.ds(at, 8, stride=ROWS), :] = tile[z, :, h * 128 : h * 128 + 128]
    mats_copy.wait()
    lane = lax.broadcasted_iota(jnp.int32, (8, 128), 1)
    ids = jnp.zeros((8, 128), jnp.int32)
    for z in range(8):
        ids = jnp.where(lane == z, mats_ref[z], ids)
    for k in range(8):
        out_ref[k * ROWS + 96 : k * ROWS + 104, :] = ids.astype(F32)


def unpack_kernel(got_ref, start_ref, field_hbm, resid_hbm, out_ref, sems):
    copies = []
    for f, ref in enumerate((field_hbm, resid_hbm)):
        for c in range(3):
            halves = []
            for h in range(2):
                at = h * 48 + f * 24 + c * 8
                rows = [got_ref[pl.ds(at + z, 8, stride=96), :] for z in range(8)]
                halves.append(jnp.stack(rows, axis=0))
            tile = swap_blocks(jnp.concatenate(halves, axis=2))
            if f == 0:
                tile = tile + start_ref[:, c]
            i = f * 3 + c
            out_ref[i] = tile
            copy = pltpu.make_async_copy(out_ref.at[i], ref.at[:, c], sems.at[i])
            copy.start()
            copies.append(copy)
    for copy in copies:
        copy.wait()


def turn_kernel(got_ref, own_ref, low_ref, high_ref, *side_refs):
    left_refs, right_refs = side_refs[:3], side_refs[3:]
    halves = []
    for h in range(2):
        rows = [got_ref[g, h * 48 + q * 8 : h * 48 + q * 8 + 8] for q in range(6) for g in range(8)]
        halves.append(jnp.transpose(jnp.concatenate(rows, axis=0)))
    turned = jnp.concatenate(halves, axis=0).reshape(YT, XT, 384)
    own_ref[...] = turned
    low, high = turned[:HALO], turned[YT - HALO :]
    for ref, value in ((low_ref, low), (high_ref, high)):
        ref[...] = value
    for refs, value in ((left_refs, (turned, low, high)), (right_refs, (turned, low, high))):
        cols = slice(0, XH) if refs is left_refs else slice(XT - XH, XT)
        for ref, part in zip(refs, value):
            ref[...] = part[:, cols]


def split(value):
    high = value.astype(BF16)
    return high, (value - high.astype(F32)).astype(BF16)


def line_rows(mats_ref, factor_ref, dst_ref, layers, step):
    lane = lax.broadcasted_iota(jnp.int32, (1, 3 * layers), 1)

    def up(z, state):
        base = mats_ref[z * step] * 27
        new = []
        for i in range(3):
            row = jnp.zeros((1, 3 * layers), F32)
            for j in range(3):
                row = jnp.where(lane == j * layers + z, factor_ref[base + i * 3 + j], row)
            for j in range(3):
                row = row + factor_ref[base + 9 + i * 3 + j] * state[j]
            dst_ref[pl.ds(i * layers + z, 1), :] = row
            new.append(row)
        return tuple(new)

    def down(t, state):
        z = layers - 1 - t
        base = mats_ref[z * step] * 27
        new = []
        for i in range(3):
            row = dst_ref[pl.ds(i * layers + z, 1), :]
            for j in range(3):
                row = row + factor_ref[base + 18 + i * 3 + j] * state[j]
            dst_ref[pl.ds(i * layers + z, 1), :] = row
            new.append(row)
        return tuple(new)

    zero = tuple(jnp.zeros((1, 3 * layers), F32) for _ in range(3))
    lax.fori_loop(0, layers, up, zero, unroll=8)
    lax.fori_loop(0, layers, down, zero, unroll=8)


def couple(sten, which, blocks):
    out = []
    for i in range(3):
        total = None
        for j in range(3):
            at = which * 9 + i * 3 + j
            term = sten[:, at : at + 1] * blocks[j]
            total = term if total is None else total + term
        out.append(total)
    return out


def above_below(block):
    row = lax.broadcasted_iota(jnp.int32, block.shape, 0)
    n = block.shape[0]
    low = jnp.where(row == 0, 0.0, pltpu.roll(block, 1, axis=0))
    high = jnp.where(row == n - 1, 0.0, pltpu.roll(block, n - 1, axis=0))
    return low + high


def store_split(ref, at, rows):
    value = jnp.transpose(jnp.concatenate(rows, axis=0))
    high, low = split(value)
    ref[0, :, at : at + value.shape[1]] = high
    ref[1, :, at : at + value.shape[1]] = low


def setup_kernel(
    mats_ref, factor_ref, sten_ref, fine_ref, coarse_ref, first_ref, line_ref, cline_ref
):
    sten = sten_ref[...]
    line_rows(mats_ref, factor_ref, line_ref, NZ, 1)
    line_rows(mats_ref, factor_ref, cline_ref, NC, 2)

    row = lax.broadcasted_iota(jnp.int32, (NZ, 256), 0)
    lane = lax.broadcasted_iota(jnp.int32, (NZ, 256), 1)
    comp = lane // NZ - 1
    layer = lane % NZ
    same = (row == layer) & (comp >= 0)
    near = ((row == layer + 1) | (row == layer - 1)) & (comp >= 0)

    def picked(which, i):
        at = which * 9 + i * 3
        return jnp.where(
            comp == 0,
            sten[:, at : at + 1],
            jnp.where(comp == 1, sten[:, at + 1 : at + 2], sten[:, at + 2 : at + 3]),
        )

    store_split(
        first_ref,
        0,
        [jnp.where(same, picked(0, i), jnp.where(near, -picked(2, i), 0.0)) for i in range(3)],
    )
    store_split(first_ref, 256, [jnp.where(same, picked(1, i), 0.0) for i in range(3)])

    def level(sten_part, scale, ref, layers):
        blocks = [ref[i * layers : (i + 1) * layers, :] for i in range(3)]
        lateral = couple(sten_part, 1, blocks)
        diag = couple(sten_part, 0, blocks)
        vert = couple(sten_part, 2, [above_below(block) for block in blocks])
        if scale is not None:
            vert = [scale * part for part in vert]
        wide = blocks[0].shape
        r = lax.broadcasted_iota(jnp.int32, wide, 0)
        q = lax.broadcasted_iota(jnp.int32, wide, 1)
        kept = [
            jnp.where(q == r + i * layers, 1.0, 0.0) - (diag[i] - vert[i]) for i in range(3)
        ]
        return blocks, kept, lateral

    blocks, kept, lateral = level(sten, None, line_ref, NZ)
    store_split(fine_ref, 0, blocks)
    store_split(fine_ref, 256, kept)
    store_split(fine_ref, 512, lateral)

    def exact(a, b):
        return jnp.dot(a, b, precision=lax.Precision.HIGHEST, preferred_element_type=F32)

    layer_at = lax.broadcasted_iota(jnp.int32, (NC, NZ), 1) // 2
    pairs = (lax.broadcasted_iota(jnp.int32, (NC, NZ), 0) == layer_at).astype(F32)
    layer_at = lax.broadcasted_iota(jnp.int32, (NZ, NC), 0) // 2
    repeats = (lax.broadcasted_iota(jnp.int32, (NZ, NC), 1) == layer_at).astype(F32)

    def paired(part):
        return [exact(pairs, block) for block in part]

    store_split(fine_ref, 768, paired(kept))
    store_split(fine_ref, 896, paired(lateral))

    coarse_sten = sten_ref[pl.ds(0, NC, stride=2), :]
    cblocks, ckept, clateral = level(coarse_sten, 0.25, cline_ref, NC)
    store_split(coarse_ref, 0, ckept)
    store_split(coarse_ref, 128, clateral)
    spread = [exact(repeats, block) for block in cblocks]
    diag = couple(sten, 0, spread)
    vert = couple(sten, 2, [above_below(block) for block in spread])
    store_split(coarse_ref, 256, spread)
    store_split(coarse_ref, 512, [d - v for d, v in zip(diag, vert)])
    store_split(coarse_ref, 768, couple(sten, 1, spread))


def cycle_kernel(
    own_ref,
    above_ref,
    below_ref,
    left_ref,
    left_above_ref,
    left_below_ref,
    right_ref,
    right_above_ref,
    right_below_ref,
    fine_ref,
    coarse_ref,
    first_ref,
    out_ref,
    x_ref,
    r_ref,
    keep_ref,
    side_ref,
    sum_ref,
    rc_ref,
    ckeep_ref,
    cside_ref,
    csum_ref,
):
    gz, gx, gy = (lax.axis_index(axis) for axis in ("gz", "gx", "gy"))
    at_left = (gx == 0) & (gz == 0)
    at_right = (gx == lax.axis_size("gx") - 1) & (gz == lax.axis_size("gz") - 1)
    at_top = gy == 0
    at_bottom = gy == lax.axis_size("gy") - 1

    for cols, refs in (
        (slice(0, XH), (left_above_ref, left_ref, left_below_ref)),
        (slice(XH + XT, XW), (right_above_ref, right_ref, right_below_ref)),
    ):
        x_ref[0:HALO, cols] = refs[0][...]
        x_ref[HALO : HALO + YT, cols] = refs[1][...]
        x_ref[HALO + YT :, cols] = refs[2][...]
    x_ref[0:HALO, XH : XH + XT] = above_ref[...]
    x_ref[HALO : HALO + YT, XH : XH + XT] = own_ref[...]
    x_ref[HALO + YT :, XH : XH + XT] = below_ref[...]

    def product(halves, w_ref, at, width):
        high, low = halves
        wh = w_ref[0, :, at : at + width]
        wl = w_ref[1, :, at : at + width]

        def dot(a, b):
            return jnp.dot(a, b, preferred_element_type=F32)

        return dot(high, wh) + (dot(high, wl) + dot(low, wh))

    def chunks(lo, hi, size):
        return [(y, min(y + size, hi)) for y in range(lo, hi, size)]

    def apply(src, lanes, lo, hi, w_ref, jobs, size=4):
        for a, b in chunks(lo, hi, size):
            value = src[a:b, :, lanes].reshape((b - a) * XW, -1)
            halves = split(value)
            for at, width, dst in jobs:
                dst[a:b] = product(halves, w_ref, at, width).reshape(b - a, XW, width)

    def spread(side, y):
        mid = side[y]
        return (side[y - 1] + side[y + 1]) + (
            pltpu.roll(mid, 1, axis=0) + pltpu.roll(mid, XW - 1, axis=0)
        )

    def clear(ref, lo, hi):
        width = ref.shape[2]

        @pl.when(at_left)
        def _():
            ref[lo:hi, 0:XH] = jnp.zeros((hi - lo, XH, width), F32)

        @pl.when(at_right)
        def _():
            ref[lo:hi, XH + XT :] = jnp.zeros((hi - lo, XH, width), F32)

        if lo < HALO:

            @pl.when(at_top)
            def _():
                ref[lo:HALO] = jnp.zeros((HALO - lo, XW, width), F32)

        if hi > HALO + YT:

            @pl.when(at_bottom)
            def _():
                ref[HALO + YT : hi] = jnp.zeros((hi - HALO - YT, XW, width), F32)

    own = slice(HALO, HALO + YT)
    inner = slice(XH, XH + XT)
    every = slice(None)

    apply(
        x_ref, slice(128, 384), 0, YW, first_ref, [(0, 192, keep_ref), (256, 192, side_ref)]
    )
    for y in range(1, YW - 1):
        r_ref[y] = (x_ref[y, :, 0:192] - keep_ref[y]) + spread(side_ref, y)
    clear(r_ref, 1, YW - 1)
    sum_ref[...] = r_ref[own, inner]

    for sweep in (1, 2):
        lo, hi = sweep, YW - sweep
        apply(r_ref, every, lo, hi, fine_ref, [(256, 192, keep_ref), (512, 192, side_ref)])
        for y in range(lo + 1, hi - 1):
            r_ref[y] = keep_ref[y] + spread(side_ref, y)
        clear(r_ref, lo + 1, hi - 1)
        sum_ref[...] += r_ref[own, inner]

    apply(r_ref, every, 3, YW - 3, fine_ref, [(768, 96, ckeep_ref), (896, 96, cside_ref)])
    apply(
        r_ref, every, HALO - 1, HALO + YT + 1, fine_ref, [(256, 192, keep_ref), (512, 192, side_ref)], 5
    )
    for y in range(4, YW - 4):
        rc_ref[y] = ckeep_ref[y] + spread(cside_ref, y)
    clear(rc_ref, 4, YW - 4)
    for y in range(HALO, HALO + YT):
        r_ref[y] = keep_ref[y] + spread(side_ref, y)
    csum_ref[HALO - 1 : HALO + YT + 1] = rc_ref[HALO - 1 : HALO + YT + 1]

    for sweep in (4, 5):
        lo, hi = sweep, YW - sweep
        apply(rc_ref, every, lo, hi, coarse_ref, [(0, 96, ckeep_ref), (128, 96, cside_ref)], 5)
        for y in range(lo + 1, hi - 1):
            rc_ref[y] = ckeep_ref[y] + spread(cside_ref, y)
        clear(rc_ref, lo + 1, hi - 1)
        csum_ref[HALO - 1 : HALO + YT + 1] += rc_ref[HALO - 1 : HALO + YT + 1]

    apply(
        csum_ref,
        every,
        HALO - 1,
        HALO + YT + 1,
        coarse_ref,
        [(512, 192, keep_ref), (768, 192, side_ref)],
        5,
    )
    resid = []
    for y in range(HALO, HALO + YT):
        resid.append(((r_ref[y] - keep_ref[y]) + spread(side_ref, y))[inner])
    resid = jnp.concatenate(resid, axis=0)
    change = product(split(sum_ref[...].reshape(YT * XT, 192)), fine_ref, 0, 192)
    change = change + product(
        split(csum_ref[own, inner].reshape(YT * XT, 96)), coarse_ref, 256, 192
    )
    for f, value in enumerate((change, resid)):
        turned = jnp.transpose(value)
        for c in range(3):
            for g in range(8):
                rows = turned[c * NZ + g * 8 : c * NZ + g * 8 + 8]
                for h in range(2):
                    at = h * 48 + f * 24 + c * 8
                    out_ref[g, at : at + 8, :] = rows[:, h * 128 : h * 128 + 128]


def shape(*dims, dtype=F32):
    return jax.ShapeDtypeStruct(dims, dtype)


def on_device(right_side, start_field, layer_material, stiffness, line_factors):
    size_y = lax.axis_size("gy")
    packed = pl.pallas_call(
        pack_kernel,
        out_shape=shape(8 * ROWS, 128),
        in_specs=[HBM, HBM, HBM],
        out_specs=VMEM,
        scratch_shapes=[
            pltpu.VMEM((6, 8, 8, 256), F32),
            pltpu.SMEM((8,), jnp.int32),
            pltpu.SemaphoreType.DMA((6,)),
            pltpu.SemaphoreType.DMA,
        ],
        compiler_params=params(60),
        name="pack",
    )(right_side, start_field, layer_material)
    got = lax.all_to_all(packed.reshape(8, ROWS, 128), "gz", 0, 0, tiled=True)
    mats = got[:, 96, :8].reshape(-1).astype(jnp.int32)

    onehot = (mats[:, None] == jnp.arange(stiffness.shape[0])[None, :]).astype(F32)
    sten = jnp.sum(onehot[:, :, None] * stiffness.reshape(1, -1, 27), axis=1)
    sten = jnp.pad(sten, ((0, 0), (0, 128 - 27)))
    fine, coarse, first = pl.pallas_call(
        setup_kernel,
        out_shape=(
            shape(2, 192, 1024, dtype=BF16),
            shape(2, 96, 1024, dtype=BF16),
            shape(2, 256, 512, dtype=BF16),
        ),
        in_specs=[SMEM, SMEM, VMEM],
        out_specs=(VMEM, VMEM, VMEM),
        scratch_shapes=[
            pltpu.VMEM((192, 192), F32),
            pltpu.VMEM((96, 96), F32),
        ],
        compiler_params=params(),
        name="setup",
    )(mats, line_factors.reshape(-1), sten)

    side = (shape(YT, XH, 384), shape(HALO, XH, 384), shape(HALO, XH, 384))
    own, low, high, *sides = pl.pallas_call(
        turn_kernel,
        out_shape=(shape(YT, XT, 384), shape(HALO, XT, 384), shape(HALO, XT, 384), *side, *side),
        in_specs=[VMEM],
        out_specs=(VMEM,) * 9,
        compiler_params=params(),
        name="turn",
    )(got)
    lefts, rights = sides[:3], sides[3:]
    count_z, count_x, count_y = (lax.axis_size(axis) for axis in ("gz", "gx", "gy"))

    def sent(value, step_x, step_y):
        pairs = []
        for x in range(count_x * count_z):
            for y in range(count_y):
                if 0 <= x + step_x < count_x * count_z and 0 <= y + step_y < count_y:
                    ends = [
                        ((p % count_z) * count_x + p // count_z) * count_y + q
                        for p, q in ((x, y), (x + step_x, y + step_y))
                    ]
                    pairs.append(tuple(ends))
        return lax.ppermute(value, ("gz", "gx", "gy"), pairs)

    above, below = sent(high, 0, 1), sent(low, 0, -1)
    left_above, left_below = sent(rights[2], 1, 1), sent(rights[1], 1, -1)
    right_above, right_below = sent(lefts[2], -1, 1), sent(lefts[1], -1, -1)
    left, right = sent(rights[0], 1, 0), sent(lefts[0], -1, 0)

    out = pl.pallas_call(
        cycle_kernel,
        out_shape=shape(8, 96, 128),
        in_specs=[VMEM] * 12,
        out_specs=VMEM,
        scratch_shapes=[
            pltpu.VMEM((YW, XW, 384), F32),
            pltpu.VMEM((YW, XW, 192), F32),
            pltpu.VMEM((YW, XW, 192), F32),
            pltpu.VMEM((YW, XW, 192), F32),
            pltpu.VMEM((YT, XT, 192), F32),
            pltpu.VMEM((YW, XW, 96), F32),
            pltpu.VMEM((YW, XW, 96), F32),
            pltpu.VMEM((YW, XW, 96), F32),
            pltpu.VMEM((YW, XW, 96), F32),
        ],
        compiler_params=params(),
        name="cycle",
    )(
        own,
        above,
        below,
        left,
        left_above,
        left_below,
        right,
        right_above,
        right_below,
        fine,
        coarse,
        first,
    )
    back = lax.all_to_all(out, "gz", 0, 0, tiled=True)
    return pl.pallas_call(
        unpack_kernel,
        out_shape=(shape(8, 3, 8, 256), shape(8, 3, 8, 256)),
        in_specs=[VMEM, VMEM],
        out_specs=(HBM, HBM),
        scratch_shapes=[pltpu.VMEM((6, 8, 8, 256), F32), pltpu.SemaphoreType.DMA((6,))],
        compiler_params=params(),
        name="unpack",
    )(back.reshape(768, 128), start_field)


def solution(mesh):
    return jax.shard_map(
        on_device,
        mesh=mesh,
        in_specs=(P("gz", None, "gy", "gx"), P("gz", None, "gy", "gx"), P("gz"), P(), P()),
        out_specs=(P("gz", None, "gy", "gx"), P("gz", None, "gy", "gx")),
        check_vma=False,
    )
```

```python
import jax
import jax.numpy as jnp
from jax import lax
from jax.experimental import pallas as pl
from jax.experimental.pallas import tpu as pltpu
from jax.sharding import PartitionSpec as P

F32 = jnp.float32
BF16 = jnp.bfloat16
HALO = 7
XH = 8
XT = 32
XW = XT + 2 * XH
YT = 8
YW = YT + 2 * HALO
ROWS = 104
NZ = 64
NC = NZ // 2
VMEM = pl.BlockSpec(memory_space=pltpu.VMEM)
HBM = pl.BlockSpec(memory_space=pltpu.HBM)
SMEM = pl.BlockSpec(memory_space=pltpu.SMEM)


def params(mib=40):
    return pltpu.CompilerParams(vmem_limit_bytes=mib * 1024 * 1024)


def swap_blocks(tile):
    sub = lax.broadcasted_iota(jnp.int32, tile.shape, 1)
    blk = lax.broadcasted_iota(jnp.int32, tile.shape, 2) // 32
    for bit in (1, 2, 4):
        up = pltpu.roll(pltpu.roll(tile, 8 - bit, axis=1), 32 * bit, axis=2)
        down = pltpu.roll(pltpu.roll(tile, bit, axis=1), 256 - 32 * bit, axis=2)
        in_sub = (sub & bit) != 0
        in_blk = (blk & bit) != 0
        tile = jnp.where(in_sub == in_blk, tile, jnp.where(in_blk, up, down))
    return tile


def fetches(pairs, sems):
    copies = [pltpu.make_async_copy(src, dst, sems.at[i]) for i, (src, dst) in enumerate(pairs)]
    for copy in copies:
        copy.start()
    return copies


def pack_kernel(load_hbm, start_hbm, mats_hbm, out_ref, in_ref, mats_ref, sems, mats_sem):
    mats_copy = pltpu.make_async_copy(mats_hbm, mats_ref, mats_sem)
    mats_copy.start()
    order = [(f, c) for f in range(2) for c in range(3)]
    copies = fetches(
        [((load_hbm, start_hbm)[f].at[:, c], in_ref.at[i]) for i, (f, c) in enumerate(order)], sems
    )
    for i, (f, c) in enumerate(order):
        copies[i].wait()
        tile = swap_blocks(in_ref[i])
        for z in range(8):
            for h in range(2):
                at = h * 48 + f * 24 + c * 8 + z
                out_ref[pl.ds(at, 8, stride=ROWS), :] = tile[z, :, h * 128 : h * 128 + 128]
    mats_copy.wait()
    lane = lax.broadcasted_iota(jnp.int32, (8, 128), 1)
    ids = jnp.zeros((8, 128), jnp.int32)
    for z in range(8):
        ids = jnp.where(lane == z, mats_ref[z], ids)
    for k in range(8):
        out_ref[k * ROWS + 96 : k * ROWS + 104, :] = ids.astype(F32)


def unpack_kernel(got_ref, start_ref, field_hbm, resid_hbm, out_ref, sems):
    copies = []
    for f, ref in enumerate((field_hbm, resid_hbm)):
        for c in range(3):
            halves = []
            for h in range(2):
                at = h * 48 + f * 24 + c * 8
                rows = [got_ref[pl.ds(at + z, 8, stride=96), :] for z in range(8)]
                halves.append(jnp.stack(rows, axis=0))
            tile = swap_blocks(jnp.concatenate(halves, axis=2))
            if f == 0:
                tile = tile + start_ref[:, c]
            i = f * 3 + c
            out_ref[i] = tile
            copy = pltpu.make_async_copy(out_ref.at[i], ref.at[:, c], sems.at[i])
            copy.start()
            copies.append(copy)
    for copy in copies:
        copy.wait()


def turn_kernel(got_ref, own_ref, first_ref, second_ref):
    halves = []
    for h in range(2):
        rows = [got_ref[g, h * 48 + q * 8 : h * 48 + q * 8 + 8] for q in range(6) for g in range(8)]
        halves.append(jnp.transpose(jnp.concatenate(rows, axis=0)))
    turned = jnp.concatenate(halves, axis=0).reshape(YT, XT, 384)
    own_ref[...] = turned
    even = lax.axis_index("gy") % 2 == 0
    low, high = turned[:HALO], turned[YT - HALO :]
    first_ref[...] = jnp.where(even, high, low)
    second_ref[...] = jnp.where(even, low, high)


def sides_kernel(own_ref, first_ref, second_ref, after_ref, send1_ref, send2_ref):
    even_x = lax.axis_index("gz") % 2 == 0
    even_y = lax.axis_index("gy") % 2 == 0

    def put(rows, value):
        left, right = value[:, 0:XH], value[:, XT - XH :]
        send1_ref[rows] = jnp.where(even_x, right, left)
        send2_ref[rows] = jnp.where(even_x, left, right)

    first, second = first_ref[...], second_ref[...]
    put(slice(0, HALO), jnp.where(even_y, second, first))
    put(slice(HALO, HALO + YT), own_ref[...])
    put(slice(HALO + YT, YW), jnp.where(even_y, first, second))


def split(value):
    high = value.astype(BF16)
    return high, (value - high.astype(F32)).astype(BF16)


def line_rows(mats_ref, factor_ref, dst_ref, layers, step):
    lane = lax.broadcasted_iota(jnp.int32, (1, 3 * layers), 1)

    def up(z, state):
        base = mats_ref[z * step] * 27
        new = []
        for i in range(3):
            row = jnp.zeros((1, 3 * layers), F32)
            for j in range(3):
                row = jnp.where(lane == j * layers + z, factor_ref[base + i * 3 + j], row)
            for j in range(3):
                row = row + factor_ref[base + 9 + i * 3 + j] * state[j]
            dst_ref[pl.ds(i * layers + z, 1), :] = row
            new.append(row)
        return tuple(new)

    def down(t, state):
        z = layers - 1 - t
        base = mats_ref[z * step] * 27
        new = []
        for i in range(3):
            row = dst_ref[pl.ds(i * layers + z, 1), :]
            for j in range(3):
                row = row + factor_ref[base + 18 + i * 3 + j] * state[j]
            dst_ref[pl.ds(i * layers + z, 1), :] = row
            new.append(row)
        return tuple(new)

    zero = tuple(jnp.zeros((1, 3 * layers), F32) for _ in range(3))
    lax.fori_loop(0, layers, up, zero, unroll=8)
    lax.fori_loop(0, layers, down, zero, unroll=8)


def couple(sten, which, blocks):
    out = []
    for i in range(3):
        total = None
        for j in range(3):
            at = which * 9 + i * 3 + j
            term = sten[:, at : at + 1] * blocks[j]
            total = term if total is None else total + term
        out.append(total)
    return out


def above_below(block):
    row = lax.broadcasted_iota(jnp.int32, block.shape, 0)
    n = block.shape[0]
    low = jnp.where(row == 0, 0.0, pltpu.roll(block, 1, axis=0))
    high = jnp.where(row == n - 1, 0.0, pltpu.roll(block, n - 1, axis=0))
    return low + high


def store_split(ref, at, rows):
    value = jnp.transpose(jnp.concatenate(rows, axis=0))
    high, low = split(value)
    ref[0, :, at : at + value.shape[1]] = high
    ref[1, :, at : at + value.shape[1]] = low


def setup_kernel(
    mats_ref, factor_ref, sten_ref, fine_ref, coarse_ref, first_ref, line_ref, cline_ref
):
    sten = sten_ref[...]
    line_rows(mats_ref, factor_ref, line_ref, NZ, 1)
    line_rows(mats_ref, factor_ref, cline_ref, NC, 2)

    row = lax.broadcasted_iota(jnp.int32, (NZ, 256), 0)
    lane = lax.broadcasted_iota(jnp.int32, (NZ, 256), 1)
    comp = lane // NZ - 1
    layer = lane % NZ
    same = (row == layer) & (comp >= 0)
    near = ((row == layer + 1) | (row == layer - 1)) & (comp >= 0)

    def picked(which, i):
        at = which * 9 + i * 3
        return jnp.where(
            comp == 0,
            sten[:, at : at + 1],
            jnp.where(comp == 1, sten[:, at + 1 : at + 2], sten[:, at + 2 : at + 3]),
        )

    store_split(
        first_ref,
        0,
        [jnp.where(same, picked(0, i), jnp.where(near, -picked(2, i), 0.0)) for i in range(3)],
    )
    store_split(first_ref, 256, [jnp.where(same, picked(1, i), 0.0) for i in range(3)])

    def level(sten_part, scale, ref, layers):
        blocks = [ref[i * layers : (i + 1) * layers, :] for i in range(3)]
        lateral = couple(sten_part, 1, blocks)
        diag = couple(sten_part, 0, blocks)
        vert = couple(sten_part, 2, [above_below(block) for block in blocks])
        if scale is not None:
            vert = [scale * part for part in vert]
        wide = blocks[0].shape
        r = lax.broadcasted_iota(jnp.int32, wide, 0)
        q = lax.broadcasted_iota(jnp.int32, wide, 1)
        kept = [
            jnp.where(q == r + i * layers, 1.0, 0.0) - (diag[i] - vert[i]) for i in range(3)
        ]
        return blocks, kept, lateral

    blocks, kept, lateral = level(sten, None, line_ref, NZ)
    store_split(fine_ref, 0, blocks)
    store_split(fine_ref, 256, kept)
    store_split(fine_ref, 512, lateral)

    def exact(a, b):
        return jnp.dot(a, b, precision=lax.Precision.HIGHEST, preferred_element_type=F32)

    layer_at = lax.broadcasted_iota(jnp.int32, (NC, NZ), 1) // 2
    pairs = (lax.broadcasted_iota(jnp.int32, (NC, NZ), 0) == layer_at).astype(F32)
    layer_at = lax.broadcasted_iota(jnp.int32, (NZ, NC), 0) // 2
    repeats = (lax.broadcasted_iota(jnp.int32, (NZ, NC), 1) == layer_at).astype(F32)

    def paired(part):
        return [exact(pairs, block) for block in part]

    store_split(fine_ref, 768, paired(kept))
    store_split(fine_ref, 896, paired(lateral))

    coarse_sten = sten_ref[pl.ds(0, NC, stride=2), :]
    cblocks, ckept, clateral = level(coarse_sten, 0.25, cline_ref, NC)
    store_split(coarse_ref, 0, ckept)
    store_split(coarse_ref, 128, clateral)
    spread = [exact(repeats, block) for block in cblocks]
    diag = couple(sten, 0, spread)
    vert = couple(sten, 2, [above_below(block) for block in spread])
    store_split(coarse_ref, 256, spread)
    store_split(coarse_ref, 512, [d - v for d, v in zip(diag, vert)])
    store_split(coarse_ref, 768, couple(sten, 1, spread))


def cycle_kernel(
    own_ref,
    y1_ref,
    y2_ref,
    x1_ref,
    x2_ref,
    fine_ref,
    coarse_ref,
    first_ref,
    out_ref,
    x_ref,
    r_ref,
    keep_ref,
    side_ref,
    sum_ref,
    rc_ref,
    ckeep_ref,
    cside_ref,
    csum_ref,
):
    gz, gx, gy = (lax.axis_index(axis) for axis in ("gz", "gx", "gy"))
    at_left = (gx == 0) & (gz == 0)
    at_right = (gx == lax.axis_size("gx") - 1) & (gz == lax.axis_size("gz") - 1)
    at_top = gy == 0
    at_bottom = gy == lax.axis_size("gy") - 1

    even_x = gz % 2 == 0
    even_y = gy % 2 == 0
    x_ref[:, 0:XH] = jnp.where(even_x, x2_ref[...], x1_ref[...])
    x_ref[:, XH + XT :] = jnp.where(even_x, x1_ref[...], x2_ref[...])
    x_ref[0:HALO, XH : XH + XT] = jnp.where(even_y, y2_ref[...], y1_ref[...])
    x_ref[HALO : HALO + YT, XH : XH + XT] = own_ref[...]
    x_ref[HALO + YT :, XH : XH + XT] = jnp.where(even_y, y1_ref[...], y2_ref[...])

    def product(halves, w_ref, at, width):
        high, low = halves
        wh = w_ref[0, :, at : at + width]
        wl = w_ref[1, :, at : at + width]

        def dot(a, b):
            return jnp.dot(a, b, preferred_element_type=F32)

        return dot(high, wh) + (dot(high, wl) + dot(low, wh))

    def chunks(lo, hi, size):
        return [(y, min(y + size, hi)) for y in range(lo, hi, size)]

    def apply(src, lanes, lo, hi, w_ref, jobs, size=4):
        for a, b in chunks(lo, hi, size):
            value = src[a:b, :, lanes].reshape((b - a) * XW, -1)
            halves = split(value)
            for at, width, dst in jobs:
                dst[a:b] = product(halves, w_ref, at, width).reshape(b - a, XW, width)

    def spread(side, y):
        mid = side[y]
        return (side[y - 1] + side[y + 1]) + (
            pltpu.roll(mid, 1, axis=0) + pltpu.roll(mid, XW - 1, axis=0)
        )

    def clear(ref, lo, hi):
        width = ref.shape[2]

        @pl.when(at_left)
        def _():
            ref[lo:hi, 0:XH] = jnp.zeros((hi - lo, XH, width), F32)

        @pl.when(at_right)
        def _():
            ref[lo:hi, XH + XT :] = jnp.zeros((hi - lo, XH, width), F32)

        if lo < HALO:

            @pl.when(at_top)
            def _():
                ref[lo:HALO] = jnp.zeros((HALO - lo, XW, width), F32)

        if hi > HALO + YT:

            @pl.when(at_bottom)
            def _():
                ref[HALO + YT : hi] = jnp.zeros((hi - HALO - YT, XW, width), F32)

    own = slice(HALO, HALO + YT)
    inner = slice(XH, XH + XT)
    every = slice(None)

    apply(
        x_ref, slice(128, 384), 0, YW, first_ref, [(0, 192, keep_ref), (256, 192, side_ref)]
    )
    for y in range(1, YW - 1):
        r_ref[y] = (x_ref[y, :, 0:192] - keep_ref[y]) + spread(side_ref, y)
    clear(r_ref, 1, YW - 1)
    sum_ref[...] = r_ref[own, inner]

    for sweep in (1, 2):
        lo, hi = sweep, YW - sweep
        apply(r_ref, every, lo, hi, fine_ref, [(256, 192, keep_ref), (512, 192, side_ref)])
        for y in range(lo + 1, hi - 1):
            r_ref[y] = keep_ref[y] + spread(side_ref, y)
        clear(r_ref, lo + 1, hi - 1)
        sum_ref[...] += r_ref[own, inner]

    apply(r_ref, every, 3, YW - 3, fine_ref, [(768, 96, ckeep_ref), (896, 96, cside_ref)])
    apply(
        r_ref, every, HALO - 1, HALO + YT + 1, fine_ref, [(256, 192, keep_ref), (512, 192, side_ref)], 5
    )
    for y in range(4, YW - 4):
        rc_ref[y] = ckeep_ref[y] + spread(cside_ref, y)
    clear(rc_ref, 4, YW - 4)
    for y in range(HALO, HALO + YT):
        r_ref[y] = keep_ref[y] + spread(side_ref, y)
    csum_ref[HALO - 1 : HALO + YT + 1] = rc_ref[HALO - 1 : HALO + YT + 1]

    for sweep in (4, 5):
        lo, hi = sweep, YW - sweep
        apply(rc_ref, every, lo, hi, coarse_ref, [(0, 96, ckeep_ref), (128, 96, cside_ref)], 5)
        for y in range(lo + 1, hi - 1):
            rc_ref[y] = ckeep_ref[y] + spread(cside_ref, y)
        clear(rc_ref, lo + 1, hi - 1)
        csum_ref[HALO - 1 : HALO + YT + 1] += rc_ref[HALO - 1 : HALO + YT + 1]

    apply(
        csum_ref,
        every,
        HALO - 1,
        HALO + YT + 1,
        coarse_ref,
        [(512, 192, keep_ref), (768, 192, side_ref)],
        5,
    )
    resid = []
    for y in range(HALO, HALO + YT):
        resid.append(((r_ref[y] - keep_ref[y]) + spread(side_ref, y))[inner])
    resid = jnp.concatenate(resid, axis=0)
    change = product(split(sum_ref[...].reshape(YT * XT, 192)), fine_ref, 0, 192)
    change = change + product(
        split(csum_ref[own, inner].reshape(YT * XT, 96)), coarse_ref, 256, 192
    )
    for f, value in enumerate((change, resid)):
        turned = jnp.transpose(value)
        for c in range(3):
            for g in range(8):
                rows = turned[c * NZ + g * 8 : c * NZ + g * 8 + 8]
                for h in range(2):
                    at = h * 48 + f * 24 + c * 8
                    out_ref[g, at : at + 8, :] = rows[:, h * 128 : h * 128 + 128]


def shape(*dims, dtype=F32):
    return jax.ShapeDtypeStruct(dims, dtype)


def swaps(line, start):
    pairs = [(line[i], line[i + 1]) for i in range(start, len(line) - 1, 2)]
    return pairs + [(b, a) for a, b in pairs]


def on_device(right_side, start_field, layer_material, stiffness, line_factors):
    size_y = lax.axis_size("gy")
    packed = pl.pallas_call(
        pack_kernel,
        out_shape=shape(8 * ROWS, 128),
        in_specs=[HBM, HBM, HBM],
        out_specs=VMEM,
        scratch_shapes=[
            pltpu.VMEM((6, 8, 8, 256), F32),
            pltpu.SMEM((8,), jnp.int32),
            pltpu.SemaphoreType.DMA((6,)),
            pltpu.SemaphoreType.DMA,
        ],
        compiler_params=params(60),
        name="pack",
    )(right_side, start_field, layer_material)
    got = lax.all_to_all(packed.reshape(8, ROWS, 128), "gz", 0, 0, tiled=True)
    mats = got[:, 96, :8].reshape(-1).astype(jnp.int32)

    onehot = (mats[:, None] == jnp.arange(stiffness.shape[0])[None, :]).astype(F32)
    sten = jnp.sum(onehot[:, :, None] * stiffness.reshape(1, -1, 27), axis=1)
    sten = jnp.pad(sten, ((0, 0), (0, 128 - 27)))
    fine, coarse, first = pl.pallas_call(
        setup_kernel,
        out_shape=(
            shape(2, 192, 1024, dtype=BF16),
            shape(2, 96, 1024, dtype=BF16),
            shape(2, 256, 512, dtype=BF16),
        ),
        in_specs=[SMEM, SMEM, VMEM],
        out_specs=(VMEM, VMEM, VMEM),
        scratch_shapes=[
            pltpu.VMEM((192, 192), F32),
            pltpu.VMEM((96, 96), F32),
        ],
        compiler_params=params(),
        name="setup",
    )(mats, line_factors.reshape(-1), sten)

    own, send1, send2 = pl.pallas_call(
        turn_kernel,
        out_shape=(shape(YT, XT, 384), shape(HALO, XT, 384), shape(HALO, XT, 384)),
        in_specs=[VMEM],
        out_specs=(VMEM, VMEM, VMEM),
        compiler_params=params(),
        name="turn",
    )(got)
    count_x, count_y, count_z = (lax.axis_size(axis) for axis in ("gx", "gy", "gz"))
    y1 = lax.ppermute(send1, "gy", swaps(range(count_y), 0))
    y2 = lax.ppermute(send2, "gy", swaps(range(count_y), 1))
    send1, send2 = pl.pallas_call(
        sides_kernel,
        out_shape=(shape(YW, XH, 384), shape(YW, XH, 384)),
        in_specs=[VMEM, VMEM, VMEM, pl.BlockSpec(memory_space=pl.ANY)],
        out_specs=(VMEM, VMEM),
        compiler_params=params(),
        name="sides",
    )(own, y1, y2, fine)
    along = [(i % count_z) * count_x + i // count_z for i in range(count_x * count_z)]
    x1 = lax.ppermute(send1, ("gz", "gx"), swaps(along, 0))
    x2 = lax.ppermute(send2, ("gz", "gx"), swaps(along, 1))

    out = pl.pallas_call(
        cycle_kernel,
        out_shape=shape(8, 96, 128),
        in_specs=[VMEM] * 8,
        out_specs=VMEM,
        scratch_shapes=[
            pltpu.VMEM((YW, XW, 384), F32),
            pltpu.VMEM((YW, XW, 192), F32),
            pltpu.VMEM((YW, XW, 192), F32),
            pltpu.VMEM((YW, XW, 192), F32),
            pltpu.VMEM((YT, XT, 192), F32),
            pltpu.VMEM((YW, XW, 96), F32),
            pltpu.VMEM((YW, XW, 96), F32),
            pltpu.VMEM((YW, XW, 96), F32),
            pltpu.VMEM((YW, XW, 96), F32),
        ],
        compiler_params=params(),
        name="cycle",
    )(own, y1, y2, x1, x2, fine, coarse, first)
    back = lax.all_to_all(out, "gz", 0, 0, tiled=True)
    return pl.pallas_call(
        unpack_kernel,
        out_shape=(shape(8, 3, 8, 256), shape(8, 3, 8, 256)),
        in_specs=[VMEM, VMEM],
        out_specs=(HBM, HBM),
        scratch_shapes=[pltpu.VMEM((6, 8, 8, 256), F32), pltpu.SemaphoreType.DMA((6,))],
        compiler_params=params(),
        name="unpack",
    )(back.reshape(768, 128), start_field)


def solution(mesh):
    return jax.shard_map(
        on_device,
        mesh=mesh,
        in_specs=(P("gz", None, "gy", "gx"), P("gz", None, "gy", "gx"), P("gz"), P(), P()),
        out_specs=(P("gz", None, "gy", "gx"), P("gz", None, "gy", "gx")),
        check_vma=False,
    )
```

```python
import jax
import jax.numpy as jnp
from jax import lax
from jax.experimental import pallas as pl
from jax.experimental.pallas import tpu as pltpu
from jax.sharding import PartitionSpec as P

F32 = jnp.float32
BF16 = jnp.bfloat16
HALO = 7
XH = 8
XT = 32
XW = XT + 2 * XH
YT = 8
YW = YT + 2 * HALO
RH = HALO - 1
RW = YT + 2 * RH
ROWS = 104
NZ = 64
NC = NZ // 2
VMEM = pl.BlockSpec(memory_space=pltpu.VMEM)
HBM = pl.BlockSpec(memory_space=pltpu.HBM)
SMEM = pl.BlockSpec(memory_space=pltpu.SMEM)


def params(mib=40):
    return pltpu.CompilerParams(vmem_limit_bytes=mib * 1024 * 1024)


def swap_blocks(tile):
    sub = lax.broadcasted_iota(jnp.int32, tile.shape, 1)
    blk = lax.broadcasted_iota(jnp.int32, tile.shape, 2) // 32
    for bit in (1, 2, 4):
        up = pltpu.roll(pltpu.roll(tile, 8 - bit, axis=1), 32 * bit, axis=2)
        down = pltpu.roll(pltpu.roll(tile, bit, axis=1), 256 - 32 * bit, axis=2)
        in_sub = (sub & bit) != 0
        in_blk = (blk & bit) != 0
        tile = jnp.where(in_sub == in_blk, tile, jnp.where(in_blk, up, down))
    return tile


def fetches(pairs, sems):
    copies = [pltpu.make_async_copy(src, dst, sems.at[i]) for i, (src, dst) in enumerate(pairs)]
    for copy in copies:
        copy.start()
    return copies


def pack_kernel(load_hbm, start_hbm, mats_hbm, out_ref, in_ref, mats_ref, sems, mats_sem):
    mats_copy = pltpu.make_async_copy(mats_hbm, mats_ref, mats_sem)
    mats_copy.start()
    order = [(f, c) for f in range(2) for c in range(3)]
    copies = fetches(
        [((load_hbm, start_hbm)[f].at[:, c], in_ref.at[i]) for i, (f, c) in enumerate(order)], sems
    )
    for i, (f, c) in enumerate(order):
        copies[i].wait()
        tile = swap_blocks(in_ref[i])
        for z in range(8):
            for h in range(2):
                at = h * 48 + f * 24 + c * 8 + z
                out_ref[pl.ds(at, 8, stride=ROWS), :] = tile[z, :, h * 128 : h * 128 + 128]
    mats_copy.wait()
    row = lax.broadcasted_iota(jnp.int32, (8, 128), 0)
    ids = jnp.zeros((8, 128), jnp.int32)
    for z in range(8):
        ids = jnp.where(row == z, mats_ref[z], ids)
    for k in range(8):
        out_ref[k * ROWS + 96 : k * ROWS + 104, :] = ids.astype(F32)


def unpack_kernel(got_ref, start_ref, field_hbm, resid_hbm, out_ref, sems):
    copies = []
    for f, ref in enumerate((field_hbm, resid_hbm)):
        for c in range(3):
            halves = []
            for h in range(2):
                at = h * 48 + f * 24 + c * 8
                rows = [got_ref[pl.ds(at + z, 8, stride=96), :] for z in range(8)]
                halves.append(jnp.stack(rows, axis=0))
            tile = swap_blocks(jnp.concatenate(halves, axis=2))
            if f == 0:
                tile = tile + start_ref[:, c]
            i = f * 3 + c
            out_ref[i] = tile
            copy = pltpu.make_async_copy(out_ref.at[i], ref.at[:, c], sems.at[i])
            copy.start()
            copies.append(copy)
    for copy in copies:
        copy.wait()


def exact(a, b):
    return jnp.dot(a, b, precision=lax.Precision.HIGHEST, preferred_element_type=F32)


def folded(value):
    half = value.shape[0] // 2
    lane = lax.broadcasted_iota(jnp.int32, (half, *value.shape[1:]), 2)
    return jnp.where(lane < 192, value[:half], pltpu.roll(value[half:], 192, axis=2))


def unfolded(value):
    return value[:, :, 0:192], pltpu.roll(value, 192, axis=2)[:, :, 0:192]


def turn_kernel(
    got_ref, table_ref, own_ref, q_ref, sten_ref, first_ref, second_ref, down_ref, up_ref
):
    groups = range(8)
    ids = jnp.concatenate([got_ref[g, 96:104] for g in groups], axis=0)
    lane = lax.broadcasted_iota(jnp.int32, ids.shape, 1)
    sten = exact((ids == lane.astype(F32)).astype(F32), table_ref[...])
    sten_ref[...] = sten

    def field(f, c):
        at = f * 24 + c * 8
        return jnp.concatenate(
            [
                jnp.concatenate(
                    [got_ref[g, h * 48 + at : h * 48 + at + 8] for g in groups], axis=0
                )
                for h in range(2)
            ],
            axis=1,
        )

    start = [field(1, c) for c in range(3)]
    q = couple(sten, 1, start)
    diag = couple(sten, 0, start)
    vert = couple(sten, 2, [above_below(part) for part in start])
    lane = lax.broadcasted_iota(jnp.int32, (NZ, 256), 1)
    x, y = lane % XT, lane // XT
    resid = []
    for c in range(3):
        near = jnp.where(x > 0, pltpu.roll(q[c], 1, axis=1), 0.0)
        near = near + jnp.where(x < XT - 1, pltpu.roll(q[c], 255, axis=1), 0.0)
        near = near + jnp.where(y > 0, pltpu.roll(q[c], XT, axis=1), 0.0)
        near = near + jnp.where(y < YT - 1, pltpu.roll(q[c], 256 - XT, axis=1), 0.0)
        resid.append((field(0, c) - (diag[c] - vert[c])) + near)
    own_ref[...] = jnp.transpose(jnp.concatenate(resid, axis=0)).reshape(YT, XT, 192)
    q_ref[...] = jnp.transpose(jnp.concatenate(q, axis=0)).reshape(YT, XT, 192)
    for ref, top, edge in ((down_ref, YT - RH, YT - 1), (up_ref, 0, 0)):
        ref[0:RH, :, 0:192] = own_ref[top : top + RH]
        ref[RH, :, 0:192] = q_ref[edge]
        ref[RH + 1, :, 0:192] = jnp.zeros((XT, 192), F32)
        for r in range(RH):
            ref[RH + 1, r : r + 1, 0:192] = q_ref[top + r, 0:1]
            ref[RH + 1, 8 + r : 9 + r, 0:192] = q_ref[top + r, XT - 1 : XT]
    down, up = folded(down_ref[...]), folded(up_ref[...])
    even = lax.axis_index("gy") % 2 == 0
    first_ref[...] = jnp.where(even, down, up)
    second_ref[...] = jnp.where(even, up, down)


def sides_kernel(
    own_ref, q_ref, y1_ref, y2_ref, after_ref, resid_ref, edge_ref, send1_ref, send2_ref, wide_ref
):
    even_x = lax.axis_index("gz") % 2 == 0
    even_y = lax.axis_index("gy") % 2 == 0
    first, second = y1_ref[...], y2_ref[...]
    sub = lax.broadcasted_iota(jnp.int32, (RW, XH, 192), 1)
    edge_ref[...] = jnp.zeros((RW, XH, 192), F32)
    resid_ref[RH : RH + YT] = own_ref[...]
    for y in range(YT):
        edge_ref[RH + y, 0:1] = q_ref[y, 0:1]
        edge_ref[RH + y, 1:2] = q_ref[y, XT - 1 : XT]
    for at, value, border, inside, mine in (
        (0, jnp.where(even_y, second, first), RH - 1, RH, 0),
        (RH + YT, jnp.where(even_y, first, second), RH + YT, RH + YT - 1, YT - 1),
    ):
        low, high = unfolded(value)
        resid_ref[at : at + 4] = low
        resid_ref[at + 4 : at + RH] = high[0:2]
        resid_ref[border] = resid_ref[border] + q_ref[mine]
        resid_ref[inside] = resid_ref[inside] + high[2]
        for r in range(RH):
            edge_ref[at + r, 0:1] = high[3, r : r + 1]
            edge_ref[at + r, 1:2] = high[3, 8 + r : 9 + r]
    wide_ref[:, :, 0:192] = jnp.where(sub == 7, edge_ref[:, 0:1], resid_ref[:, 0:XH])
    left = folded(wide_ref[...])
    wide_ref[:, :, 0:192] = jnp.where(sub == 0, edge_ref[:, 1:2], resid_ref[:, XT - XH :])
    right = folded(wide_ref[...])
    send1_ref[...] = jnp.where(even_x, right, left)
    send2_ref[...] = jnp.where(even_x, left, right)


def split(value):
    high = value.astype(BF16)
    return high, (value - high.astype(F32)).astype(BF16)


def line_rows(mats_ref, factor_ref, dst_ref, layers, step):
    lane = lax.broadcasted_iota(jnp.int32, (1, 3 * layers), 1)

    def up(z, state):
        base = mats_ref[z * step] * 27
        new = []
        for i in range(3):
            row = jnp.zeros((1, 3 * layers), F32)
            for j in range(3):
                row = jnp.where(lane == j * layers + z, factor_ref[base + i * 3 + j], row)
            for j in range(3):
                row = row + factor_ref[base + 9 + i * 3 + j] * state[j]
            dst_ref[pl.ds(i * layers + z, 1), :] = row
            new.append(row)
        return tuple(new)

    def down(t, state):
        z = layers - 1 - t
        base = mats_ref[z * step] * 27
        new = []
        for i in range(3):
            row = dst_ref[pl.ds(i * layers + z, 1), :]
            for j in range(3):
                row = row + factor_ref[base + 18 + i * 3 + j] * state[j]
            dst_ref[pl.ds(i * layers + z, 1), :] = row
            new.append(row)
        return tuple(new)

    zero = tuple(jnp.zeros((1, 3 * layers), F32) for _ in range(3))
    lax.fori_loop(0, layers, up, zero, unroll=8)
    lax.fori_loop(0, layers, down, zero, unroll=8)


def couple(sten, which, blocks):
    out = []
    for i in range(3):
        total = None
        for j in range(3):
            at = which * 9 + i * 3 + j
            term = sten[:, at : at + 1] * blocks[j]
            total = term if total is None else total + term
        out.append(total)
    return out


def above_below(block):
    row = lax.broadcasted_iota(jnp.int32, block.shape, 0)
    n = block.shape[0]
    low = jnp.where(row == 0, 0.0, pltpu.roll(block, 1, axis=0))
    high = jnp.where(row == n - 1, 0.0, pltpu.roll(block, n - 1, axis=0))
    return low + high


def store_split(ref, at, rows):
    value = jnp.transpose(jnp.concatenate(rows, axis=0))
    high, low = split(value)
    ref[0, :, at : at + value.shape[1]] = high
    ref[1, :, at : at + value.shape[1]] = low


def setup_kernel(
    mats_ref, factor_ref, sten_ref, fine_ref, coarse_ref, line_ref, cline_ref
):
    sten = sten_ref[...]
    line_rows(mats_ref, factor_ref, line_ref, NZ, 1)
    line_rows(mats_ref, factor_ref, cline_ref, NC, 2)

    def level(sten_part, scale, ref, layers):
        blocks = [ref[i * layers : (i + 1) * layers, :] for i in range(3)]
        lateral = couple(sten_part, 1, blocks)
        diag = couple(sten_part, 0, blocks)
        vert = couple(sten_part, 2, [above_below(block) for block in blocks])
        if scale is not None:
            vert = [scale * part for part in vert]
        wide = blocks[0].shape
        r = lax.broadcasted_iota(jnp.int32, wide, 0)
        q = lax.broadcasted_iota(jnp.int32, wide, 1)
        kept = [
            jnp.where(q == r + i * layers, 1.0, 0.0) - (diag[i] - vert[i]) for i in range(3)
        ]
        return blocks, kept, lateral

    blocks, kept, lateral = level(sten, None, line_ref, NZ)
    store_split(fine_ref, 0, blocks)
    store_split(fine_ref, 256, kept)
    store_split(fine_ref, 512, lateral)

    layer_at = lax.broadcasted_iota(jnp.int32, (NC, NZ), 1) // 2
    pairs = (lax.broadcasted_iota(jnp.int32, (NC, NZ), 0) == layer_at).astype(F32)
    layer_at = lax.broadcasted_iota(jnp.int32, (NZ, NC), 0) // 2
    repeats = (lax.broadcasted_iota(jnp.int32, (NZ, NC), 1) == layer_at).astype(F32)

    def paired(part):
        return [exact(pairs, block) for block in part]

    store_split(fine_ref, 768, paired(kept))
    store_split(fine_ref, 896, paired(lateral))

    coarse_sten = sten_ref[pl.ds(0, NC, stride=2), :]
    cblocks, ckept, clateral = level(coarse_sten, 0.25, cline_ref, NC)
    store_split(coarse_ref, 0, ckept)
    store_split(coarse_ref, 128, clateral)
    spread = [exact(repeats, block) for block in cblocks]
    diag = couple(sten, 0, spread)
    vert = couple(sten, 2, [above_below(block) for block in spread])
    store_split(coarse_ref, 256, spread)
    store_split(coarse_ref, 512, [d - v for d, v in zip(diag, vert)])
    store_split(coarse_ref, 768, couple(sten, 1, spread))


def cycle_kernel(
    resid_ref,
    edge_ref,
    x1_ref,
    x2_ref,
    fine_ref,
    coarse_ref,
    out_ref,
    r_ref,
    keep_ref,
    side_ref,
    sum_ref,
    rc_ref,
    ckeep_ref,
    cside_ref,
    csum_ref,
):
    gz, gx, gy = (lax.axis_index(axis) for axis in ("gz", "gx", "gy"))
    at_left = (gx == 0) & (gz == 0)
    at_right = (gx == lax.axis_size("gx") - 1) & (gz == lax.axis_size("gz") - 1)
    at_top = gy == 0
    at_bottom = gy == lax.axis_size("gy") - 1

    def product(halves, w_ref, at, width):
        high, low = halves
        wh = w_ref[0, :, at : at + width]
        wl = w_ref[1, :, at : at + width]

        def dot(a, b):
            return jnp.dot(a, b, preferred_element_type=F32)

        return dot(high, wh) + (dot(high, wl) + dot(low, wh))

    def chunks(lo, hi, size):
        return [(y, min(y + size, hi)) for y in range(lo, hi, size)]

    def apply(src, lanes, lo, hi, w_ref, jobs, size=4):
        for a, b in chunks(lo, hi, size):
            value = src[a:b, :, lanes].reshape((b - a) * XW, -1)
            halves = split(value)
            for at, width, dst in jobs:
                if isinstance(dst, tuple):
                    both = product(halves, w_ref, at, width)
                    for i, part in enumerate(dst):
                        part[a:b] = both[:, i * 128 : i * 128 + 96].reshape(b - a, XW, 96)
                else:
                    dst[a:b] = product(halves, w_ref, at, width).reshape(b - a, XW, width)

    def spread(side, y):
        mid = side[y]
        return (side[y - 1] + side[y + 1]) + (
            pltpu.roll(mid, 1, axis=0) + pltpu.roll(mid, XW - 1, axis=0)
        )

    def clear(ref, lo, hi):
        width = ref.shape[2]

        @pl.when(at_left)
        def _():
            ref[lo:hi, 0:XH] = jnp.zeros((hi - lo, XH, width), F32)

        @pl.when(at_right)
        def _():
            ref[lo:hi, XH + XT :] = jnp.zeros((hi - lo, XH, width), F32)

        if lo < HALO:

            @pl.when(at_top)
            def _():
                ref[lo:HALO] = jnp.zeros((HALO - lo, XW, width), F32)

        if hi > HALO + YT:

            @pl.when(at_bottom)
            def _():
                ref[HALO + YT : hi] = jnp.zeros((hi - HALO - YT, XW, width), F32)

    own = slice(HALO, HALO + YT)
    inner = slice(XH, XH + XT)
    every = slice(None)

    even_x = gz % 2 == 0
    sub = lax.broadcasted_iota(jnp.int32, (RW // 2, XH, 192), 1)
    left = unfolded(jnp.where(even_x, x2_ref[...], x1_ref[...]))
    right = unfolded(jnp.where(even_x, x1_ref[...], x2_ref[...]))
    r_ref[1 : YW - 1, 2 * XH : XT] = resid_ref[:, XH : XT - XH]
    for half in range(2):
        at = slice(half * (RW // 2), (half + 1) * (RW // 2))
        rows = slice(1 + at.start, 1 + at.stop)
        from_left, from_right = left[half], right[half]
        mine_left, mine_right = edge_ref[at, 0:1], edge_ref[at, 1:2]
        r_ref[rows, 0:XH] = jnp.where(sub >= 2, from_left, 0.0) + jnp.where(
            sub == 7, mine_left, 0.0
        )
        r_ref[rows, XH : 2 * XH] = resid_ref[at, 0:XH] + jnp.where(sub == 0, from_left[:, 0:1], 0.0)
        r_ref[rows, XT : XH + XT] = resid_ref[at, XT - XH :] + jnp.where(
            sub == 7, from_right[:, 7:8], 0.0
        )
        r_ref[rows, XH + XT :] = jnp.where(sub <= 5, from_right, 0.0) + jnp.where(
            sub == 0, mine_right, 0.0
        )
    clear(r_ref, 1, YW - 1)
    sum_ref[...] = r_ref[own, inner]

    for sweep in (1, 2):
        lo, hi = sweep, YW - sweep
        apply(r_ref, every, lo, hi, fine_ref, [(256, 192, keep_ref), (512, 192, side_ref)])
        for y in range(lo + 1, hi - 1):
            r_ref[y] = keep_ref[y] + spread(side_ref, y)
        clear(r_ref, lo + 1, hi - 1)
        sum_ref[...] += r_ref[own, inner]

    apply(r_ref, every, 3, YW - 3, fine_ref, [(768, 224, (ckeep_ref, cside_ref))])
    apply(
        r_ref, every, HALO - 1, HALO + YT + 1, fine_ref, [(256, 192, keep_ref), (512, 192, side_ref)], 5
    )
    for y in range(4, YW - 4):
        rc_ref[y] = ckeep_ref[y] + spread(cside_ref, y)
    clear(rc_ref, 4, YW - 4)
    for y in range(HALO, HALO + YT):
        r_ref[y] = keep_ref[y] + spread(side_ref, y)
    csum_ref[HALO - 1 : HALO + YT + 1] = rc_ref[HALO - 1 : HALO + YT + 1]

    for sweep in (4, 5):
        lo, hi = sweep, YW - sweep
        apply(rc_ref, every, lo, hi, coarse_ref, [(0, 224, (ckeep_ref, cside_ref))], 5)
        for y in range(lo + 1, hi - 1):
            rc_ref[y] = ckeep_ref[y] + spread(cside_ref, y)
        clear(rc_ref, lo + 1, hi - 1)
        csum_ref[HALO - 1 : HALO + YT + 1] += rc_ref[HALO - 1 : HALO + YT + 1]

    apply(
        csum_ref,
        every,
        HALO - 1,
        HALO + YT + 1,
        coarse_ref,
        [(512, 192, keep_ref), (768, 192, side_ref)],
        5,
    )
    resid = []
    for y in range(HALO, HALO + YT):
        resid.append(((r_ref[y] - keep_ref[y]) + spread(side_ref, y))[inner])
    resid = jnp.concatenate(resid, axis=0)
    change = product(split(sum_ref[...].reshape(YT * XT, 192)), fine_ref, 0, 192)
    change = change + product(
        split(csum_ref[own, inner].reshape(YT * XT, 96)), coarse_ref, 256, 192
    )
    for f, value in enumerate((change, resid)):
        turned = jnp.transpose(value)
        for c in range(3):
            for g in range(8):
                rows = turned[c * NZ + g * 8 : c * NZ + g * 8 + 8]
                for h in range(2):
                    at = h * 48 + f * 24 + c * 8
                    out_ref[g, at : at + 8, :] = rows[:, h * 128 : h * 128 + 128]


def shape(*dims, dtype=F32):
    return jax.ShapeDtypeStruct(dims, dtype)


def swaps(line, start):
    pairs = [(line[i], line[i + 1]) for i in range(start, len(line) - 1, 2)]
    return pairs + [(b, a) for a, b in pairs]


def on_device(right_side, start_field, layer_material, stiffness, line_factors):
    size_y = lax.axis_size("gy")
    packed = pl.pallas_call(
        pack_kernel,
        out_shape=shape(8 * ROWS, 128),
        in_specs=[HBM, HBM, HBM],
        out_specs=VMEM,
        scratch_shapes=[
            pltpu.VMEM((6, 8, 8, 256), F32),
            pltpu.SMEM((8,), jnp.int32),
            pltpu.SemaphoreType.DMA((6,)),
            pltpu.SemaphoreType.DMA,
        ],
        compiler_params=params(60),
        name="pack",
    )(right_side, start_field, layer_material)
    got = lax.all_to_all(packed.reshape(8, ROWS, 128), "gz", 0, 0, tiled=True)
    mats = got[:, 96:, 0].reshape(-1).astype(jnp.int32)

    table = jnp.pad(stiffness.reshape(-1, 27), ((0, 128 - stiffness.shape[0]), (0, 128 - 27)))
    own, q, sten, send1, send2 = pl.pallas_call(
        turn_kernel,
        out_shape=(
            shape(YT, XT, 192),
            shape(YT, XT, 192),
            shape(NZ, 128),
            shape(4, XT, 384),
            shape(4, XT, 384),
        ),
        in_specs=[VMEM, VMEM],
        out_specs=(VMEM,) * 5,
        scratch_shapes=[pltpu.VMEM((8, XT, 384), F32), pltpu.VMEM((8, XT, 384), F32)],
        compiler_params=params(),
        name="turn",
    )(got, table)
    fine, coarse = pl.pallas_call(
        setup_kernel,
        out_shape=(
            shape(2, 192, 1024, dtype=BF16),
            shape(2, 96, 1024, dtype=BF16),
        ),
        in_specs=[SMEM, SMEM, VMEM],
        out_specs=(VMEM, VMEM),
        scratch_shapes=[
            pltpu.VMEM((192, 192), F32),
            pltpu.VMEM((96, 96), F32),
        ],
        compiler_params=params(),
        name="setup",
    )(mats, line_factors.reshape(-1), sten)

    count_x, count_y, count_z = (lax.axis_size(axis) for axis in ("gx", "gy", "gz"))
    y1 = lax.ppermute(send1, "gy", swaps(range(count_y), 0))
    y2 = lax.ppermute(send2, "gy", swaps(range(count_y), 1))
    resid, edge, send1, send2 = pl.pallas_call(
        sides_kernel,
        out_shape=(
            shape(RW, XT, 192),
            shape(RW, XH, 192),
            shape(RW // 2, XH, 384),
            shape(RW // 2, XH, 384),
        ),
        in_specs=[VMEM, VMEM, VMEM, VMEM, pl.BlockSpec(memory_space=pl.ANY)],
        out_specs=(VMEM,) * 4,
        scratch_shapes=[pltpu.VMEM((RW, XH, 384), F32)],
        compiler_params=params(),
        name="sides",
    )(own, q, y1, y2, fine)
    along = [(i % count_z) * count_x + i // count_z for i in range(count_x * count_z)]
    x1 = lax.ppermute(send1, ("gz", "gx"), swaps(along, 0))
    x2 = lax.ppermute(send2, ("gz", "gx"), swaps(along, 1))

    out = pl.pallas_call(
        cycle_kernel,
        out_shape=shape(8, 96, 128),
        in_specs=[VMEM] * 6,
        out_specs=VMEM,
        scratch_shapes=[
            pltpu.VMEM((YW, XW, 192), F32),
            pltpu.VMEM((YW, XW, 192), F32),
            pltpu.VMEM((YW, XW, 192), F32),
            pltpu.VMEM((YT, XT, 192), F32),
            pltpu.VMEM((YW, XW, 96), F32),
            pltpu.VMEM((YW, XW, 96), F32),
            pltpu.VMEM((YW, XW, 96), F32),
            pltpu.VMEM((YW, XW, 96), F32),
        ],
        compiler_params=params(),
        name="cycle",
    )(resid, edge, x1, x2, fine, coarse)
    back = lax.all_to_all(out, "gz", 0, 0, tiled=True)
    return pl.pallas_call(
        unpack_kernel,
        out_shape=(shape(8, 3, 8, 256), shape(8, 3, 8, 256)),
        in_specs=[VMEM, VMEM],
        out_specs=(HBM, HBM),
        scratch_shapes=[pltpu.VMEM((6, 8, 8, 256), F32), pltpu.SemaphoreType.DMA((6,))],
        compiler_params=params(),
        name="unpack",
    )(back.reshape(768, 128), start_field)


def solution(mesh):
    return jax.shard_map(
        on_device,
        mesh=mesh,
        in_specs=(P("gz", None, "gy", "gx"), P("gz", None, "gy", "gx"), P("gz"), P(), P()),
        out_specs=(P("gz", None, "gy", "gx"), P("gz", None, "gy", "gx")),
        check_vma=False,
    )
```

```python
import jax
import jax.numpy as jnp
from jax import lax
from jax.experimental import pallas as pl
from jax.experimental.pallas import tpu as pltpu
from jax.sharding import PartitionSpec as P

F32 = jnp.float32
BF16 = jnp.bfloat16
HALO = 7
XH = 8
XT = 32
XW = XT + 2 * XH
YT = 8
YW = YT + 2 * HALO
RH = HALO - 1
RW = YT + 2 * RH
ROWS = 104
NZ = 64
NC = NZ // 2
VMEM = pl.BlockSpec(memory_space=pltpu.VMEM)
HBM = pl.BlockSpec(memory_space=pltpu.HBM)
SMEM = pl.BlockSpec(memory_space=pltpu.SMEM)


def params(mib=40):
    return pltpu.CompilerParams(vmem_limit_bytes=mib * 1024 * 1024)


def swap_blocks(tile):
    sub = lax.broadcasted_iota(jnp.int32, tile.shape, 1)
    blk = lax.broadcasted_iota(jnp.int32, tile.shape, 2) // 32
    for bit in (1, 2, 4):
        up = pltpu.roll(pltpu.roll(tile, 8 - bit, axis=1), 32 * bit, axis=2)
        down = pltpu.roll(pltpu.roll(tile, bit, axis=1), 256 - 32 * bit, axis=2)
        in_sub = (sub & bit) != 0
        in_blk = (blk & bit) != 0
        tile = jnp.where(in_sub == in_blk, tile, jnp.where(in_blk, up, down))
    return tile


def fetches(pairs, sems):
    copies = [pltpu.make_async_copy(src, dst, sems.at[i]) for i, (src, dst) in enumerate(pairs)]
    for copy in copies:
        copy.start()
    return copies


def pack_kernel(load_hbm, start_hbm, mats_hbm, out_ref, in_ref, mats_ref, sems, mats_sem):
    mats_copy = pltpu.make_async_copy(mats_hbm, mats_ref, mats_sem)
    mats_copy.start()
    order = [(f, c) for f in range(2) for c in range(3)]
    copies = fetches(
        [((load_hbm, start_hbm)[f].at[:, c], in_ref.at[i]) for i, (f, c) in enumerate(order)], sems
    )
    for i, (f, c) in enumerate(order):
        copies[i].wait()
        tile = swap_blocks(in_ref[i])
        for z in range(8):
            for h in range(2):
                at = h * 48 + f * 24 + c * 8 + z
                out_ref[pl.ds(at, 8, stride=ROWS), :] = tile[z, :, h * 128 : h * 128 + 128]
    mats_copy.wait()
    row = lax.broadcasted_iota(jnp.int32, (8, 128), 0)
    ids = jnp.zeros((8, 128), jnp.int32)
    for z in range(8):
        ids = jnp.where(row == z, mats_ref[z], ids)
    for k in range(8):
        out_ref[k * ROWS + 96 : k * ROWS + 104, :] = ids.astype(F32)


def unpack_kernel(got_ref, start_ref, field_hbm, resid_hbm, out_ref, sems):
    copies = []
    for f, ref in enumerate((field_hbm, resid_hbm)):
        for c in range(3):
            halves = []
            for h in range(2):
                at = h * 48 + f * 24 + c * 8
                rows = [got_ref[pl.ds(at + z, 8, stride=96), :] for z in range(8)]
                halves.append(jnp.stack(rows, axis=0))
            tile = swap_blocks(jnp.concatenate(halves, axis=2))
            if f == 0:
                tile = tile + start_ref[:, c]
            i = f * 3 + c
            out_ref[i] = tile
            copy = pltpu.make_async_copy(out_ref.at[i], ref.at[:, c], sems.at[i])
            copy.start()
            copies.append(copy)
    for copy in copies:
        copy.wait()


def exact(a, b):
    return jnp.dot(a, b, precision=lax.Precision.HIGHEST, preferred_element_type=F32)


def folded(value):
    half = value.shape[0] // 2
    lane = lax.broadcasted_iota(jnp.int32, (half, *value.shape[1:]), 2)
    return jnp.where(lane < 192, value[:half], pltpu.roll(value[half:], 192, axis=2))


def unfolded(value):
    return value[:, :, 0:192], pltpu.roll(value, 192, axis=2)[:, :, 0:192]


def turn_kernel(
    got_ref, table_ref, own_ref, q_ref, sten_ref, first_ref, second_ref, down_ref, up_ref
):
    groups = range(8)
    ids = jnp.concatenate([got_ref[g, 96:104] for g in groups], axis=0)
    lane = lax.broadcasted_iota(jnp.int32, ids.shape, 1)
    sten = exact((ids == lane.astype(F32)).astype(F32), table_ref[...])
    sten_ref[...] = sten

    def field(f, c):
        at = f * 24 + c * 8
        return jnp.concatenate(
            [
                jnp.concatenate(
                    [got_ref[g, h * 48 + at : h * 48 + at + 8] for g in groups], axis=0
                )
                for h in range(2)
            ],
            axis=1,
        )

    start = [field(1, c) for c in range(3)]
    q = couple(sten, 1, start)
    diag = couple(sten, 0, start)
    vert = couple(sten, 2, [above_below(part) for part in start])
    lane = lax.broadcasted_iota(jnp.int32, (NZ, 256), 1)
    x, y = lane % XT, lane // XT
    resid = []
    for c in range(3):
        near = jnp.where(x > 0, pltpu.roll(q[c], 1, axis=1), 0.0)
        near = near + jnp.where(x < XT - 1, pltpu.roll(q[c], 255, axis=1), 0.0)
        near = near + jnp.where(y > 0, pltpu.roll(q[c], XT, axis=1), 0.0)
        near = near + jnp.where(y < YT - 1, pltpu.roll(q[c], 256 - XT, axis=1), 0.0)
        resid.append((field(0, c) - (diag[c] - vert[c])) + near)
    own_ref[...] = jnp.transpose(jnp.concatenate(resid, axis=0)).reshape(YT, XT, 192)
    q_ref[...] = jnp.transpose(jnp.concatenate(q, axis=0)).reshape(YT, XT, 192)
    for ref, top, edge in ((down_ref, YT - RH, YT - 1), (up_ref, 0, 0)):
        ref[0:RH, :, 0:192] = own_ref[top : top + RH]
        ref[RH, :, 0:192] = q_ref[edge]
        ref[RH + 1, :, 0:192] = jnp.zeros((XT, 192), F32)
        for r in range(RH):
            ref[RH + 1, r : r + 1, 0:192] = q_ref[top + r, 0:1]
            ref[RH + 1, 8 + r : 9 + r, 0:192] = q_ref[top + r, XT - 1 : XT]
    down, up = folded(down_ref[...]), folded(up_ref[...])
    even = lax.axis_index("gy") % 2 == 0
    first_ref[...] = jnp.where(even, down, up)
    second_ref[...] = jnp.where(even, up, down)


def sides_kernel(
    own_ref, q_ref, y1_ref, y2_ref, after_ref, resid_ref, edge_ref, send1_ref, send2_ref, wide_ref
):
    even_x = lax.axis_index("gz") % 2 == 0
    even_y = lax.axis_index("gy") % 2 == 0
    first, second = y1_ref[...], y2_ref[...]
    sub = lax.broadcasted_iota(jnp.int32, (RW, XH, 192), 1)
    edge_ref[...] = jnp.zeros((RW, XH, 192), F32)
    resid_ref[RH : RH + YT] = own_ref[...]
    for y in range(YT):
        edge_ref[RH + y, 0:1] = q_ref[y, 0:1]
        edge_ref[RH + y, 1:2] = q_ref[y, XT - 1 : XT]
    for at, value, border, inside, mine in (
        (0, jnp.where(even_y, second, first), RH - 1, RH, 0),
        (RH + YT, jnp.where(even_y, first, second), RH + YT, RH + YT - 1, YT - 1),
    ):
        low, high = unfolded(value)
        resid_ref[at : at + 4] = low
        resid_ref[at + 4 : at + RH] = high[0:2]
        resid_ref[border] = resid_ref[border] + q_ref[mine]
        resid_ref[inside] = resid_ref[inside] + high[2]
        for r in range(RH):
            edge_ref[at + r, 0:1] = high[3, r : r + 1]
            edge_ref[at + r, 1:2] = high[3, 8 + r : 9 + r]
    wide_ref[:, :, 0:192] = jnp.where(sub == 7, edge_ref[:, 0:1], resid_ref[:, 0:XH])
    left = folded(wide_ref[...])
    wide_ref[:, :, 0:192] = jnp.where(sub == 0, edge_ref[:, 1:2], resid_ref[:, XT - XH :])
    right = folded(wide_ref[...])
    send1_ref[...] = jnp.where(even_x, right, left)
    send2_ref[...] = jnp.where(even_x, left, right)


def split(value):
    high = value.astype(BF16)
    return high, (value - high.astype(F32)).astype(BF16)


def line_rows(mats_ref, factor_ref, dst_ref, layers, step):
    lane = lax.broadcasted_iota(jnp.int32, (1, 3 * layers), 1)

    def up(z, state):
        base = mats_ref[z * step] * 27
        new = []
        for i in range(3):
            row = jnp.zeros((1, 3 * layers), F32)
            for j in range(3):
                row = jnp.where(lane == j * layers + z, factor_ref[base + i * 3 + j], row)
            for j in range(3):
                row = row + factor_ref[base + 9 + i * 3 + j] * state[j]
            dst_ref[pl.ds(i * layers + z, 1), :] = row
            new.append(row)
        return tuple(new)

    def down(t, state):
        z = layers - 1 - t
        base = mats_ref[z * step] * 27
        new = []
        for i in range(3):
            row = dst_ref[pl.ds(i * layers + z, 1), :]
            for j in range(3):
                row = row + factor_ref[base + 18 + i * 3 + j] * state[j]
            dst_ref[pl.ds(i * layers + z, 1), :] = row
            new.append(row)
        return tuple(new)

    zero = tuple(jnp.zeros((1, 3 * layers), F32) for _ in range(3))
    lax.fori_loop(0, layers, up, zero, unroll=8)
    lax.fori_loop(0, layers, down, zero, unroll=8)


def couple(sten, which, blocks):
    out = []
    for i in range(3):
        total = None
        for j in range(3):
            at = which * 9 + i * 3 + j
            term = sten[:, at : at + 1] * blocks[j]
            total = term if total is None else total + term
        out.append(total)
    return out


def above_below(block):
    row = lax.broadcasted_iota(jnp.int32, block.shape, 0)
    n = block.shape[0]
    low = jnp.where(row == 0, 0.0, pltpu.roll(block, 1, axis=0))
    high = jnp.where(row == n - 1, 0.0, pltpu.roll(block, n - 1, axis=0))
    return low + high


def store_split(ref, at, rows):
    value = jnp.transpose(jnp.concatenate(rows, axis=0))
    high, low = split(value)
    ref[0, :, at : at + value.shape[1]] = high
    ref[1, :, at : at + value.shape[1]] = low


def lines_kernel(mats_ref, factor_ref, line_ref, cline_ref):
    line_rows(mats_ref, factor_ref, line_ref, NZ, 1)
    line_rows(mats_ref, factor_ref, cline_ref, NC, 2)


def setup_kernel(line_ref, cline_ref, sten_ref, after_ref, fine_ref, coarse_ref):
    sten = sten_ref[...]

    def level(sten_part, scale, ref, layers):
        blocks = [ref[i * layers : (i + 1) * layers, :] for i in range(3)]
        lateral = couple(sten_part, 1, blocks)
        diag = couple(sten_part, 0, blocks)
        vert = couple(sten_part, 2, [above_below(block) for block in blocks])
        if scale is not None:
            vert = [scale * part for part in vert]
        wide = blocks[0].shape
        r = lax.broadcasted_iota(jnp.int32, wide, 0)
        q = lax.broadcasted_iota(jnp.int32, wide, 1)
        kept = [
            jnp.where(q == r + i * layers, 1.0, 0.0) - (diag[i] - vert[i]) for i in range(3)
        ]
        return blocks, kept, lateral

    blocks, kept, lateral = level(sten, None, line_ref, NZ)
    store_split(fine_ref, 0, blocks)
    store_split(fine_ref, 256, kept)
    store_split(fine_ref, 512, lateral)

    layer_at = lax.broadcasted_iota(jnp.int32, (NC, NZ), 1) // 2
    pairs = (lax.broadcasted_iota(jnp.int32, (NC, NZ), 0) == layer_at).astype(F32)
    layer_at = lax.broadcasted_iota(jnp.int32, (NZ, NC), 0) // 2
    repeats = (lax.broadcasted_iota(jnp.int32, (NZ, NC), 1) == layer_at).astype(F32)

    def paired(part):
        return [exact(pairs, block) for block in part]

    store_split(fine_ref, 768, paired(kept))
    store_split(fine_ref, 896, paired(lateral))

    coarse_sten = sten_ref[pl.ds(0, NC, stride=2), :]
    cblocks, ckept, clateral = level(coarse_sten, 0.25, cline_ref, NC)
    store_split(coarse_ref, 0, ckept)
    store_split(coarse_ref, 128, clateral)
    spread = [exact(repeats, block) for block in cblocks]
    diag = couple(sten, 0, spread)
    vert = couple(sten, 2, [above_below(block) for block in spread])
    store_split(coarse_ref, 256, spread)
    store_split(coarse_ref, 512, [d - v for d, v in zip(diag, vert)])
    store_split(coarse_ref, 768, couple(sten, 1, spread))


def cycle_kernel(
    resid_ref,
    edge_ref,
    x1_ref,
    x2_ref,
    fine_ref,
    coarse_ref,
    out_ref,
    r_ref,
    keep_ref,
    side_ref,
    sum_ref,
    rc_ref,
    ckeep_ref,
    cside_ref,
    csum_ref,
):
    gz, gx, gy = (lax.axis_index(axis) for axis in ("gz", "gx", "gy"))

    def unless(outside):
        return jnp.where(outside, 0.0, 1.0).astype(F32)

    at_left = unless((gx == 0) & (gz == 0))
    at_right = unless((gx == lax.axis_size("gx") - 1) & (gz == lax.axis_size("gz") - 1))
    at_top = unless(gy == 0)
    at_bottom = unless(gy == lax.axis_size("gy") - 1)

    def inside(value, y):
        value = jnp.concatenate(
            [value[0:XH] * at_left, value[XH : XH + XT], value[XH + XT :] * at_right], axis=0
        )
        if y < HALO:
            value = value * at_top
        if y >= HALO + YT:
            value = value * at_bottom
        return value

    def product(halves, w_ref, at, width):
        high, low = halves
        wh = w_ref[0, :, at : at + width]
        wl = w_ref[1, :, at : at + width]

        def dot(a, b):
            return jnp.dot(a, b, preferred_element_type=F32)

        return dot(high, wh) + (dot(high, wl) + dot(low, wh))

    def chunks(lo, hi, size):
        return [(y, min(y + size, hi)) for y in range(lo, hi, size)]

    def stage(src, lo, hi, w_ref, jobs, emit, size=4):
        ready = lo + 1
        for a, b in chunks(lo, hi, size):
            halves = split(src[a:b].reshape((b - a) * XW, -1))
            for at, width, dst in jobs:
                value = product(halves, w_ref, at, width)
                if isinstance(dst, tuple):
                    for i, part in enumerate(dst):
                        part[a:b] = value[:, i * 128 : i * 128 + 96].reshape(b - a, XW, 96)
                else:
                    dst[a:b] = value.reshape(b - a, XW, width)
            for y in range(ready, a - 1):
                emit(y)
            ready = max(ready, a - 1)
        for y in range(ready, hi - 1):
            emit(y)

    def spread(side, y):
        mid = side[y]
        return (side[y - 1] + side[y + 1]) + (
            pltpu.roll(mid, 1, axis=0) + pltpu.roll(mid, XW - 1, axis=0)
        )

    own = slice(HALO, HALO + YT)
    inner = slice(XH, XH + XT)

    even_x = gz % 2 == 0
    sub = lax.broadcasted_iota(jnp.int32, (RW // 2, XH, 192), 1)
    left = unfolded(jnp.where(even_x, x2_ref[...], x1_ref[...]))
    right = unfolded(jnp.where(even_x, x1_ref[...], x2_ref[...]))
    r_ref[1 : YW - 1, 2 * XH : XT] = resid_ref[:, XH : XT - XH]
    for half in range(2):
        at = slice(half * (RW // 2), (half + 1) * (RW // 2))
        rows = slice(1 + at.start, 1 + at.stop)
        from_left, from_right = left[half], right[half]
        mine_left, mine_right = edge_ref[at, 0:1], edge_ref[at, 1:2]
        r_ref[rows, 0:XH] = jnp.where(sub >= 2, from_left, 0.0) + jnp.where(
            sub == 7, mine_left, 0.0
        )
        r_ref[rows, XH : 2 * XH] = resid_ref[at, 0:XH] + jnp.where(sub == 0, from_left[:, 0:1], 0.0)
        r_ref[rows, XT : XH + XT] = resid_ref[at, XT - XH :] + jnp.where(
            sub == 7, from_right[:, 7:8], 0.0
        )
        r_ref[rows, XH + XT :] = jnp.where(sub <= 5, from_right, 0.0) + jnp.where(
            sub == 0, mine_right, 0.0
        )
    for y in range(1, YW - 1):
        r_ref[y] = inside(r_ref[y], y)
    sum_ref[...] = r_ref[own, inner]

    def next_fine(y):
        r_ref[y] = inside(keep_ref[y] + spread(side_ref, y), y)

    def next_coarse(y):
        rc_ref[y] = inside(ckeep_ref[y] + spread(cside_ref, y), y)

    for sweep in (1, 2):
        stage(
            r_ref,
            sweep,
            YW - sweep,
            fine_ref,
            [(256, 192, keep_ref), (512, 192, side_ref)],
            next_fine,
        )
        sum_ref[...] += r_ref[own, inner]

    stage(r_ref, 3, YW - 3, fine_ref, [(768, 224, (ckeep_ref, cside_ref))], next_coarse)
    stage(
        r_ref,
        HALO - 1,
        HALO + YT + 1,
        fine_ref,
        [(256, 192, keep_ref), (512, 192, side_ref)],
        next_fine,
        5,
    )
    near = slice(HALO - 1, HALO + YT + 1)
    csum_ref[near] = rc_ref[near]
    for sweep in (4, 5):
        stage(
            rc_ref, sweep, YW - sweep, coarse_ref, [(0, 224, (ckeep_ref, cside_ref))], next_coarse
        )
        csum_ref[near] += rc_ref[near]

    resid = []

    def last(y):
        resid.append(((r_ref[y] - keep_ref[y]) + spread(side_ref, y))[inner])

    stage(
        csum_ref,
        HALO - 1,
        HALO + YT + 1,
        coarse_ref,
        [(512, 192, keep_ref), (768, 192, side_ref)],
        last,
        5,
    )
    resid = jnp.concatenate(resid, axis=0)
    change = product(split(sum_ref[...].reshape(YT * XT, 192)), fine_ref, 0, 192)
    change = change + product(
        split(csum_ref[own, inner].reshape(YT * XT, 96)), coarse_ref, 256, 192
    )
    for f, value in enumerate((change, resid)):
        turned = jnp.transpose(value)
        for c in range(3):
            for g in range(8):
                rows = turned[c * NZ + g * 8 : c * NZ + g * 8 + 8]
                for h in range(2):
                    at = h * 48 + f * 24 + c * 8
                    out_ref[g, at : at + 8, :] = rows[:, h * 128 : h * 128 + 128]


def shape(*dims, dtype=F32):
    return jax.ShapeDtypeStruct(dims, dtype)


def swaps(line, start):
    pairs = [(line[i], line[i + 1]) for i in range(start, len(line) - 1, 2)]
    return pairs + [(b, a) for a, b in pairs]


def on_device(right_side, start_field, layer_material, stiffness, line_factors):
    size_y = lax.axis_size("gy")
    packed = pl.pallas_call(
        pack_kernel,
        out_shape=shape(8 * ROWS, 128),
        in_specs=[HBM, HBM, HBM],
        out_specs=VMEM,
        scratch_shapes=[
            pltpu.VMEM((6, 8, 8, 256), F32),
            pltpu.SMEM((8,), jnp.int32),
            pltpu.SemaphoreType.DMA((6,)),
            pltpu.SemaphoreType.DMA,
        ],
        compiler_params=params(60),
        name="pack",
    )(right_side, start_field, layer_material)
    got = lax.all_to_all(packed.reshape(8, ROWS, 128), "gz", 0, 0, tiled=True)
    mats = got[:, 96:, 0].reshape(-1).astype(jnp.int32)

    table = jnp.pad(stiffness.reshape(-1, 27), ((0, 128 - stiffness.shape[0]), (0, 128 - 27)))
    own, q, sten, send1, send2 = pl.pallas_call(
        turn_kernel,
        out_shape=(
            shape(YT, XT, 192),
            shape(YT, XT, 192),
            shape(NZ, 128),
            shape(4, XT, 384),
            shape(4, XT, 384),
        ),
        in_specs=[VMEM, VMEM],
        out_specs=(VMEM,) * 5,
        scratch_shapes=[pltpu.VMEM((8, XT, 384), F32), pltpu.VMEM((8, XT, 384), F32)],
        compiler_params=params(),
        name="turn",
    )(got, table)
    line, cline = pl.pallas_call(
        lines_kernel,
        out_shape=(shape(192, 192), shape(96, 96)),
        in_specs=[SMEM, SMEM],
        out_specs=(VMEM, VMEM),
        compiler_params=params(),
        name="lines",
    )(mats, line_factors.reshape(-1))
    count_x, count_y, count_z = (lax.axis_size(axis) for axis in ("gx", "gy", "gz"))
    y1 = lax.ppermute(send1, "gy", swaps(range(count_y), 0))
    y2 = lax.ppermute(send2, "gy", swaps(range(count_y), 1))
    resid, edge, send1, send2 = pl.pallas_call(
        sides_kernel,
        out_shape=(
            shape(RW, XT, 192),
            shape(RW, XH, 192),
            shape(RW // 2, XH, 384),
            shape(RW // 2, XH, 384),
        ),
        in_specs=[VMEM, VMEM, VMEM, VMEM, pl.BlockSpec(memory_space=pl.ANY)],
        out_specs=(VMEM,) * 4,
        scratch_shapes=[pltpu.VMEM((RW, XH, 384), F32)],
        compiler_params=params(),
        name="sides",
    )(own, q, y1, y2, line)
    along = [(i % count_z) * count_x + i // count_z for i in range(count_x * count_z)]
    x1 = lax.ppermute(send1, ("gz", "gx"), swaps(along, 0))
    x2 = lax.ppermute(send2, ("gz", "gx"), swaps(along, 1))

    fine, coarse = pl.pallas_call(
        setup_kernel,
        out_shape=(shape(2, 192, 1024, dtype=BF16), shape(2, 96, 1024, dtype=BF16)),
        in_specs=[VMEM, VMEM, VMEM, pl.BlockSpec(memory_space=pl.ANY)],
        out_specs=(VMEM, VMEM),
        compiler_params=params(),
        name="setup",
    )(line, cline, sten, edge)
    out = pl.pallas_call(
        cycle_kernel,
        out_shape=shape(8, 96, 128),
        in_specs=[VMEM] * 6,
        out_specs=VMEM,
        scratch_shapes=[
            pltpu.VMEM((YW, XW, 192), F32),
            pltpu.VMEM((YW, XW, 192), F32),
            pltpu.VMEM((YW, XW, 192), F32),
            pltpu.VMEM((YT, XT, 192), F32),
            pltpu.VMEM((YW, XW, 96), F32),
            pltpu.VMEM((YW, XW, 96), F32),
            pltpu.VMEM((YW, XW, 96), F32),
            pltpu.VMEM((YW, XW, 96), F32),
        ],
        compiler_params=params(),
        name="cycle",
    )(resid, edge, x1, x2, fine, coarse)
    back = lax.all_to_all(out, "gz", 0, 0, tiled=True)
    return pl.pallas_call(
        unpack_kernel,
        out_shape=(shape(8, 3, 8, 256), shape(8, 3, 8, 256)),
        in_specs=[VMEM, VMEM],
        out_specs=(HBM, HBM),
        scratch_shapes=[pltpu.VMEM((6, 8, 8, 256), F32), pltpu.SemaphoreType.DMA((6,))],
        compiler_params=params(),
        name="unpack",
    )(back.reshape(768, 128), start_field)


def solution(mesh):
    return jax.shard_map(
        on_device,
        mesh=mesh,
        in_specs=(P("gz", None, "gy", "gx"), P("gz", None, "gy", "gx"), P("gz"), P(), P()),
        out_specs=(P("gz", None, "gy", "gx"), P("gz", None, "gy", "gx")),
        check_vma=False,
    )
```

```python
import jax
import jax.numpy as jnp
from jax import lax
from jax.experimental import pallas as pl
from jax.experimental.pallas import tpu as pltpu
from jax.sharding import PartitionSpec as P

F32 = jnp.float32
BF16 = jnp.bfloat16
HALO = 7
XH = 8
XT = 32
XW = XT + 2 * XH
YT = 8
YW = YT + 2 * HALO
RH = HALO - 1
RW = YT + 2 * RH
MID = slice(8, 24)
ROWS = 104
NZ = 64
NC = NZ // 2
VMEM = pl.BlockSpec(memory_space=pltpu.VMEM)
HBM = pl.BlockSpec(memory_space=pltpu.HBM)
SMEM = pl.BlockSpec(memory_space=pltpu.SMEM)


def params(mib=40):
    return pltpu.CompilerParams(vmem_limit_bytes=mib * 1024 * 1024)


def swap_blocks(tile):
    sub = lax.broadcasted_iota(jnp.int32, tile.shape, 1)
    blk = lax.broadcasted_iota(jnp.int32, tile.shape, 2) // 32
    for bit in (1, 2, 4):
        up = pltpu.roll(pltpu.roll(tile, 8 - bit, axis=1), 32 * bit, axis=2)
        down = pltpu.roll(pltpu.roll(tile, bit, axis=1), 256 - 32 * bit, axis=2)
        in_sub = (sub & bit) != 0
        in_blk = (blk & bit) != 0
        tile = jnp.where(in_sub == in_blk, tile, jnp.where(in_blk, up, down))
    return tile


def fetches(pairs, sems):
    copies = [pltpu.make_async_copy(src, dst, sems.at[i]) for i, (src, dst) in enumerate(pairs)]
    for copy in copies:
        copy.start()
    return copies


def pack_kernel(load_hbm, start_hbm, mats_hbm, out_ref, in_ref, mats_ref, sems, mats_sem):
    mats_copy = pltpu.make_async_copy(mats_hbm, mats_ref, mats_sem)
    mats_copy.start()
    order = [(f, c) for f in range(2) for c in range(3)]
    copies = fetches(
        [((load_hbm, start_hbm)[f].at[:, c], in_ref.at[i]) for i, (f, c) in enumerate(order)], sems
    )
    for i, (f, c) in enumerate(order):
        copies[i].wait()
        tile = swap_blocks(in_ref[i])
        for z in range(8):
            for h in range(2):
                at = h * 48 + f * 24 + c * 8 + z
                out_ref[pl.ds(at, 8, stride=ROWS), :] = tile[z, :, h * 128 : h * 128 + 128]
    mats_copy.wait()
    row = lax.broadcasted_iota(jnp.int32, (8, 128), 0)
    ids = jnp.zeros((8, 128), jnp.int32)
    for z in range(8):
        ids = jnp.where(row == z, mats_ref[z], ids)
    for k in range(8):
        out_ref[k * ROWS + 96 : k * ROWS + 104, :] = ids.astype(F32)


def unpack_kernel(got_ref, start_ref, field_hbm, resid_hbm, out_ref, sems):
    copies = []
    for f, ref in enumerate((field_hbm, resid_hbm)):
        for c in range(3):
            halves = []
            for h in range(2):
                at = h * 48 + f * 24 + c * 8
                rows = [got_ref[pl.ds(at + z, 8, stride=96), :] for z in range(8)]
                halves.append(jnp.stack(rows, axis=0))
            tile = swap_blocks(jnp.concatenate(halves, axis=2))
            if f == 0:
                tile = tile + start_ref[:, c]
            i = f * 3 + c
            out_ref[i] = tile
            copy = pltpu.make_async_copy(out_ref.at[i], ref.at[:, c], sems.at[i])
            copy.start()
            copies.append(copy)
    for copy in copies:
        copy.wait()


def exact(a, b):
    return jnp.dot(a, b, precision=lax.Precision.HIGHEST, preferred_element_type=F32)


def folded(value):
    half = value.shape[0] // 2
    lane = lax.broadcasted_iota(jnp.int32, (half, *value.shape[1:]), 2)
    return jnp.where(lane < 192, value[:half], pltpu.roll(value[half:], 192, axis=2))


def unfolded(value):
    return value[:, :, 0:192], pltpu.roll(value, 192, axis=2)[:, :, 0:192]


def turn_kernel(
    got_ref, table_ref, own_ref, q_ref, sten_ref, first_ref, second_ref, down_ref, up_ref
):
    groups = range(8)
    ids = jnp.concatenate([got_ref[g, 96:104] for g in groups], axis=0)
    lane = lax.broadcasted_iota(jnp.int32, ids.shape, 1)
    sten = exact((ids == lane.astype(F32)).astype(F32), table_ref[...])
    sten_ref[...] = sten

    def field(f, c):
        at = f * 24 + c * 8
        return jnp.concatenate(
            [
                jnp.concatenate(
                    [got_ref[g, h * 48 + at : h * 48 + at + 8] for g in groups], axis=0
                )
                for h in range(2)
            ],
            axis=1,
        )

    start = [field(1, c) for c in range(3)]
    q = couple(sten, 1, start)
    diag = couple(sten, 0, start)
    vert = couple(sten, 2, [above_below(part) for part in start])
    lane = lax.broadcasted_iota(jnp.int32, (NZ, 256), 1)
    x, y = lane % XT, lane // XT
    resid = []
    for c in range(3):
        near = jnp.where(x > 0, pltpu.roll(q[c], 1, axis=1), 0.0)
        near = near + jnp.where(x < XT - 1, pltpu.roll(q[c], 255, axis=1), 0.0)
        near = near + jnp.where(y > 0, pltpu.roll(q[c], XT, axis=1), 0.0)
        near = near + jnp.where(y < YT - 1, pltpu.roll(q[c], 256 - XT, axis=1), 0.0)
        resid.append((field(0, c) - (diag[c] - vert[c])) + near)
    own_ref[...] = jnp.transpose(jnp.concatenate(resid, axis=0)).reshape(YT, XT, 192)
    q_ref[...] = jnp.transpose(jnp.concatenate(q, axis=0)).reshape(YT, XT, 192)
    for ref, top, edge in ((down_ref, YT - RH, YT - 1), (up_ref, 0, 0)):
        ref[0:RH, :, 0:192] = own_ref[top : top + RH]
        ref[RH, :, 0:192] = q_ref[edge]
        ref[RH + 1, :, 0:192] = jnp.zeros((XT, 192), F32)
        for r in range(RH):
            ref[RH + 1, r : r + 1, 0:192] = q_ref[top + r, 0:1]
            ref[RH + 1, 8 + r : 9 + r, 0:192] = q_ref[top + r, XT - 1 : XT]
    down, up = folded(down_ref[...]), folded(up_ref[...])
    even = lax.axis_index("gy") % 2 == 0
    first_ref[...] = jnp.where(even, down, up)
    second_ref[...] = jnp.where(even, up, down)


def sides_kernel(
    own_ref, q_ref, y1_ref, y2_ref, after_ref, resid_ref, edge_ref, send1_ref, send2_ref, wide_ref
):
    even_x = lax.axis_index("gz") % 2 == 0
    even_y = lax.axis_index("gy") % 2 == 0
    first, second = y1_ref[...], y2_ref[...]
    sub = lax.broadcasted_iota(jnp.int32, (RW, XH, 192), 1)
    edge_ref[...] = jnp.zeros((RW, XH, 192), F32)
    resid_ref[RH : RH + YT] = own_ref[...]
    for y in range(YT):
        edge_ref[RH + y, 0:1] = q_ref[y, 0:1]
        edge_ref[RH + y, 1:2] = q_ref[y, XT - 1 : XT]
    for at, value, border, inside, mine in (
        (0, jnp.where(even_y, second, first), RH - 1, RH, 0),
        (RH + YT, jnp.where(even_y, first, second), RH + YT, RH + YT - 1, YT - 1),
    ):
        low, high = unfolded(value)
        resid_ref[at : at + 4] = low
        resid_ref[at + 4 : at + RH] = high[0:2]
        resid_ref[border] = resid_ref[border] + q_ref[mine]
        resid_ref[inside] = resid_ref[inside] + high[2]
        for r in range(RH):
            edge_ref[at + r, 0:1] = high[3, r : r + 1]
            edge_ref[at + r, 1:2] = high[3, 8 + r : 9 + r]
    wide_ref[:, :, 0:192] = jnp.where(sub == 7, edge_ref[:, 0:1], resid_ref[:, 0:XH])
    left = folded(wide_ref[...])
    wide_ref[:, :, 0:192] = jnp.where(sub == 0, edge_ref[:, 1:2], resid_ref[:, XT - XH :])
    right = folded(wide_ref[...])
    send1_ref[...] = jnp.where(even_x, right, left)
    send2_ref[...] = jnp.where(even_x, left, right)


def split(value):
    high = value.astype(BF16)
    return high, (value - high.astype(F32)).astype(BF16)


def line_rows(mats_ref, factor_ref, dst_ref, layers, step):
    lane = lax.broadcasted_iota(jnp.int32, (1, 3 * layers), 1)

    def up(z, state):
        base = mats_ref[z * step] * 27
        new = []
        for i in range(3):
            row = jnp.zeros((1, 3 * layers), F32)
            for j in range(3):
                row = jnp.where(lane == j * layers + z, factor_ref[base + i * 3 + j], row)
            for j in range(3):
                row = row + factor_ref[base + 9 + i * 3 + j] * state[j]
            dst_ref[pl.ds(i * layers + z, 1), :] = row
            new.append(row)
        return tuple(new)

    def down(t, state):
        z = layers - 1 - t
        base = mats_ref[z * step] * 27
        new = []
        for i in range(3):
            row = dst_ref[pl.ds(i * layers + z, 1), :]
            for j in range(3):
                row = row + factor_ref[base + 18 + i * 3 + j] * state[j]
            dst_ref[pl.ds(i * layers + z, 1), :] = row
            new.append(row)
        return tuple(new)

    zero = tuple(jnp.zeros((1, 3 * layers), F32) for _ in range(3))
    lax.fori_loop(0, layers, up, zero, unroll=8)
    lax.fori_loop(0, layers, down, zero, unroll=8)


def couple(sten, which, blocks):
    out = []
    for i in range(3):
        total = None
        for j in range(3):
            at = which * 9 + i * 3 + j
            term = sten[:, at : at + 1] * blocks[j]
            total = term if total is None else total + term
        out.append(total)
    return out


def above_below(block):
    row = lax.broadcasted_iota(jnp.int32, block.shape, 0)
    n = block.shape[0]
    low = jnp.where(row == 0, 0.0, pltpu.roll(block, 1, axis=0))
    high = jnp.where(row == n - 1, 0.0, pltpu.roll(block, n - 1, axis=0))
    return low + high


def store_split(ref, at, rows):
    value = jnp.transpose(jnp.concatenate(rows, axis=0))
    high, low = split(value)
    ref[0, :, at : at + value.shape[1]] = high
    ref[1, :, at : at + value.shape[1]] = low


def lines_kernel(mats_ref, factor_ref, line_ref, cline_ref):
    line_rows(mats_ref, factor_ref, line_ref, NZ, 1)
    line_rows(mats_ref, factor_ref, cline_ref, NC, 2)


def setup_kernel(line_ref, cline_ref, sten_ref, after_ref, fine_ref, coarse_ref):
    sten = sten_ref[...]

    def level(sten_part, scale, ref, layers):
        blocks = [ref[i * layers : (i + 1) * layers, :] for i in range(3)]
        lateral = couple(sten_part, 1, blocks)
        diag = couple(sten_part, 0, blocks)
        vert = couple(sten_part, 2, [above_below(block) for block in blocks])
        if scale is not None:
            vert = [scale * part for part in vert]
        wide = blocks[0].shape
        r = lax.broadcasted_iota(jnp.int32, wide, 0)
        q = lax.broadcasted_iota(jnp.int32, wide, 1)
        kept = [
            jnp.where(q == r + i * layers, 1.0, 0.0) - (diag[i] - vert[i]) for i in range(3)
        ]
        return blocks, kept, lateral

    blocks, kept, lateral = level(sten, None, line_ref, NZ)
    store_split(fine_ref, 0, blocks)
    store_split(fine_ref, 256, kept)
    store_split(fine_ref, 512, lateral)

    layer_at = lax.broadcasted_iota(jnp.int32, (NC, NZ), 1) // 2
    pairs = (lax.broadcasted_iota(jnp.int32, (NC, NZ), 0) == layer_at).astype(F32)
    layer_at = lax.broadcasted_iota(jnp.int32, (NZ, NC), 0) // 2
    repeats = (lax.broadcasted_iota(jnp.int32, (NZ, NC), 1) == layer_at).astype(F32)

    def paired(part):
        return [exact(pairs, block) for block in part]

    store_split(fine_ref, 768, paired(kept))
    store_split(fine_ref, 896, paired(lateral))

    coarse_sten = sten_ref[pl.ds(0, NC, stride=2), :]
    cblocks, ckept, clateral = level(coarse_sten, 0.25, cline_ref, NC)
    store_split(coarse_ref, 0, ckept)
    store_split(coarse_ref, 128, clateral)
    spread = [exact(repeats, block) for block in cblocks]
    diag = couple(sten, 0, spread)
    vert = couple(sten, 2, [above_below(block) for block in spread])
    store_split(coarse_ref, 256, spread)
    store_split(coarse_ref, 512, [d - v for d, v in zip(diag, vert)])
    store_split(coarse_ref, 768, couple(sten, 1, spread))


def unless(outside):
    return jnp.where(outside, 0.0, 1.0).astype(F32)


def product(halves, w_ref, at, width):
    high, low = halves
    wh = w_ref[0, :, at : at + width]
    wl = w_ref[1, :, at : at + width]

    def dot(a, b):
        return jnp.dot(a, b, preferred_element_type=F32)

    return dot(high, wh) + (dot(high, wl) + dot(low, wh))


def run_cycle(
    sides,
    spread,
    inside,
    fine_ref,
    coarse_ref,
    r_ref,
    keep_ref,
    sum_ref,
    rc_ref,
    ckeep_ref,
    csum_ref,
):
    def stage(i, src, lo, hi, w_ref, at, emit, size=6):
        ready = lo + 1
        for a in range(lo, hi, size):
            b = min(a + size, hi)
            halves = split(src[a:b].reshape((b - a) * XT, -1))
            if isinstance(at, tuple):
                for start, dst in zip(at, (keep_ref, sides[i])):
                    value = product(halves, w_ref, start, 192)
                    dst[a:b] = value.reshape(b - a, XT, 192)
            else:
                value = product(halves, w_ref, at, 224)
                for start, dst in ((0, ckeep_ref), (128, sides[i])):
                    dst[a:b] = value[:, start : start + 96].reshape(b - a, XT, 96)
            for y in range(ready, a - 1):
                emit(i, y)
            ready = max(ready, a - 1)
        for y in range(ready, hi - 1):
            emit(i, y)

    def next_fine(i, y):
        r_ref[y] = inside(keep_ref[y] + spread(i, y), y)

    def next_coarse(i, y):
        rc_ref[y] = inside(ckeep_ref[y] + spread(i, y), y)

    resid = []

    def last(i, y):
        resid.append(((r_ref[y] - keep_ref[y]) + spread(i, y))[MID])

    own = slice(HALO, HALO + YT)
    near = slice(HALO - 1, HALO + YT + 1)
    sum_ref[...] = r_ref[own, MID]
    for i, lo in ((0, 1), (1, 2)):
        stage(i, r_ref, lo, YW - lo, fine_ref, (256, 512), next_fine)
        sum_ref[...] += r_ref[own, MID]
    stage(2, r_ref, 3, YW - 3, fine_ref, 768, next_coarse)
    stage(3, r_ref, near.start, near.stop, fine_ref, (256, 512), next_fine, 5)
    csum_ref[near] = rc_ref[near]
    for i, lo in ((4, 4), (5, 5)):
        stage(i, rc_ref, lo, YW - lo, coarse_ref, 0, next_coarse)
        csum_ref[near] += rc_ref[near]
    stage(6, csum_ref, near.start, near.stop, coarse_ref, (512, 768), last, 5)
    change = product(split(sum_ref[...].reshape(YT * 16, 192)), fine_ref, 0, 192)
    change = change + product(
        split(csum_ref[own, MID].reshape(YT * 16, 96)), coarse_ref, 256, 192
    )
    return change.reshape(YT, 16, 192), jnp.stack(resid, axis=0)


def rows_inside(value, y):
    gy = lax.axis_index("gy")
    if y < HALO:
        value = value * unless(gy == 0)
    if y >= HALO + YT:
        value = value * unless(gy == lax.axis_size("gy") - 1)
    return value


def middle_kernel(resid_ref, fine_ref, coarse_ref, *refs):
    sides, change_ref, out_ref, scratch = refs[:7], refs[7], refs[8], refs[9:]
    r_ref = scratch[0]

    def spread(i, y):
        mid = sides[i][y]
        return (sides[i][y - 1] + sides[i][y + 1]) + (
            pltpu.roll(mid, 1, axis=0) + pltpu.roll(mid, XT - 1, axis=0)
        )

    for y in range(1, YW - 1):
        r_ref[y] = rows_inside(resid_ref[y - 1], y)
    change_ref[...], out_ref[...] = run_cycle(
        sides, spread, rows_inside, fine_ref, coarse_ref, *scratch
    )


def strips_kernel(resid_ref, edge_ref, x1_ref, x2_ref, fine_ref, coarse_ref, *refs):
    saved, change_ref, mid_ref, out_ref = refs[:7], refs[7], refs[8], refs[9]
    side_ref, cside_ref, scratch = refs[10], refs[11], refs[12:]
    r_ref = scratch[0]
    gz, gx = lax.axis_index("gz"), lax.axis_index("gx")
    at_left = unless((gx == 0) & (gz == 0))
    at_right = unless((gx == lax.axis_size("gx") - 1) & (gz == lax.axis_size("gz") - 1))
    sides = [cside_ref if i in (2, 4, 5) else side_ref for i in range(7)]

    def inside(value, y):
        value = jnp.concatenate(
            [value[0:XH] * at_left, value[XH : 3 * XH], value[3 * XH :] * at_right], axis=0
        )
        return rows_inside(value, y)

    def spread(i, y):
        side = sides[i]
        mid = side[y]
        row = jnp.concatenate([mid[0:16], saved[i][y, MID], mid[16:32]], axis=0)
        row = pltpu.roll(row, 1, axis=0) + pltpu.roll(row, XW - 1, axis=0)
        return (side[y - 1] + side[y + 1]) + jnp.concatenate([row[0:16], row[XT:]], axis=0)

    even_x = gz % 2 == 0
    sub = lax.broadcasted_iota(jnp.int32, (RW // 2, XH, 192), 1)
    left = unfolded(jnp.where(even_x, x2_ref[...], x1_ref[...]))
    right = unfolded(jnp.where(even_x, x1_ref[...], x2_ref[...]))
    for half in range(2):
        at = slice(half * (RW // 2), (half + 1) * (RW // 2))
        rows = slice(1 + at.start, 1 + at.stop)
        from_left, from_right = left[half], right[half]
        mine_left, mine_right = edge_ref[at, 0:1], edge_ref[at, 1:2]
        r_ref[rows, 0:XH] = jnp.where(sub >= 2, from_left, 0.0) + jnp.where(
            sub == 7, mine_left, 0.0
        )
        r_ref[rows, XH : 2 * XH] = resid_ref[at, 0:XH] + jnp.where(sub == 0, from_left[:, 0:1], 0.0)
        r_ref[rows, 2 * XH : 3 * XH] = resid_ref[at, XT - XH :] + jnp.where(
            sub == 7, from_right[:, 7:8], 0.0
        )
        r_ref[rows, 3 * XH :] = jnp.where(sub <= 5, from_right, 0.0) + jnp.where(
            sub == 0, mine_right, 0.0
        )
    for y in range(1, YW - 1):
        r_ref[y] = inside(r_ref[y], y)
    change, resid = run_cycle(sides, spread, inside, fine_ref, coarse_ref, *scratch)
    for f, (value, middle) in enumerate(((change, change_ref[...]), (resid, mid_ref[...]))):
        value = jnp.concatenate([value[:, 0:8], middle, value[:, 8:16]], axis=1)
        turned = jnp.transpose(value.reshape(YT * XT, 192))
        for c in range(3):
            for g in range(8):
                rows = turned[c * NZ + g * 8 : c * NZ + g * 8 + 8]
                for h in range(2):
                    at = h * 48 + f * 24 + c * 8
                    out_ref[g, at : at + 8, :] = rows[:, h * 128 : h * 128 + 128]


def cycle_scratch():
    fine, coarse = pltpu.VMEM((YW, XT, 192), F32), pltpu.VMEM((YW, XT, 96), F32)
    return [fine, fine, pltpu.VMEM((YT, 16, 192), F32), coarse, coarse, coarse]


def shape(*dims, dtype=F32):
    return jax.ShapeDtypeStruct(dims, dtype)


def swaps(line, start):
    pairs = [(line[i], line[i + 1]) for i in range(start, len(line) - 1, 2)]
    return pairs + [(b, a) for a, b in pairs]


def on_device(right_side, start_field, layer_material, stiffness, line_factors):
    size_y = lax.axis_size("gy")
    packed = pl.pallas_call(
        pack_kernel,
        out_shape=shape(8 * ROWS, 128),
        in_specs=[HBM, HBM, HBM],
        out_specs=VMEM,
        scratch_shapes=[
            pltpu.VMEM((6, 8, 8, 256), F32),
            pltpu.SMEM((8,), jnp.int32),
            pltpu.SemaphoreType.DMA((6,)),
            pltpu.SemaphoreType.DMA,
        ],
        compiler_params=params(60),
        name="pack",
    )(right_side, start_field, layer_material)
    got = lax.all_to_all(packed.reshape(8, ROWS, 128), "gz", 0, 0, tiled=True)
    mats = got[:, 96:, 0].reshape(-1).astype(jnp.int32)

    table = jnp.pad(stiffness.reshape(-1, 27), ((0, 128 - stiffness.shape[0]), (0, 128 - 27)))
    own, q, sten, send1, send2 = pl.pallas_call(
        turn_kernel,
        out_shape=(
            shape(YT, XT, 192),
            shape(YT, XT, 192),
            shape(NZ, 128),
            shape(4, XT, 384),
            shape(4, XT, 384),
        ),
        in_specs=[VMEM, VMEM],
        out_specs=(VMEM,) * 5,
        scratch_shapes=[pltpu.VMEM((8, XT, 384), F32), pltpu.VMEM((8, XT, 384), F32)],
        compiler_params=params(),
        name="turn",
    )(got, table)
    line, cline = pl.pallas_call(
        lines_kernel,
        out_shape=(shape(192, 192), shape(96, 96)),
        in_specs=[SMEM, SMEM],
        out_specs=(VMEM, VMEM),
        compiler_params=params(),
        name="lines",
    )(mats, line_factors.reshape(-1))
    count_x, count_y, count_z = (lax.axis_size(axis) for axis in ("gx", "gy", "gz"))
    y1 = lax.ppermute(send1, "gy", swaps(range(count_y), 0))
    y2 = lax.ppermute(send2, "gy", swaps(range(count_y), 1))
    resid, edge, send1, send2 = pl.pallas_call(
        sides_kernel,
        out_shape=(
            shape(RW, XT, 192),
            shape(RW, XH, 192),
            shape(RW // 2, XH, 384),
            shape(RW // 2, XH, 384),
        ),
        in_specs=[VMEM, VMEM, VMEM, VMEM, pl.BlockSpec(memory_space=pl.ANY)],
        out_specs=(VMEM,) * 4,
        scratch_shapes=[pltpu.VMEM((RW, XH, 384), F32)],
        compiler_params=params(),
        name="sides",
    )(own, q, y1, y2, line)
    along = [(i % count_z) * count_x + i // count_z for i in range(count_x * count_z)]
    x1 = lax.ppermute(send1, ("gz", "gx"), swaps(along, 0))
    x2 = lax.ppermute(send2, ("gz", "gx"), swaps(along, 1))

    fine, coarse = pl.pallas_call(
        setup_kernel,
        out_shape=(shape(2, 192, 1024, dtype=BF16), shape(2, 96, 1024, dtype=BF16)),
        in_specs=[VMEM, VMEM, VMEM, pl.BlockSpec(memory_space=pl.ANY)],
        out_specs=(VMEM, VMEM),
        compiler_params=params(),
        name="setup",
    )(line, cline, sten, edge)
    sides = tuple(shape(YW, XT, 96 if i in (2, 4, 5) else 192) for i in range(7))
    middle = pl.pallas_call(
        middle_kernel,
        out_shape=(*sides, shape(YT, 16, 192), shape(YT, 16, 192)),
        in_specs=[VMEM] * 3,
        out_specs=(VMEM,) * 9,
        scratch_shapes=cycle_scratch(),
        compiler_params=params(),
        name="middle",
    )(resid, fine, coarse)
    out = pl.pallas_call(
        strips_kernel,
        out_shape=shape(8, 96, 128),
        in_specs=[VMEM] * 15,
        out_specs=VMEM,
        scratch_shapes=[
            pltpu.VMEM((YW, XT, 192), F32),
            pltpu.VMEM((YW, XT, 96), F32),
            *cycle_scratch(),
        ],
        compiler_params=params(),
        name="strips",
    )(resid, edge, x1, x2, fine, coarse, *middle)
    back = lax.all_to_all(out, "gz", 0, 0, tiled=True)
    return pl.pallas_call(
        unpack_kernel,
        out_shape=(shape(8, 3, 8, 256), shape(8, 3, 8, 256)),
        in_specs=[VMEM, VMEM],
        out_specs=(HBM, HBM),
        scratch_shapes=[pltpu.VMEM((6, 8, 8, 256), F32), pltpu.SemaphoreType.DMA((6,))],
        compiler_params=params(),
        name="unpack",
    )(back.reshape(768, 128), start_field)


def solution(mesh):
    return jax.shard_map(
        on_device,
        mesh=mesh,
        in_specs=(P("gz", None, "gy", "gx"), P("gz", None, "gy", "gx"), P("gz"), P(), P()),
        out_specs=(P("gz", None, "gy", "gx"), P("gz", None, "gy", "gx")),
        check_vma=False,
    )
```

```python
import jax
import jax.numpy as jnp
from jax import lax
from jax.experimental import pallas as pl
from jax.experimental.pallas import tpu as pltpu
from jax.sharding import PartitionSpec as P

F32 = jnp.float32
BF16 = jnp.bfloat16
HALO = 7
XH = 8
XT = 32
XW = XT + 2 * XH
YT = 8
YW = YT + 2 * HALO
RH = HALO - 1
RW = YT + 2 * RH
MID = slice(8, 24)
ROWS = 104
NZ = 64
NC = NZ // 2
VMEM = pl.BlockSpec(memory_space=pltpu.VMEM)
HBM = pl.BlockSpec(memory_space=pltpu.HBM)
SMEM = pl.BlockSpec(memory_space=pltpu.SMEM)


def params(mib=40):
    return pltpu.CompilerParams(vmem_limit_bytes=mib * 1024 * 1024)


def swap_blocks(tile, form=0):
    sub = lax.broadcasted_iota(jnp.int32, tile.shape, 1)
    blk = lax.broadcasted_iota(jnp.int32, tile.shape, 2) // 32
    for bit in (1, 2, 4):
        in_sub = (sub & bit) != 0
        in_blk = (blk & bit) != 0
        sub_up, sub_down = pltpu.roll(tile, 8 - bit, axis=1), pltpu.roll(tile, bit, axis=1)
        if form == 0:
            up = pltpu.roll(sub_up, 32 * bit, axis=2)
            down = pltpu.roll(sub_down, 256 - 32 * bit, axis=2)
            tile = jnp.where(in_sub == in_blk, tile, jnp.where(in_blk, up, down))
        else:
            by_sub = jnp.where(in_sub, sub_down, sub_up)
            blk_up = pltpu.roll(tile, 256 - 32 * bit, axis=2)
            blk_down = pltpu.roll(tile, 32 * bit, axis=2)
            by_blk = jnp.where(in_blk, blk_down, blk_up)
            same = in_sub == in_blk
            tile = jnp.where(same, by_blk, by_sub) if form == 1 else jnp.where(same, by_sub, by_blk)
    return tile


def odd_block():
    return lax.axis_index("gx") % 2 == 1


def x_slice():
    gz = lax.axis_index("gz")
    return jnp.where(odd_block(), lax.axis_size("gz") - 1 - gz, gz)


def fetches(pairs, sems):
    copies = [pltpu.make_async_copy(src, dst, sems.at[i]) for i, (src, dst) in enumerate(pairs)]
    for copy in copies:
        copy.start()
    return copies


def pack_kernel(load_hbm, start_hbm, mats_hbm, out_ref, in_ref, mats_ref, sems, mats_sem):
    mats_copy = pltpu.make_async_copy(mats_hbm, mats_ref, mats_sem)
    mats_copy.start()
    order = [(f, c) for f in range(2) for c in range(3)]
    copies = fetches(
        [((load_hbm, start_hbm)[f].at[:, c], in_ref.at[i]) for i, (f, c) in enumerate(order)], sems
    )
    for i, (f, c) in enumerate(order):
        copies[i].wait()
        for form in (0, 1):

            @pl.when(odd_block() == (form == 1))
            def _():
                tile = swap_blocks(in_ref[i], form)
                for z in range(8):
                    for h in range(2):
                        at = h * 48 + f * 24 + c * 8 + z
                        out_ref[pl.ds(at, 8, stride=ROWS), :] = tile[z, :, h * 128 : h * 128 + 128]

    mats_copy.wait()
    row = lax.broadcasted_iota(jnp.int32, (8, 128), 0)
    ids = jnp.zeros((8, 128), jnp.int32)
    for z in range(8):
        ids = jnp.where(row == z, mats_ref[z], ids)
    for k in range(8):
        out_ref[k * ROWS + 96 : k * ROWS + 104, :] = ids.astype(F32)


def unpack_kernel(got_ref, start_ref, field_hbm, resid_hbm, out_ref, sems):
    order = [(f, c) for f in range(2) for c in range(3)]
    copies = [
        pltpu.make_async_copy(
            out_ref.at[i], (field_hbm, resid_hbm)[f].at[:, c], sems.at[i]
        )
        for i, (f, c) in enumerate(order)
    ]

    def fill(form):
        for i, (f, c) in enumerate(order):
            halves = []
            for h in range(2):
                at = h * 48 + f * 24 + c * 8
                rows = [got_ref[pl.ds(at + z, 8, stride=96), :] for z in range(8)]
                halves.append(jnp.stack(rows, axis=0))
            tile = swap_blocks(jnp.concatenate(halves, axis=2), form)
            if f == 0:
                tile = tile + start_ref[:, c]
            out_ref[i] = tile
            copies[i].start()

    for form in (0, 2):

        @pl.when(odd_block() == (form == 2))
        def _():
            fill(form)

    for copy in copies:
        copy.wait()


def exact(a, b):
    return jnp.dot(a, b, precision=lax.Precision.HIGHEST, preferred_element_type=F32)


def folded(value):
    half = value.shape[0] // 2
    lane = lax.broadcasted_iota(jnp.int32, (half, *value.shape[1:]), 2)
    return jnp.where(lane < 192, value[:half], pltpu.roll(value[half:], 192, axis=2))


def unfolded(value):
    return value[:, :, 0:192], pltpu.roll(value, 192, axis=2)[:, :, 0:192]


def turn_kernel(
    got_ref, table_ref, own_ref, q_ref, sten_ref, first_ref, second_ref, down_ref, up_ref
):
    groups = range(8)
    ids = jnp.concatenate([got_ref[g, 96:104] for g in groups], axis=0)
    lane = lax.broadcasted_iota(jnp.int32, ids.shape, 1)
    sten = exact((ids == lane.astype(F32)).astype(F32), table_ref[...])
    sten_ref[...] = sten

    def field(f, c):
        at = f * 24 + c * 8
        return jnp.concatenate(
            [
                jnp.concatenate(
                    [got_ref[g, h * 48 + at : h * 48 + at + 8] for g in groups], axis=0
                )
                for h in range(2)
            ],
            axis=1,
        )

    start = [field(1, c) for c in range(3)]
    q = couple(sten, 1, start)
    diag = couple(sten, 0, start)
    vert = couple(sten, 2, [above_below(part) for part in start])
    lane = lax.broadcasted_iota(jnp.int32, (NZ, 256), 1)
    x, y = lane % XT, lane // XT
    resid = []
    for c in range(3):
        near = jnp.where(x > 0, pltpu.roll(q[c], 1, axis=1), 0.0)
        near = near + jnp.where(x < XT - 1, pltpu.roll(q[c], 255, axis=1), 0.0)
        near = near + jnp.where(y > 0, pltpu.roll(q[c], XT, axis=1), 0.0)
        near = near + jnp.where(y < YT - 1, pltpu.roll(q[c], 256 - XT, axis=1), 0.0)
        resid.append((field(0, c) - (diag[c] - vert[c])) + near)
    own_ref[...] = jnp.transpose(jnp.concatenate(resid, axis=0)).reshape(YT, XT, 192)
    q_ref[...] = jnp.transpose(jnp.concatenate(q, axis=0)).reshape(YT, XT, 192)
    for ref, top, edge in ((down_ref, YT - RH, YT - 1), (up_ref, 0, 0)):
        ref[0:RH, :, 0:192] = own_ref[top : top + RH]
        ref[RH, :, 0:192] = q_ref[edge]
        ref[RH + 1, :, 0:192] = jnp.zeros((XT, 192), F32)
        for r in range(RH):
            ref[RH + 1, r : r + 1, 0:192] = q_ref[top + r, 0:1]
            ref[RH + 1, 8 + r : 9 + r, 0:192] = q_ref[top + r, XT - 1 : XT]
    down, up = folded(down_ref[...]), folded(up_ref[...])
    even = lax.axis_index("gy") % 2 == 0
    first_ref[...] = jnp.where(even, down, up)
    second_ref[...] = jnp.where(even, up, down)


def sides_kernel(
    own_ref, q_ref, y1_ref, y2_ref, after_ref, resid_ref, edge_ref, send1_ref, send2_ref, wide_ref
):
    even_x = x_slice() % 2 == 0
    even_y = lax.axis_index("gy") % 2 == 0
    first, second = y1_ref[...], y2_ref[...]
    sub = lax.broadcasted_iota(jnp.int32, (RW, XH, 192), 1)
    edge_ref[...] = jnp.zeros((RW, XH, 192), F32)
    resid_ref[RH : RH + YT] = own_ref[...]
    for y in range(YT):
        edge_ref[RH + y, 0:1] = q_ref[y, 0:1]
        edge_ref[RH + y, 1:2] = q_ref[y, XT - 1 : XT]
    for at, value, border, inside, mine in (
        (0, jnp.where(even_y, second, first), RH - 1, RH, 0),
        (RH + YT, jnp.where(even_y, first, second), RH + YT, RH + YT - 1, YT - 1),
    ):
        low, high = unfolded(value)
        resid_ref[at : at + 4] = low
        resid_ref[at + 4 : at + RH] = high[0:2]
        resid_ref[border] = resid_ref[border] + q_ref[mine]
        resid_ref[inside] = resid_ref[inside] + high[2]
        for r in range(RH):
            edge_ref[at + r, 0:1] = high[3, r : r + 1]
            edge_ref[at + r, 1:2] = high[3, 8 + r : 9 + r]
    wide_ref[:, :, 0:192] = jnp.where(sub == 7, edge_ref[:, 0:1], resid_ref[:, 0:XH])
    left = folded(wide_ref[...])
    wide_ref[:, :, 0:192] = jnp.where(sub == 0, edge_ref[:, 1:2], resid_ref[:, XT - XH :])
    right = folded(wide_ref[...])
    send1_ref[...] = jnp.where(even_x, right, left)
    send2_ref[...] = jnp.where(even_x, left, right)


def split(value):
    high = value.astype(BF16)
    return high, (value - high.astype(F32)).astype(BF16)


def line_rows(mats_ref, factor_ref, dst_ref, layers, step):
    lane = lax.broadcasted_iota(jnp.int32, (1, 3 * layers), 1)

    def up(z, state):
        base = mats_ref[z * step] * 27
        new = []
        for i in range(3):
            row = jnp.zeros((1, 3 * layers), F32)
            for j in range(3):
                row = jnp.where(lane == j * layers + z, factor_ref[base + i * 3 + j], row)
            for j in range(3):
                row = row + factor_ref[base + 9 + i * 3 + j] * state[j]
            dst_ref[pl.ds(i * layers + z, 1), :] = row
            new.append(row)
        return tuple(new)

    def down(t, state):
        z = layers - 1 - t
        base = mats_ref[z * step] * 27
        new = []
        for i in range(3):
            row = dst_ref[pl.ds(i * layers + z, 1), :]
            for j in range(3):
                row = row + factor_ref[base + 18 + i * 3 + j] * state[j]
            dst_ref[pl.ds(i * layers + z, 1), :] = row
            new.append(row)
        return tuple(new)

    zero = tuple(jnp.zeros((1, 3 * layers), F32) for _ in range(3))
    lax.fori_loop(0, layers, up, zero, unroll=8)
    lax.fori_loop(0, layers, down, zero, unroll=8)


def couple(sten, which, blocks):
    out = []
    for i in range(3):
        total = None
        for j in range(3):
            at = which * 9 + i * 3 + j
            term = sten[:, at : at + 1] * blocks[j]
            total = term if total is None else total + term
        out.append(total)
    return out


def above_below(block):
    row = lax.broadcasted_iota(jnp.int32, block.shape, 0)
    n = block.shape[0]
    low = jnp.where(row == 0, 0.0, pltpu.roll(block, 1, axis=0))
    high = jnp.where(row == n - 1, 0.0, pltpu.roll(block, n - 1, axis=0))
    return low + high


def store_split(ref, at, rows):
    value = jnp.transpose(jnp.concatenate(rows, axis=0))
    high, low = split(value)
    ref[0, :, at : at + value.shape[1]] = high
    ref[1, :, at : at + value.shape[1]] = low


def lines_kernel(mats_ref, factor_ref, line_ref, cline_ref):
    line_rows(mats_ref, factor_ref, line_ref, NZ, 1)
    line_rows(mats_ref, factor_ref, cline_ref, NC, 2)


def setup_kernel(line_ref, cline_ref, sten_ref, after_ref, fine_ref, coarse_ref):
    sten = sten_ref[...]

    def level(sten_part, scale, ref, layers):
        blocks = [ref[i * layers : (i + 1) * layers, :] for i in range(3)]
        lateral = couple(sten_part, 1, blocks)
        diag = couple(sten_part, 0, blocks)
        vert = couple(sten_part, 2, [above_below(block) for block in blocks])
        if scale is not None:
            vert = [scale * part for part in vert]
        wide = blocks[0].shape
        r = lax.broadcasted_iota(jnp.int32, wide, 0)
        q = lax.broadcasted_iota(jnp.int32, wide, 1)
        kept = [
            jnp.where(q == r + i * layers, 1.0, 0.0) - (diag[i] - vert[i]) for i in range(3)
        ]
        return blocks, kept, lateral

    blocks, kept, lateral = level(sten, None, line_ref, NZ)
    store_split(fine_ref, 0, blocks)
    store_split(fine_ref, 256, kept)
    store_split(fine_ref, 512, lateral)

    layer_at = lax.broadcasted_iota(jnp.int32, (NC, NZ), 1) // 2
    pairs = (lax.broadcasted_iota(jnp.int32, (NC, NZ), 0) == layer_at).astype(F32)
    layer_at = lax.broadcasted_iota(jnp.int32, (NZ, NC), 0) // 2
    repeats = (lax.broadcasted_iota(jnp.int32, (NZ, NC), 1) == layer_at).astype(F32)

    def paired(part):
        return [exact(pairs, block) for block in part]

    store_split(fine_ref, 768, paired(kept))
    store_split(fine_ref, 896, paired(lateral))

    coarse_sten = sten_ref[pl.ds(0, NC, stride=2), :]
    cblocks, ckept, clateral = level(coarse_sten, 0.25, cline_ref, NC)
    store_split(coarse_ref, 0, ckept)
    store_split(coarse_ref, 128, clateral)
    spread = [exact(repeats, block) for block in cblocks]
    diag = couple(sten, 0, spread)
    vert = couple(sten, 2, [above_below(block) for block in spread])
    store_split(coarse_ref, 256, spread)
    store_split(coarse_ref, 512, [d - v for d, v in zip(diag, vert)])
    store_split(coarse_ref, 768, couple(sten, 1, spread))


def unless(outside):
    return jnp.where(outside, 0.0, 1.0).astype(F32)


def product(halves, w_ref, at, width):
    high, low = halves
    wh = w_ref[0, :, at : at + width]
    wl = w_ref[1, :, at : at + width]

    def dot(a, b):
        return jnp.dot(a, b, preferred_element_type=F32)

    return dot(high, wh) + (dot(high, wl) + dot(low, wh))


def run_cycle(
    sides,
    spread,
    inside,
    fine_ref,
    coarse_ref,
    r_ref,
    keep_ref,
    sum_ref,
    rc_ref,
    ckeep_ref,
    csum_ref,
):
    def stage(i, src, lo, hi, w_ref, at, emit, size=6):
        ready = lo + 1
        for a in range(lo, hi, size):
            b = min(a + size, hi)
            halves = split(src[a:b].reshape((b - a) * XT, -1))
            if isinstance(at, tuple):
                for start, dst in zip(at, (keep_ref, sides[i])):
                    value = product(halves, w_ref, start, 192)
                    dst[a:b] = value.reshape(b - a, XT, 192)
            else:
                value = product(halves, w_ref, at, 224)
                for start, dst in ((0, ckeep_ref), (128, sides[i])):
                    dst[a:b] = value[:, start : start + 96].reshape(b - a, XT, 96)
            for y in range(ready, a - 1):
                emit(i, y)
            ready = max(ready, a - 1)
        for y in range(ready, hi - 1):
            emit(i, y)

    def next_fine(i, y):
        r_ref[y] = inside(keep_ref[y] + spread(i, y), y)

    def next_coarse(i, y):
        rc_ref[y] = inside(ckeep_ref[y] + spread(i, y), y)

    resid = []

    def last(i, y):
        resid.append(((r_ref[y] - keep_ref[y]) + spread(i, y))[MID])

    own = slice(HALO, HALO + YT)
    near = slice(HALO - 1, HALO + YT + 1)
    sum_ref[...] = r_ref[own, MID]
    for i, lo in ((0, 1), (1, 2)):
        stage(i, r_ref, lo, YW - lo, fine_ref, (256, 512), next_fine)
        sum_ref[...] += r_ref[own, MID]
    stage(2, r_ref, 3, YW - 3, fine_ref, 768, next_coarse)
    stage(3, r_ref, near.start, near.stop, fine_ref, (256, 512), next_fine, 5)
    csum_ref[near] = rc_ref[near]
    for i, lo in ((4, 4), (5, 5)):
        stage(i, rc_ref, lo, YW - lo, coarse_ref, 0, next_coarse)
        csum_ref[near] += rc_ref[near]
    stage(6, csum_ref, near.start, near.stop, coarse_ref, (512, 768), last, 5)
    change = product(split(sum_ref[...].reshape(YT * 16, 192)), fine_ref, 0, 192)
    change = change + product(
        split(csum_ref[own, MID].reshape(YT * 16, 96)), coarse_ref, 256, 192
    )
    return change.reshape(YT, 16, 192), jnp.stack(resid, axis=0)


def rows_inside(value, y):
    gy = lax.axis_index("gy")
    if y < HALO:
        value = value * unless(gy == 0)
    if y >= HALO + YT:
        value = value * unless(gy == lax.axis_size("gy") - 1)
    return value


def middle_kernel(resid_ref, fine_ref, coarse_ref, *refs):
    sides, change_ref, out_ref, scratch = refs[:7], refs[7], refs[8], refs[9:]
    r_ref = scratch[0]

    def spread(i, y):
        mid = sides[i][y]
        return (sides[i][y - 1] + sides[i][y + 1]) + (
            pltpu.roll(mid, 1, axis=0) + pltpu.roll(mid, XT - 1, axis=0)
        )

    for y in range(1, YW - 1):
        r_ref[y] = rows_inside(resid_ref[y - 1], y)
    change_ref[...], out_ref[...] = run_cycle(
        sides, spread, rows_inside, fine_ref, coarse_ref, *scratch
    )


def strips_kernel(resid_ref, edge_ref, x1_ref, x2_ref, fine_ref, coarse_ref, *refs):
    saved, change_ref, mid_ref, out_ref = refs[:7], refs[7], refs[8], refs[9]
    side_ref, cside_ref, scratch = refs[10], refs[11], refs[12:]
    r_ref = scratch[0]
    place, gx = x_slice(), lax.axis_index("gx")
    at_left = unless((gx == 0) & (place == 0))
    at_right = unless((gx == lax.axis_size("gx") - 1) & (place == lax.axis_size("gz") - 1))
    sides = [cside_ref if i in (2, 4, 5) else side_ref for i in range(7)]

    def inside(value, y):
        value = jnp.concatenate(
            [value[0:XH] * at_left, value[XH : 3 * XH], value[3 * XH :] * at_right], axis=0
        )
        return rows_inside(value, y)

    def spread(i, y):
        side = sides[i]
        mid = side[y]
        row = jnp.concatenate([mid[0:16], saved[i][y, MID], mid[16:32]], axis=0)
        row = pltpu.roll(row, 1, axis=0) + pltpu.roll(row, XW - 1, axis=0)
        return (side[y - 1] + side[y + 1]) + jnp.concatenate([row[0:16], row[XT:]], axis=0)

    even_x = place % 2 == 0
    sub = lax.broadcasted_iota(jnp.int32, (RW // 2, XH, 192), 1)
    left = unfolded(jnp.where(even_x, x2_ref[...], x1_ref[...]))
    right = unfolded(jnp.where(even_x, x1_ref[...], x2_ref[...]))
    for half in range(2):
        at = slice(half * (RW // 2), (half + 1) * (RW // 2))
        rows = slice(1 + at.start, 1 + at.stop)
        from_left, from_right = left[half], right[half]
        mine_left, mine_right = edge_ref[at, 0:1], edge_ref[at, 1:2]
        r_ref[rows, 0:XH] = jnp.where(sub >= 2, from_left, 0.0) + jnp.where(
            sub == 7, mine_left, 0.0
        )
        r_ref[rows, XH : 2 * XH] = resid_ref[at, 0:XH] + jnp.where(sub == 0, from_left[:, 0:1], 0.0)
        r_ref[rows, 2 * XH : 3 * XH] = resid_ref[at, XT - XH :] + jnp.where(
            sub == 7, from_right[:, 7:8], 0.0
        )
        r_ref[rows, 3 * XH :] = jnp.where(sub <= 5, from_right, 0.0) + jnp.where(
            sub == 0, mine_right, 0.0
        )
    for y in range(1, YW - 1):
        r_ref[y] = inside(r_ref[y], y)
    change, resid = run_cycle(sides, spread, inside, fine_ref, coarse_ref, *scratch)
    for f, (value, middle) in enumerate(((change, change_ref[...]), (resid, mid_ref[...]))):
        value = jnp.concatenate([value[:, 0:8], middle, value[:, 8:16]], axis=1)
        turned = jnp.transpose(value.reshape(YT * XT, 192))
        for c in range(3):
            for g in range(8):
                rows = turned[c * NZ + g * 8 : c * NZ + g * 8 + 8]
                for h in range(2):
                    at = h * 48 + f * 24 + c * 8
                    out_ref[g, at : at + 8, :] = rows[:, h * 128 : h * 128 + 128]


def cycle_scratch():
    fine, coarse = pltpu.VMEM((YW, XT, 192), F32), pltpu.VMEM((YW, XT, 96), F32)
    return [fine, fine, pltpu.VMEM((YT, 16, 192), F32), coarse, coarse, coarse]


def shape(*dims, dtype=F32):
    return jax.ShapeDtypeStruct(dims, dtype)


def swaps(line, start):
    pairs = [(line[i], line[i + 1]) for i in range(start, len(line) - 1, 2)]
    return pairs + [(b, a) for a, b in pairs]


def on_device(right_side, start_field, layer_material, stiffness, line_factors):
    size_y = lax.axis_size("gy")
    packed = pl.pallas_call(
        pack_kernel,
        out_shape=shape(8 * ROWS, 128),
        in_specs=[HBM, HBM, HBM],
        out_specs=VMEM,
        scratch_shapes=[
            pltpu.VMEM((6, 8, 8, 256), F32),
            pltpu.SMEM((8,), jnp.int32),
            pltpu.SemaphoreType.DMA((6,)),
            pltpu.SemaphoreType.DMA,
        ],
        compiler_params=params(60),
        name="pack",
    )(right_side, start_field, layer_material)
    got = lax.all_to_all(packed.reshape(8, ROWS, 128), "gz", 0, 0, tiled=True)
    mats = got[:, 96:, 0].reshape(-1).astype(jnp.int32)

    table = jnp.pad(stiffness.reshape(-1, 27), ((0, 128 - stiffness.shape[0]), (0, 128 - 27)))
    own, q, sten, send1, send2 = pl.pallas_call(
        turn_kernel,
        out_shape=(
            shape(YT, XT, 192),
            shape(YT, XT, 192),
            shape(NZ, 128),
            shape(4, XT, 384),
            shape(4, XT, 384),
        ),
        in_specs=[VMEM, VMEM],
        out_specs=(VMEM,) * 5,
        scratch_shapes=[pltpu.VMEM((8, XT, 384), F32), pltpu.VMEM((8, XT, 384), F32)],
        compiler_params=params(),
        name="turn",
    )(got, table)
    line, cline = pl.pallas_call(
        lines_kernel,
        out_shape=(shape(192, 192), shape(96, 96)),
        in_specs=[SMEM, SMEM],
        out_specs=(VMEM, VMEM),
        compiler_params=params(),
        name="lines",
    )(mats, line_factors.reshape(-1))
    count_x, count_y, count_z = (lax.axis_size(axis) for axis in ("gx", "gy", "gz"))
    y1 = lax.ppermute(send1, "gy", swaps(range(count_y), 0))
    y2 = lax.ppermute(send2, "gy", swaps(range(count_y), 1))
    resid, edge, send1, send2 = pl.pallas_call(
        sides_kernel,
        out_shape=(
            shape(RW, XT, 192),
            shape(RW, XH, 192),
            shape(RW // 2, XH, 384),
            shape(RW // 2, XH, 384),
        ),
        in_specs=[VMEM, VMEM, VMEM, VMEM, pl.BlockSpec(memory_space=pl.ANY)],
        out_specs=(VMEM,) * 4,
        scratch_shapes=[pltpu.VMEM((RW, XH, 384), F32)],
        compiler_params=params(),
        name="sides",
    )(own, q, y1, y2, line)
    along = [
        (count_z - 1 - i if x % 2 else i) * count_x + x
        for x in range(count_x)
        for i in range(count_z)
    ]
    x1 = lax.ppermute(send1, ("gz", "gx"), swaps(along, 0))
    x2 = lax.ppermute(send2, ("gz", "gx"), swaps(along, 1))

    fine, coarse = pl.pallas_call(
        setup_kernel,
        out_shape=(shape(2, 192, 1024, dtype=BF16), shape(2, 96, 1024, dtype=BF16)),
        in_specs=[VMEM, VMEM, VMEM, pl.BlockSpec(memory_space=pl.ANY)],
        out_specs=(VMEM, VMEM),
        compiler_params=params(),
        name="setup",
    )(line, cline, sten, edge)
    sides = tuple(shape(YW, XT, 96 if i in (2, 4, 5) else 192) for i in range(7))
    middle = pl.pallas_call(
        middle_kernel,
        out_shape=(*sides, shape(YT, 16, 192), shape(YT, 16, 192)),
        in_specs=[VMEM] * 3,
        out_specs=(VMEM,) * 9,
        scratch_shapes=cycle_scratch(),
        compiler_params=params(),
        name="middle",
    )(resid, fine, coarse)
    out = pl.pallas_call(
        strips_kernel,
        out_shape=shape(8, 96, 128),
        in_specs=[VMEM] * 15,
        out_specs=VMEM,
        scratch_shapes=[
            pltpu.VMEM((YW, XT, 192), F32),
            pltpu.VMEM((YW, XT, 96), F32),
            *cycle_scratch(),
        ],
        compiler_params=params(),
        name="strips",
    )(resid, edge, x1, x2, fine, coarse, *middle)
    back = lax.all_to_all(out, "gz", 0, 0, tiled=True)
    return pl.pallas_call(
        unpack_kernel,
        out_shape=(shape(8, 3, 8, 256), shape(8, 3, 8, 256)),
        in_specs=[VMEM, VMEM],
        out_specs=(HBM, HBM),
        scratch_shapes=[pltpu.VMEM((6, 8, 8, 256), F32), pltpu.SemaphoreType.DMA((6,))],
        compiler_params=params(),
        name="unpack",
    )(back.reshape(768, 128), start_field)


def solution(mesh):
    return jax.shard_map(
        on_device,
        mesh=mesh,
        in_specs=(P("gz", None, "gy", "gx"), P("gz", None, "gy", "gx"), P("gz"), P(), P()),
        out_specs=(P("gz", None, "gy", "gx"), P("gz", None, "gy", "gx")),
        check_vma=False,
    )
```

```python
import jax
import jax.numpy as jnp
from jax import lax
from jax.experimental import pallas as pl
from jax.experimental.pallas import tpu as pltpu
from jax.sharding import PartitionSpec as P

F32 = jnp.float32
BF16 = jnp.bfloat16
HALO = 7
XH = 8
XT = 32
XW = XT + 2 * XH
YT = 8
YW = YT + 2 * HALO
RH = HALO - 1
RW = YT + 2 * RH
MID = slice(8, 24)
ROWS = 104
NZ = 64
NC = NZ // 2
VMEM = pl.BlockSpec(memory_space=pltpu.VMEM)
HBM = pl.BlockSpec(memory_space=pltpu.HBM)
SMEM = pl.BlockSpec(memory_space=pltpu.SMEM)


def params(mib=40):
    return pltpu.CompilerParams(vmem_limit_bytes=mib * 1024 * 1024)


def swap_blocks(tile, form=0):
    sub = lax.broadcasted_iota(jnp.int32, tile.shape, 1)
    blk = lax.broadcasted_iota(jnp.int32, tile.shape, 2) // 32
    for bit in (1, 2, 4):
        in_sub = (sub & bit) != 0
        in_blk = (blk & bit) != 0
        sub_up, sub_down = pltpu.roll(tile, 8 - bit, axis=1), pltpu.roll(tile, bit, axis=1)
        if form == 0:
            up = pltpu.roll(sub_up, 32 * bit, axis=2)
            down = pltpu.roll(sub_down, 256 - 32 * bit, axis=2)
            tile = jnp.where(in_sub == in_blk, tile, jnp.where(in_blk, up, down))
        else:
            by_sub = jnp.where(in_sub, sub_down, sub_up)
            blk_up = pltpu.roll(tile, 256 - 32 * bit, axis=2)
            blk_down = pltpu.roll(tile, 32 * bit, axis=2)
            by_blk = jnp.where(in_blk, blk_down, blk_up)
            same = in_sub == in_blk
            tile = jnp.where(same, by_blk, by_sub) if form == 1 else jnp.where(same, by_sub, by_blk)
    return tile


def odd_block():
    return lax.axis_index("gx") % 2 == 1


def x_slice():
    gz = lax.axis_index("gz")
    return jnp.where(odd_block(), lax.axis_size("gz") - 1 - gz, gz)


def fetches(pairs, sems):
    copies = [pltpu.make_async_copy(src, dst, sems.at[i]) for i, (src, dst) in enumerate(pairs)]
    for copy in copies:
        copy.start()
    return copies


def pack_kernel(load_hbm, start_hbm, mats_hbm, out_ref, in_ref, mats_ref, sems, mats_sem):
    mats_copy = pltpu.make_async_copy(mats_hbm, mats_ref, mats_sem)
    mats_copy.start()
    order = [(f, c) for f in range(2) for c in range(3)]
    copies = fetches(
        [((load_hbm, start_hbm)[f].at[:, c], in_ref.at[i]) for i, (f, c) in enumerate(order)], sems
    )
    for i, (f, c) in enumerate(order):
        copies[i].wait()
        for form in (0, 1):

            @pl.when(odd_block() == (form == 1))
            def _():
                tile = swap_blocks(in_ref[i], form)
                for z in range(8):
                    for h in range(2):
                        at = h * 48 + f * 24 + c * 8 + z
                        out_ref[pl.ds(at, 8, stride=ROWS), :] = tile[z, :, h * 128 : h * 128 + 128]

    mats_copy.wait()
    row = lax.broadcasted_iota(jnp.int32, (8, 128), 0)
    ids = jnp.zeros((8, 128), jnp.int32)
    for z in range(8):
        ids = jnp.where(row == z, mats_ref[z], ids)
    for k in range(8):
        out_ref[k * ROWS + 96 : k * ROWS + 104, :] = ids.astype(F32)


def unpack_kernel(got_ref, start_ref, field_hbm, resid_hbm, out_ref, sems):
    order = [(f, c) for f in range(2) for c in range(3)]
    copies = [
        pltpu.make_async_copy(
            out_ref.at[i], (field_hbm, resid_hbm)[f].at[:, c], sems.at[i]
        )
        for i, (f, c) in enumerate(order)
    ]

    def fill(form):
        for i, (f, c) in enumerate(order):
            halves = []
            for h in range(2):
                at = h * 48 + f * 24 + c * 8
                rows = [got_ref[pl.ds(at + z, 8, stride=96), :] for z in range(8)]
                halves.append(jnp.stack(rows, axis=0))
            tile = swap_blocks(jnp.concatenate(halves, axis=2), form)
            if f == 0:
                tile = tile + start_ref[:, c]
            out_ref[i] = tile
            copies[i].start()

    for form in (0, 2):

        @pl.when(odd_block() == (form == 2))
        def _():
            fill(form)

    for copy in copies:
        copy.wait()


def exact(a, b):
    return jnp.dot(a, b, precision=lax.Precision.HIGHEST, preferred_element_type=F32)


def folded(value):
    half = value.shape[0] // 2
    lane = lax.broadcasted_iota(jnp.int32, (half, *value.shape[1:]), 2)
    return jnp.where(lane < 192, value[:half], pltpu.roll(value[half:], 192, axis=2))


def unfolded(value):
    return value[:, :, 0:192], pltpu.roll(value, 192, axis=2)[:, :, 0:192]


def turn_kernel(
    got_ref, table_ref, own_ref, q_ref, sten_ref, first_ref, second_ref, down_ref, up_ref
):
    groups = range(8)
    ids = jnp.concatenate([got_ref[g, 96:104] for g in groups], axis=0)
    lane = lax.broadcasted_iota(jnp.int32, ids.shape, 1)
    sten = exact((ids == lane.astype(F32)).astype(F32), table_ref[...])
    sten_ref[...] = sten

    def field(f, c):
        at = f * 24 + c * 8
        return jnp.concatenate(
            [
                jnp.concatenate(
                    [got_ref[g, h * 48 + at : h * 48 + at + 8] for g in groups], axis=0
                )
                for h in range(2)
            ],
            axis=1,
        )

    start = [field(1, c) for c in range(3)]
    q = couple(sten, 1, start)
    diag = couple(sten, 0, start)
    vert = couple(sten, 2, [above_below(part) for part in start])
    lane = lax.broadcasted_iota(jnp.int32, (NZ, 256), 1)
    x, y = lane % XT, lane // XT
    resid = []
    for c in range(3):
        near = jnp.where(x > 0, pltpu.roll(q[c], 1, axis=1), 0.0)
        near = near + jnp.where(x < XT - 1, pltpu.roll(q[c], 255, axis=1), 0.0)
        near = near + jnp.where(y > 0, pltpu.roll(q[c], XT, axis=1), 0.0)
        near = near + jnp.where(y < YT - 1, pltpu.roll(q[c], 256 - XT, axis=1), 0.0)
        resid.append((field(0, c) - (diag[c] - vert[c])) + near)
    own_ref[...] = jnp.transpose(jnp.concatenate(resid, axis=0)).reshape(YT, XT, 192)
    q_ref[...] = jnp.transpose(jnp.concatenate(q, axis=0)).reshape(YT, XT, 192)
    for ref, top, edge in ((down_ref, YT - RH, YT - 1), (up_ref, 0, 0)):
        ref[0:RH, :, 0:192] = own_ref[top : top + RH]
        ref[RH, :, 0:192] = q_ref[edge]
        ref[RH + 1, :, 0:192] = jnp.zeros((XT, 192), F32)
        for r in range(RH):
            ref[RH + 1, r : r + 1, 0:192] = q_ref[top + r, 0:1]
            ref[RH + 1, 8 + r : 9 + r, 0:192] = q_ref[top + r, XT - 1 : XT]
    down, up = folded(down_ref[...]), folded(up_ref[...])
    even = lax.axis_index("gy") % 2 == 0
    first_ref[...] = jnp.where(even, down, up)
    second_ref[...] = jnp.where(even, up, down)


def sides_kernel(
    own_ref, q_ref, y1_ref, y2_ref, after_ref, resid_ref, edge_ref, send1_ref, send2_ref, wide_ref
):
    even_x = x_slice() % 2 == 0
    even_y = lax.axis_index("gy") % 2 == 0
    first, second = y1_ref[...], y2_ref[...]
    sub = lax.broadcasted_iota(jnp.int32, (RW, XH, 192), 1)
    edge_ref[...] = jnp.zeros((RW, XH, 192), F32)
    resid_ref[RH : RH + YT] = own_ref[...]
    for y in range(YT):
        edge_ref[RH + y, 0:1] = q_ref[y, 0:1]
        edge_ref[RH + y, 1:2] = q_ref[y, XT - 1 : XT]
    for at, value, border, inside, mine in (
        (0, jnp.where(even_y, second, first), RH - 1, RH, 0),
        (RH + YT, jnp.where(even_y, first, second), RH + YT, RH + YT - 1, YT - 1),
    ):
        low, high = unfolded(value)
        resid_ref[at : at + 4] = low
        resid_ref[at + 4 : at + RH] = high[0:2]
        resid_ref[border] = resid_ref[border] + q_ref[mine]
        resid_ref[inside] = resid_ref[inside] + high[2]
        for r in range(RH):
            edge_ref[at + r, 0:1] = high[3, r : r + 1]
            edge_ref[at + r, 1:2] = high[3, 8 + r : 9 + r]
    wide_ref[:, :, 0:192] = jnp.where(sub == 7, edge_ref[:, 0:1], resid_ref[:, 0:XH])
    left = folded(wide_ref[...])
    wide_ref[:, :, 0:192] = jnp.where(sub == 0, edge_ref[:, 1:2], resid_ref[:, XT - XH :])
    right = folded(wide_ref[...])
    send1_ref[...] = jnp.where(even_x, right, left)
    send2_ref[...] = jnp.where(even_x, left, right)


def split(value):
    high = value.astype(BF16)
    return high, (value - high.astype(F32)).astype(BF16)


def up_row(mats_ref, factor_ref, dst_ref, layers, step, z, state):
    lane = lax.broadcasted_iota(jnp.int32, (1, 3 * layers), 1)
    base = mats_ref[z * step] * 27
    new = []
    for i in range(3):
        row = jnp.zeros((1, 3 * layers), F32)
        for j in range(3):
            row = jnp.where(lane == j * layers + z, factor_ref[base + i * 3 + j], row)
        for j in range(3):
            row = row + factor_ref[base + 9 + i * 3 + j] * state[j]
        dst_ref[pl.ds(i * layers + z, 1), :] = row
        new.append(row)
    return new


def down_row(mats_ref, factor_ref, dst_ref, layers, step, z, state):
    lane = lax.broadcasted_iota(jnp.int32, (1, 3 * layers), 1)
    base = mats_ref[z * step] * 27
    new = []
    for i in range(3):
        row = jnp.where(lane == i * layers + z, 1.0, 0.0)
        for j in range(3):
            row = row + factor_ref[base + 18 + i * 3 + j] * state[j]
        dst_ref[pl.ds(i * layers + z, 1), :] = row
        new.append(row)
    return new


def couple(sten, which, blocks):
    out = []
    for i in range(3):
        total = None
        for j in range(3):
            at = which * 9 + i * 3 + j
            term = sten[:, at : at + 1] * blocks[j]
            total = term if total is None else total + term
        out.append(total)
    return out


def above_below(block):
    row = lax.broadcasted_iota(jnp.int32, block.shape, 0)
    n = block.shape[0]
    low = jnp.where(row == 0, 0.0, pltpu.roll(block, 1, axis=0))
    high = jnp.where(row == n - 1, 0.0, pltpu.roll(block, n - 1, axis=0))
    return low + high


def store_split(ref, at, rows):
    value = jnp.transpose(jnp.concatenate(rows, axis=0))
    high, low = split(value)
    ref[0, :, at : at + value.shape[1]] = high
    ref[1, :, at : at + value.shape[1]] = low


def lines_kernel(mats_ref, factor_ref, up_ref, down_ref, cup_ref, cdown_ref):
    def step(t, state):
        up, down, cup, cdown = (state[i * 3 : i * 3 + 3] for i in range(4))
        for half in range(2):
            z = 2 * t + half
            up = up_row(mats_ref, factor_ref, up_ref, NZ, 1, z, up)
            down = down_row(mats_ref, factor_ref, down_ref, NZ, 1, NZ - 1 - z, down)
        cup = up_row(mats_ref, factor_ref, cup_ref, NC, 2, t, cup)
        cdown = down_row(mats_ref, factor_ref, cdown_ref, NC, 2, NC - 1 - t, cdown)
        return (*up, *down, *cup, *cdown)

    fine, coarse = (jnp.zeros((1, 3 * n), F32) for n in (NZ, NC))
    lax.fori_loop(0, NC, step, (fine,) * 6 + (coarse,) * 6, unroll=4)


def setup_kernel(
    up_ref, down_ref, cup_ref, cdown_ref, sten_ref, fine_ref, coarse_ref, line_ref, cline_ref
):
    sten = sten_ref[...]
    line_ref[...] = exact(down_ref[...], up_ref[...])
    cline_ref[...] = exact(cdown_ref[...], cup_ref[...])

    def level(sten_part, scale, ref, layers):
        blocks = [ref[i * layers : (i + 1) * layers, :] for i in range(3)]
        lateral = couple(sten_part, 1, blocks)
        diag = couple(sten_part, 0, blocks)
        vert = couple(sten_part, 2, [above_below(block) for block in blocks])
        if scale is not None:
            vert = [scale * part for part in vert]
        wide = blocks[0].shape
        r = lax.broadcasted_iota(jnp.int32, wide, 0)
        q = lax.broadcasted_iota(jnp.int32, wide, 1)
        kept = [
            jnp.where(q == r + i * layers, 1.0, 0.0) - (diag[i] - vert[i]) for i in range(3)
        ]
        return blocks, kept, lateral

    blocks, kept, lateral = level(sten, None, line_ref, NZ)
    store_split(fine_ref, 0, blocks)
    store_split(fine_ref, 256, kept)
    store_split(fine_ref, 512, lateral)

    layer_at = lax.broadcasted_iota(jnp.int32, (NC, NZ), 1) // 2
    pairs = (lax.broadcasted_iota(jnp.int32, (NC, NZ), 0) == layer_at).astype(F32)
    layer_at = lax.broadcasted_iota(jnp.int32, (NZ, NC), 0) // 2
    repeats = (lax.broadcasted_iota(jnp.int32, (NZ, NC), 1) == layer_at).astype(F32)

    def paired(part):
        return [exact(pairs, block) for block in part]

    store_split(fine_ref, 768, paired(kept))
    store_split(fine_ref, 896, paired(lateral))

    coarse_sten = sten_ref[pl.ds(0, NC, stride=2), :]
    cblocks, ckept, clateral = level(coarse_sten, 0.25, cline_ref, NC)
    store_split(coarse_ref, 0, ckept)
    store_split(coarse_ref, 128, clateral)
    spread = [exact(repeats, block) for block in cblocks]
    diag = couple(sten, 0, spread)
    vert = couple(sten, 2, [above_below(block) for block in spread])
    store_split(coarse_ref, 256, spread)
    store_split(coarse_ref, 512, [d - v for d, v in zip(diag, vert)])
    store_split(coarse_ref, 768, couple(sten, 1, spread))


def unless(outside):
    return jnp.where(outside, 0.0, 1.0).astype(F32)


def product(halves, w_ref, at, width):
    high, low = halves
    wh = w_ref[0, :, at : at + width]
    wl = w_ref[1, :, at : at + width]

    def dot(a, b):
        return jnp.dot(a, b, preferred_element_type=F32)

    return dot(high, wh) + (dot(high, wl) + dot(low, wh))


def run_cycle(
    sides,
    spread,
    inside,
    fine_ref,
    coarse_ref,
    r_ref,
    keep_ref,
    sum_ref,
    rc_ref,
    ckeep_ref,
    csum_ref,
):
    def stage(i, src, lo, hi, w_ref, at, emit, size=6):
        ready = lo + 1
        for a in range(lo, hi, size):
            b = min(a + size, hi)
            halves = split(src[a:b].reshape((b - a) * XT, -1))
            if isinstance(at, tuple):
                for start, dst in zip(at, (keep_ref, sides[i])):
                    value = product(halves, w_ref, start, 192)
                    dst[a:b] = value.reshape(b - a, XT, 192)
            else:
                value = product(halves, w_ref, at, 224)
                for start, dst in ((0, ckeep_ref), (128, sides[i])):
                    dst[a:b] = value[:, start : start + 96].reshape(b - a, XT, 96)
            for y in range(ready, a - 1):
                emit(i, y)
            ready = max(ready, a - 1)
        for y in range(ready, hi - 1):
            emit(i, y)

    def next_fine(i, y):
        r_ref[y] = inside(keep_ref[y] + spread(i, y), y)

    def next_coarse(i, y):
        rc_ref[y] = inside(ckeep_ref[y] + spread(i, y), y)

    resid = []

    def last(i, y):
        resid.append(((r_ref[y] - keep_ref[y]) + spread(i, y))[MID])

    own = slice(HALO, HALO + YT)
    near = slice(HALO - 1, HALO + YT + 1)
    sum_ref[...] = r_ref[own, MID]
    for i, lo in ((0, 1), (1, 2)):
        stage(i, r_ref, lo, YW - lo, fine_ref, (256, 512), next_fine)
        sum_ref[...] += r_ref[own, MID]
    stage(2, r_ref, 3, YW - 3, fine_ref, 768, next_coarse)
    stage(3, r_ref, near.start, near.stop, fine_ref, (256, 512), next_fine, 5)
    csum_ref[near] = rc_ref[near]
    for i, lo in ((4, 4), (5, 5)):
        stage(i, rc_ref, lo, YW - lo, coarse_ref, 0, next_coarse)
        csum_ref[near] += rc_ref[near]
    stage(6, csum_ref, near.start, near.stop, coarse_ref, (512, 768), last, 5)
    change = product(split(sum_ref[...].reshape(YT * 16, 192)), fine_ref, 0, 192)
    change = change + product(
        split(csum_ref[own, MID].reshape(YT * 16, 96)), coarse_ref, 256, 192
    )
    return change.reshape(YT, 16, 192), jnp.stack(resid, axis=0)


def rows_inside(value, y):
    gy = lax.axis_index("gy")
    if y < HALO:
        value = value * unless(gy == 0)
    if y >= HALO + YT:
        value = value * unless(gy == lax.axis_size("gy") - 1)
    return value


def middle_kernel(resid_ref, fine_ref, coarse_ref, *refs):
    sides, change_ref, out_ref, scratch = refs[:7], refs[7], refs[8], refs[9:]
    r_ref = scratch[0]

    def spread(i, y):
        mid = sides[i][y]
        return (sides[i][y - 1] + sides[i][y + 1]) + (
            pltpu.roll(mid, 1, axis=0) + pltpu.roll(mid, XT - 1, axis=0)
        )

    for y in range(1, YW - 1):
        r_ref[y] = rows_inside(resid_ref[y - 1], y)
    change_ref[...], out_ref[...] = run_cycle(
        sides, spread, rows_inside, fine_ref, coarse_ref, *scratch
    )


def strips_kernel(resid_ref, edge_ref, x1_ref, x2_ref, fine_ref, coarse_ref, *refs):
    saved, change_ref, mid_ref, out_ref = refs[:7], refs[7], refs[8], refs[9]
    side_ref, cside_ref, scratch = refs[10], refs[11], refs[12:]
    r_ref = scratch[0]
    place, gx = x_slice(), lax.axis_index("gx")
    at_left = unless((gx == 0) & (place == 0))
    at_right = unless((gx == lax.axis_size("gx") - 1) & (place == lax.axis_size("gz") - 1))
    sides = [cside_ref if i in (2, 4, 5) else side_ref for i in range(7)]

    def inside(value, y):
        value = jnp.concatenate(
            [value[0:XH] * at_left, value[XH : 3 * XH], value[3 * XH :] * at_right], axis=0
        )
        return rows_inside(value, y)

    def spread(i, y):
        side = sides[i]
        mid = side[y]
        row = jnp.concatenate([mid[0:16], saved[i][y, MID], mid[16:32]], axis=0)
        row = pltpu.roll(row, 1, axis=0) + pltpu.roll(row, XW - 1, axis=0)
        return (side[y - 1] + side[y + 1]) + jnp.concatenate([row[0:16], row[XT:]], axis=0)

    even_x = place % 2 == 0
    sub = lax.broadcasted_iota(jnp.int32, (RW // 2, XH, 192), 1)
    left = unfolded(jnp.where(even_x, x2_ref[...], x1_ref[...]))
    right = unfolded(jnp.where(even_x, x1_ref[...], x2_ref[...]))
    for half in range(2):
        at = slice(half * (RW // 2), (half + 1) * (RW // 2))
        rows = slice(1 + at.start, 1 + at.stop)
        from_left, from_right = left[half], right[half]
        mine_left, mine_right = edge_ref[at, 0:1], edge_ref[at, 1:2]
        r_ref[rows, 0:XH] = jnp.where(sub >= 2, from_left, 0.0) + jnp.where(
            sub == 7, mine_left, 0.0
        )
        r_ref[rows, XH : 2 * XH] = resid_ref[at, 0:XH] + jnp.where(sub == 0, from_left[:, 0:1], 0.0)
        r_ref[rows, 2 * XH : 3 * XH] = resid_ref[at, XT - XH :] + jnp.where(
            sub == 7, from_right[:, 7:8], 0.0
        )
        r_ref[rows, 3 * XH :] = jnp.where(sub <= 5, from_right, 0.0) + jnp.where(
            sub == 0, mine_right, 0.0
        )
    for y in range(1, YW - 1):
        r_ref[y] = inside(r_ref[y], y)
    change, resid = run_cycle(sides, spread, inside, fine_ref, coarse_ref, *scratch)
    for f, (value, middle) in enumerate(((change, change_ref[...]), (resid, mid_ref[...]))):
        value = jnp.concatenate([value[:, 0:8], middle, value[:, 8:16]], axis=1)
        turned = jnp.transpose(value.reshape(YT * XT, 192))
        for c in range(3):
            for g in range(8):
                rows = turned[c * NZ + g * 8 : c * NZ + g * 8 + 8]
                for h in range(2):
                    at = h * 48 + f * 24 + c * 8
                    out_ref[g, at : at + 8, :] = rows[:, h * 128 : h * 128 + 128]


def cycle_scratch():
    fine, coarse = pltpu.VMEM((YW, XT, 192), F32), pltpu.VMEM((YW, XT, 96), F32)
    return [fine, fine, pltpu.VMEM((YT, 16, 192), F32), coarse, coarse, coarse]


def shape(*dims, dtype=F32):
    return jax.ShapeDtypeStruct(dims, dtype)


def swaps(line, start):
    pairs = [(line[i], line[i + 1]) for i in range(start, len(line) - 1, 2)]
    return pairs + [(b, a) for a, b in pairs]


def on_device(right_side, start_field, layer_material, stiffness, line_factors):
    size_y = lax.axis_size("gy")
    packed = pl.pallas_call(
        pack_kernel,
        out_shape=shape(8 * ROWS, 128),
        in_specs=[HBM, HBM, HBM],
        out_specs=VMEM,
        scratch_shapes=[
            pltpu.VMEM((6, 8, 8, 256), F32),
            pltpu.SMEM((8,), jnp.int32),
            pltpu.SemaphoreType.DMA((6,)),
            pltpu.SemaphoreType.DMA,
        ],
        compiler_params=params(60),
        name="pack",
    )(right_side, start_field, layer_material)
    got = lax.all_to_all(packed.reshape(8, ROWS, 128), "gz", 0, 0, tiled=True)
    mats = got[:, 96:, 0].reshape(-1).astype(jnp.int32)

    table = jnp.pad(stiffness.reshape(-1, 27), ((0, 128 - stiffness.shape[0]), (0, 128 - 27)))
    own, q, sten, send1, send2 = pl.pallas_call(
        turn_kernel,
        out_shape=(
            shape(YT, XT, 192),
            shape(YT, XT, 192),
            shape(NZ, 128),
            shape(4, XT, 384),
            shape(4, XT, 384),
        ),
        in_specs=[VMEM, VMEM],
        out_specs=(VMEM,) * 5,
        scratch_shapes=[pltpu.VMEM((8, XT, 384), F32), pltpu.VMEM((8, XT, 384), F32)],
        compiler_params=params(),
        name="turn",
    )(got, table)
    lines = pl.pallas_call(
        lines_kernel,
        out_shape=(shape(192, 192), shape(192, 192), shape(96, 96), shape(96, 96)),
        in_specs=[SMEM, SMEM],
        out_specs=(VMEM,) * 4,
        compiler_params=params(),
        name="lines",
    )(mats, line_factors.reshape(-1))
    fine, coarse = pl.pallas_call(
        setup_kernel,
        out_shape=(shape(2, 192, 1024, dtype=BF16), shape(2, 96, 1024, dtype=BF16)),
        in_specs=[VMEM] * 5,
        out_specs=(VMEM, VMEM),
        scratch_shapes=[pltpu.VMEM((192, 192), F32), pltpu.VMEM((96, 96), F32)],
        compiler_params=params(),
        name="setup",
    )(*lines, sten)
    count_x, count_y, count_z = (lax.axis_size(axis) for axis in ("gx", "gy", "gz"))
    y1 = lax.ppermute(send1, "gy", swaps(range(count_y), 0))
    y2 = lax.ppermute(send2, "gy", swaps(range(count_y), 1))
    resid, edge, send1, send2 = pl.pallas_call(
        sides_kernel,
        out_shape=(
            shape(RW, XT, 192),
            shape(RW, XH, 192),
            shape(RW // 2, XH, 384),
            shape(RW // 2, XH, 384),
        ),
        in_specs=[VMEM, VMEM, VMEM, VMEM, pl.BlockSpec(memory_space=pl.ANY)],
        out_specs=(VMEM,) * 4,
        scratch_shapes=[pltpu.VMEM((RW, XH, 384), F32)],
        compiler_params=params(),
        name="sides",
    )(own, q, y1, y2, fine)
    along = [
        (count_z - 1 - i if x % 2 else i) * count_x + x
        for x in range(count_x)
        for i in range(count_z)
    ]
    x1 = lax.ppermute(send1, ("gz", "gx"), swaps(along, 0))
    x2 = lax.ppermute(send2, ("gz", "gx"), swaps(along, 1))

    sides = tuple(shape(YW, XT, 96 if i in (2, 4, 5) else 192) for i in range(7))
    middle = pl.pallas_call(
        middle_kernel,
        out_shape=(*sides, shape(YT, 16, 192), shape(YT, 16, 192)),
        in_specs=[VMEM] * 3,
        out_specs=(VMEM,) * 9,
        scratch_shapes=cycle_scratch(),
        compiler_params=params(),
        name="middle",
    )(resid, fine, coarse)
    out = pl.pallas_call(
        strips_kernel,
        out_shape=shape(8, 96, 128),
        in_specs=[VMEM] * 15,
        out_specs=VMEM,
        scratch_shapes=[
            pltpu.VMEM((YW, XT, 192), F32),
            pltpu.VMEM((YW, XT, 96), F32),
            *cycle_scratch(),
        ],
        compiler_params=params(),
        name="strips",
    )(resid, edge, x1, x2, fine, coarse, *middle)
    back = lax.all_to_all(out, "gz", 0, 0, tiled=True)
    return pl.pallas_call(
        unpack_kernel,
        out_shape=(shape(8, 3, 8, 256), shape(8, 3, 8, 256)),
        in_specs=[VMEM, VMEM],
        out_specs=(HBM, HBM),
        scratch_shapes=[pltpu.VMEM((6, 8, 8, 256), F32), pltpu.SemaphoreType.DMA((6,))],
        compiler_params=params(),
        name="unpack",
    )(back.reshape(768, 128), start_field)


def solution(mesh):
    return jax.shard_map(
        on_device,
        mesh=mesh,
        in_specs=(P("gz", None, "gy", "gx"), P("gz", None, "gy", "gx"), P("gz"), P(), P()),
        out_specs=(P("gz", None, "gy", "gx"), P("gz", None, "gy", "gx")),
        check_vma=False,
    )
```

```python
import jax
import jax.numpy as jnp
from jax import lax
from jax.experimental import pallas as pl
from jax.experimental.pallas import tpu as pltpu
from jax.sharding import PartitionSpec as P

F32 = jnp.float32
BF16 = jnp.bfloat16
HALO = 7
XH = 8
XT = 32
XW = XT + 2 * XH
YT = 8
YW = YT + 2 * HALO
RH = HALO - 1
RW = YT + 2 * RH
MID = slice(8, 24)
ROWS = 104
NZ = 64
NC = NZ // 2
VMEM = pl.BlockSpec(memory_space=pltpu.VMEM)
HBM = pl.BlockSpec(memory_space=pltpu.HBM)
SMEM = pl.BlockSpec(memory_space=pltpu.SMEM)


def params(mib=40):
    return pltpu.CompilerParams(vmem_limit_bytes=mib * 1024 * 1024)


def swap_blocks(tile, form=0):
    sub = lax.broadcasted_iota(jnp.int32, tile.shape, 1)
    blk = lax.broadcasted_iota(jnp.int32, tile.shape, 2) // 32
    for bit in (1, 2, 4):
        in_sub = (sub & bit) != 0
        in_blk = (blk & bit) != 0
        sub_up, sub_down = pltpu.roll(tile, 8 - bit, axis=1), pltpu.roll(tile, bit, axis=1)
        if form == 0:
            up = pltpu.roll(sub_up, 32 * bit, axis=2)
            down = pltpu.roll(sub_down, 256 - 32 * bit, axis=2)
            tile = jnp.where(in_sub == in_blk, tile, jnp.where(in_blk, up, down))
        else:
            by_sub = jnp.where(in_sub, sub_down, sub_up)
            blk_up = pltpu.roll(tile, 256 - 32 * bit, axis=2)
            blk_down = pltpu.roll(tile, 32 * bit, axis=2)
            by_blk = jnp.where(in_blk, blk_down, blk_up)
            same = in_sub == in_blk
            tile = jnp.where(same, by_blk, by_sub) if form == 1 else jnp.where(same, by_sub, by_blk)
    return tile


def odd_block():
    return lax.axis_index("gx") % 2 == 1


def x_slice():
    gz = lax.axis_index("gz")
    return jnp.where(odd_block(), lax.axis_size("gz") - 1 - gz, gz)


def fetches(pairs, sems):
    copies = [pltpu.make_async_copy(src, dst, sems.at[i]) for i, (src, dst) in enumerate(pairs)]
    for copy in copies:
        copy.start()
    return copies


def pack_kernel(load_hbm, start_hbm, mats_hbm, out_ref, in_ref, mats_ref, sems, mats_sem):
    mats_copy = pltpu.make_async_copy(mats_hbm, mats_ref, mats_sem)
    mats_copy.start()
    order = [(f, c) for f in range(2) for c in range(3)]
    copies = fetches(
        [((load_hbm, start_hbm)[f].at[:, c], in_ref.at[i]) for i, (f, c) in enumerate(order)], sems
    )
    for i, (f, c) in enumerate(order):
        copies[i].wait()
        for form in (0, 1):

            @pl.when(odd_block() == (form == 1))
            def _():
                tile = swap_blocks(in_ref[i], form)
                for z in range(8):
                    for h in range(2):
                        at = h * 48 + f * 24 + c * 8 + z
                        out_ref[pl.ds(at, 8, stride=ROWS), :] = tile[z, :, h * 128 : h * 128 + 128]

    mats_copy.wait()
    row = lax.broadcasted_iota(jnp.int32, (8, 128), 0)
    ids = jnp.zeros((8, 128), jnp.int32)
    for z in range(8):
        ids = jnp.where(row == z, mats_ref[z], ids)
    for k in range(8):
        out_ref[k * ROWS + 96 : k * ROWS + 104, :] = ids.astype(F32)


def unpack_kernel(got_ref, start_ref, field_hbm, resid_hbm, out_ref, sems):
    order = [(f, c) for f in range(2) for c in range(3)]
    copies = [
        pltpu.make_async_copy(out_ref.at[f], ref, sems.at[f])
        for f, ref in enumerate((field_hbm, resid_hbm))
    ]

    def fill(form):
        for f, c in order:
            halves = []
            for h in range(2):
                at = h * 48 + f * 24 + c * 8
                rows = [got_ref[pl.ds(at + z, 8, stride=96), :] for z in range(8)]
                halves.append(jnp.stack(rows, axis=0))
            tile = swap_blocks(jnp.concatenate(halves, axis=2), form)
            if f == 0:
                tile = tile + start_ref[:, c]
            out_ref[f, :, c] = tile
            if c == 2:
                copies[f].start()

    for form in (0, 2):

        @pl.when(odd_block() == (form == 2))
        def _():
            fill(form)

    for copy in copies:
        copy.wait()


def exact(a, b):
    return jnp.dot(a, b, precision=lax.Precision.HIGHEST, preferred_element_type=F32)


def folded(value):
    half = value.shape[0] // 2
    lane = lax.broadcasted_iota(jnp.int32, (half, *value.shape[1:]), 2)
    return jnp.where(lane < 192, value[:half], pltpu.roll(value[half:], 192, axis=2))


def unfolded(value):
    return value[:, :, 0:192], pltpu.roll(value, 192, axis=2)[:, :, 0:192]


def turn_kernel(
    got_ref, table_ref, own_ref, q_ref, sten_ref, first_ref, second_ref, down_ref, up_ref
):
    groups = range(8)
    ids = jnp.concatenate([got_ref[g, 96:104] for g in groups], axis=0)
    lane = lax.broadcasted_iota(jnp.int32, ids.shape, 1)
    sten = exact((ids == lane.astype(F32)).astype(F32), table_ref[...])
    sten_ref[...] = sten

    def field(f, c):
        at = f * 24 + c * 8
        return jnp.concatenate(
            [
                jnp.concatenate(
                    [got_ref[g, h * 48 + at : h * 48 + at + 8] for g in groups], axis=0
                )
                for h in range(2)
            ],
            axis=1,
        )

    start = [field(1, c) for c in range(3)]
    q = couple(sten, 1, start)
    diag = couple(sten, 0, start)
    vert = couple(sten, 2, [above_below(part) for part in start])
    lane = lax.broadcasted_iota(jnp.int32, (NZ, 256), 1)
    x, y = lane % XT, lane // XT
    resid = []
    for c in range(3):
        near = jnp.where(x > 0, pltpu.roll(q[c], 1, axis=1), 0.0)
        near = near + jnp.where(x < XT - 1, pltpu.roll(q[c], 255, axis=1), 0.0)
        near = near + jnp.where(y > 0, pltpu.roll(q[c], XT, axis=1), 0.0)
        near = near + jnp.where(y < YT - 1, pltpu.roll(q[c], 256 - XT, axis=1), 0.0)
        resid.append((field(0, c) - (diag[c] - vert[c])) + near)
    own_ref[...] = jnp.transpose(jnp.concatenate(resid, axis=0)).reshape(YT, XT, 192)
    q_ref[...] = jnp.transpose(jnp.concatenate(q, axis=0)).reshape(YT, XT, 192)
    for ref, top, edge in ((down_ref, YT - RH, YT - 1), (up_ref, 0, 0)):
        ref[0:RH, :, 0:192] = own_ref[top : top + RH]
        ref[RH, :, 0:192] = q_ref[edge]
        ref[RH + 1, :, 0:192] = jnp.zeros((XT, 192), F32)
        for r in range(RH):
            ref[RH + 1, r : r + 1, 0:192] = q_ref[top + r, 0:1]
            ref[RH + 1, 8 + r : 9 + r, 0:192] = q_ref[top + r, XT - 1 : XT]
    down, up = folded(down_ref[...]), folded(up_ref[...])
    even = lax.axis_index("gy") % 2 == 0
    first_ref[...] = jnp.where(even, down, up)
    second_ref[...] = jnp.where(even, up, down)


def sides_kernel(
    own_ref, q_ref, y1_ref, y2_ref, after_ref, resid_ref, edge_ref, send1_ref, send2_ref, wide_ref
):
    even_x = x_slice() % 2 == 0
    even_y = lax.axis_index("gy") % 2 == 0
    first, second = y1_ref[...], y2_ref[...]
    sub = lax.broadcasted_iota(jnp.int32, (RW, XH, 192), 1)
    edge_ref[...] = jnp.zeros((RW, XH, 192), F32)
    resid_ref[RH : RH + YT] = own_ref[...]
    for y in range(YT):
        edge_ref[RH + y, 0:1] = q_ref[y, 0:1]
        edge_ref[RH + y, 1:2] = q_ref[y, XT - 1 : XT]
    for at, value, border, inside, mine in (
        (0, jnp.where(even_y, second, first), RH - 1, RH, 0),
        (RH + YT, jnp.where(even_y, first, second), RH + YT, RH + YT - 1, YT - 1),
    ):
        low, high = unfolded(value)
        resid_ref[at : at + 4] = low
        resid_ref[at + 4 : at + RH] = high[0:2]
        resid_ref[border] = resid_ref[border] + q_ref[mine]
        resid_ref[inside] = resid_ref[inside] + high[2]
        for r in range(RH):
            edge_ref[at + r, 0:1] = high[3, r : r + 1]
            edge_ref[at + r, 1:2] = high[3, 8 + r : 9 + r]
    wide_ref[:, :, 0:192] = jnp.where(sub == 7, edge_ref[:, 0:1], resid_ref[:, 0:XH])
    left = folded(wide_ref[...])
    wide_ref[:, :, 0:192] = jnp.where(sub == 0, edge_ref[:, 1:2], resid_ref[:, XT - XH :])
    right = folded(wide_ref[...])
    send1_ref[...] = jnp.where(even_x, right, left)
    send2_ref[...] = jnp.where(even_x, left, right)


def split(value):
    high = value.astype(BF16)
    return high, (value - high.astype(F32)).astype(BF16)


def up_row(mats_ref, factor_ref, dst_ref, layers, step, z, state):
    lane = lax.broadcasted_iota(jnp.int32, (1, 3 * layers), 1)
    base = mats_ref[z * step] * 27
    new = []
    for i in range(3):
        row = jnp.zeros((1, 3 * layers), F32)
        for j in range(3):
            row = jnp.where(lane == j * layers + z, factor_ref[base + i * 3 + j], row)
        for j in range(3):
            row = row + factor_ref[base + 9 + i * 3 + j] * state[j]
        dst_ref[pl.ds(i * layers + z, 1), :] = row
        new.append(row)
    return new


def down_row(mats_ref, factor_ref, dst_ref, layers, step, z, state):
    lane = lax.broadcasted_iota(jnp.int32, (1, 3 * layers), 1)
    base = mats_ref[z * step] * 27
    new = []
    for i in range(3):
        row = jnp.where(lane == i * layers + z, 1.0, 0.0)
        for j in range(3):
            row = row + factor_ref[base + 18 + i * 3 + j] * state[j]
        dst_ref[pl.ds(i * layers + z, 1), :] = row
        new.append(row)
    return new


def couple(sten, which, blocks):
    out = []
    for i in range(3):
        total = None
        for j in range(3):
            at = which * 9 + i * 3 + j
            term = sten[:, at : at + 1] * blocks[j]
            total = term if total is None else total + term
        out.append(total)
    return out


def above_below(block):
    row = lax.broadcasted_iota(jnp.int32, block.shape, 0)
    n = block.shape[0]
    low = jnp.where(row == 0, 0.0, pltpu.roll(block, 1, axis=0))
    high = jnp.where(row == n - 1, 0.0, pltpu.roll(block, n - 1, axis=0))
    return low + high


def store_split(ref, at, rows):
    value = jnp.transpose(jnp.concatenate(rows, axis=0))
    high, low = split(value)
    ref[0, :, at : at + value.shape[1]] = high
    ref[1, :, at : at + value.shape[1]] = low


def lines_kernel(mats_ref, factor_ref, up_ref, down_ref, cup_ref, cdown_ref):
    def step(t, state):
        up, down, cup, cdown = (state[i * 3 : i * 3 + 3] for i in range(4))
        for half in range(2):
            z = 2 * t + half
            up = up_row(mats_ref, factor_ref, up_ref, NZ, 1, z, up)
            down = down_row(mats_ref, factor_ref, down_ref, NZ, 1, NZ - 1 - z, down)
        cup = up_row(mats_ref, factor_ref, cup_ref, NC, 2, t, cup)
        cdown = down_row(mats_ref, factor_ref, cdown_ref, NC, 2, NC - 1 - t, cdown)
        return (*up, *down, *cup, *cdown)

    fine, coarse = (jnp.zeros((1, 3 * n), F32) for n in (NZ, NC))
    lax.fori_loop(0, NC, step, (fine,) * 6 + (coarse,) * 6, unroll=4)


def setup_kernel(
    up_ref, down_ref, cup_ref, cdown_ref, sten_ref, fine_ref, coarse_ref, line_ref, cline_ref
):
    sten = sten_ref[...]
    line_ref[...] = exact(down_ref[...], up_ref[...])
    cline_ref[...] = exact(cdown_ref[...], cup_ref[...])

    def level(sten_part, scale, ref, layers):
        blocks = [ref[i * layers : (i + 1) * layers, :] for i in range(3)]
        lateral = couple(sten_part, 1, blocks)
        diag = couple(sten_part, 0, blocks)
        vert = couple(sten_part, 2, [above_below(block) for block in blocks])
        if scale is not None:
            vert = [scale * part for part in vert]
        wide = blocks[0].shape
        r = lax.broadcasted_iota(jnp.int32, wide, 0)
        q = lax.broadcasted_iota(jnp.int32, wide, 1)
        kept = [
            jnp.where(q == r + i * layers, 1.0, 0.0) - (diag[i] - vert[i]) for i in range(3)
        ]
        return blocks, kept, lateral

    blocks, kept, lateral = level(sten, None, line_ref, NZ)
    store_split(fine_ref, 0, blocks)
    store_split(fine_ref, 256, kept)
    store_split(fine_ref, 512, lateral)

    layer_at = lax.broadcasted_iota(jnp.int32, (NC, NZ), 1) // 2
    pairs = (lax.broadcasted_iota(jnp.int32, (NC, NZ), 0) == layer_at).astype(F32)
    layer_at = lax.broadcasted_iota(jnp.int32, (NZ, NC), 0) // 2
    repeats = (lax.broadcasted_iota(jnp.int32, (NZ, NC), 1) == layer_at).astype(F32)

    def paired(part):
        return [exact(pairs, block) for block in part]

    store_split(fine_ref, 768, paired(kept))
    store_split(fine_ref, 896, paired(lateral))

    coarse_sten = sten_ref[pl.ds(0, NC, stride=2), :]
    cblocks, ckept, clateral = level(coarse_sten, 0.25, cline_ref, NC)
    store_split(coarse_ref, 0, ckept)
    store_split(coarse_ref, 128, clateral)
    spread = [exact(repeats, block) for block in cblocks]
    diag = couple(sten, 0, spread)
    vert = couple(sten, 2, [above_below(block) for block in spread])
    store_split(coarse_ref, 256, spread)
    store_split(coarse_ref, 512, [d - v for d, v in zip(diag, vert)])
    store_split(coarse_ref, 768, couple(sten, 1, spread))


def unless(outside):
    return jnp.where(outside, 0.0, 1.0).astype(F32)


def product(halves, w_ref, at, width):
    high, low = halves
    wh = w_ref[0, :, at : at + width]
    wl = w_ref[1, :, at : at + width]

    def dot(a, b):
        return jnp.dot(a, b, preferred_element_type=F32)

    return dot(high, wh) + (dot(high, wl) + dot(low, wh))


def run_cycle(
    sides,
    spread,
    inside,
    fine_ref,
    coarse_ref,
    r_ref,
    keep_ref,
    sum_ref,
    rc_ref,
    ckeep_ref,
    csum_ref,
):
    def stage(i, src, lo, hi, w_ref, at, emit, size=6):
        ready = lo + 1
        for a in range(lo, hi, size):
            b = min(a + size, hi)
            halves = split(src[a:b].reshape((b - a) * XT, -1))
            if isinstance(at, tuple):
                for start, dst in zip(at, (keep_ref, sides[i])):
                    value = product(halves, w_ref, start, 192)
                    dst[a:b] = value.reshape(b - a, XT, 192)
            else:
                value = product(halves, w_ref, at, 224)
                for start, dst in ((0, ckeep_ref), (128, sides[i])):
                    dst[a:b] = value[:, start : start + 96].reshape(b - a, XT, 96)
            for y in range(ready, a - 1):
                emit(i, y)
            ready = max(ready, a - 1)
        for y in range(ready, hi - 1):
            emit(i, y)

    def next_fine(i, y):
        r_ref[y] = inside(keep_ref[y] + spread(i, y), y)

    def next_coarse(i, y):
        rc_ref[y] = inside(ckeep_ref[y] + spread(i, y), y)

    resid = []

    def last(i, y):
        resid.append(((r_ref[y] - keep_ref[y]) + spread(i, y))[MID])

    own = slice(HALO, HALO + YT)
    near = slice(HALO - 1, HALO + YT + 1)
    sum_ref[...] = r_ref[own, MID]
    for i, lo in ((0, 1), (1, 2)):
        stage(i, r_ref, lo, YW - lo, fine_ref, (256, 512), next_fine)
        sum_ref[...] += r_ref[own, MID]
    stage(2, r_ref, 3, YW - 3, fine_ref, 768, next_coarse)
    stage(3, r_ref, near.start, near.stop, fine_ref, (256, 512), next_fine, 5)
    csum_ref[near] = rc_ref[near]
    for i, lo in ((4, 4), (5, 5)):
        stage(i, rc_ref, lo, YW - lo, coarse_ref, 0, next_coarse)
        csum_ref[near] += rc_ref[near]
    stage(6, csum_ref, near.start, near.stop, coarse_ref, (512, 768), last, 5)
    change = product(split(sum_ref[...].reshape(YT * 16, 192)), fine_ref, 0, 192)
    change = change + product(
        split(csum_ref[own, MID].reshape(YT * 16, 96)), coarse_ref, 256, 192
    )
    return change.reshape(YT, 16, 192), jnp.stack(resid, axis=0)


def rows_inside(value, y):
    gy = lax.axis_index("gy")
    if y < HALO:
        value = value * unless(gy == 0)
    if y >= HALO + YT:
        value = value * unless(gy == lax.axis_size("gy") - 1)
    return value


def middle_kernel(resid_ref, fine_ref, coarse_ref, *refs):
    sides, change_ref, out_ref, scratch = refs[:7], refs[7], refs[8], refs[9:]
    r_ref = scratch[0]

    def spread(i, y):
        mid = sides[i][y]
        return (sides[i][y - 1] + sides[i][y + 1]) + (
            pltpu.roll(mid, 1, axis=0) + pltpu.roll(mid, XT - 1, axis=0)
        )

    for y in range(1, YW - 1):
        r_ref[y] = rows_inside(resid_ref[y - 1], y)
    change_ref[...], out_ref[...] = run_cycle(
        sides, spread, rows_inside, fine_ref, coarse_ref, *scratch
    )


def strips_kernel(resid_ref, edge_ref, x1_ref, x2_ref, fine_ref, coarse_ref, *refs):
    saved, change_ref, mid_ref, out_ref = refs[:7], refs[7], refs[8], refs[9]
    side_ref, cside_ref, scratch = refs[10], refs[11], refs[12:]
    r_ref = scratch[0]
    place, gx = x_slice(), lax.axis_index("gx")
    at_left = unless((gx == 0) & (place == 0))
    at_right = unless((gx == lax.axis_size("gx") - 1) & (place == lax.axis_size("gz") - 1))
    sides = [cside_ref if i in (2, 4, 5) else side_ref for i in range(7)]

    def inside(value, y):
        value = jnp.concatenate(
            [value[0:XH] * at_left, value[XH : 3 * XH], value[3 * XH :] * at_right], axis=0
        )
        return rows_inside(value, y)

    def spread(i, y):
        side = sides[i]
        mid = side[y]
        row = jnp.concatenate([mid[0:16], saved[i][y, MID], mid[16:32]], axis=0)
        row = pltpu.roll(row, 1, axis=0) + pltpu.roll(row, XW - 1, axis=0)
        return (side[y - 1] + side[y + 1]) + jnp.concatenate([row[0:16], row[XT:]], axis=0)

    even_x = place % 2 == 0
    sub = lax.broadcasted_iota(jnp.int32, (RW // 2, XH, 192), 1)
    left = unfolded(jnp.where(even_x, x2_ref[...], x1_ref[...]))
    right = unfolded(jnp.where(even_x, x1_ref[...], x2_ref[...]))
    for half in range(2):
        at = slice(half * (RW // 2), (half + 1) * (RW // 2))
        rows = slice(1 + at.start, 1 + at.stop)
        from_left, from_right = left[half], right[half]
        mine_left, mine_right = edge_ref[at, 0:1], edge_ref[at, 1:2]
        r_ref[rows, 0:XH] = jnp.where(sub >= 2, from_left, 0.0) + jnp.where(
            sub == 7, mine_left, 0.0
        )
        r_ref[rows, XH : 2 * XH] = resid_ref[at, 0:XH] + jnp.where(sub == 0, from_left[:, 0:1], 0.0)
        r_ref[rows, 2 * XH : 3 * XH] = resid_ref[at, XT - XH :] + jnp.where(
            sub == 7, from_right[:, 7:8], 0.0
        )
        r_ref[rows, 3 * XH :] = jnp.where(sub <= 5, from_right, 0.0) + jnp.where(
            sub == 0, mine_right, 0.0
        )
    for y in range(1, YW - 1):
        r_ref[y] = inside(r_ref[y], y)
    change, resid = run_cycle(sides, spread, inside, fine_ref, coarse_ref, *scratch)
    for f, (value, middle) in enumerate(((change, change_ref[...]), (resid, mid_ref[...]))):
        value = jnp.concatenate([value[:, 0:8], middle, value[:, 8:16]], axis=1)
        turned = jnp.transpose(value.reshape(YT * XT, 192))
        for c in range(3):
            for g in range(8):
                rows = turned[c * NZ + g * 8 : c * NZ + g * 8 + 8]
                for h in range(2):
                    at = h * 48 + f * 24 + c * 8
                    out_ref[g, at : at + 8, :] = rows[:, h * 128 : h * 128 + 128]


def cycle_scratch():
    fine, coarse = pltpu.VMEM((YW, XT, 192), F32), pltpu.VMEM((YW, XT, 96), F32)
    return [fine, fine, pltpu.VMEM((YT, 16, 192), F32), coarse, coarse, coarse]


def shape(*dims, dtype=F32):
    return jax.ShapeDtypeStruct(dims, dtype)


def swaps(line, start):
    pairs = [(line[i], line[i + 1]) for i in range(start, len(line) - 1, 2)]
    return pairs + [(b, a) for a, b in pairs]


def on_device(right_side, start_field, layer_material, stiffness, line_factors):
    size_y = lax.axis_size("gy")
    packed = pl.pallas_call(
        pack_kernel,
        out_shape=shape(8 * ROWS, 128),
        in_specs=[HBM, HBM, HBM],
        out_specs=VMEM,
        scratch_shapes=[
            pltpu.VMEM((6, 8, 8, 256), F32),
            pltpu.SMEM((8,), jnp.int32),
            pltpu.SemaphoreType.DMA((6,)),
            pltpu.SemaphoreType.DMA,
        ],
        compiler_params=params(60),
        name="pack",
    )(right_side, start_field, layer_material)
    got = lax.all_to_all(packed.reshape(8, ROWS, 128), "gz", 0, 0, tiled=True)
    mats = got[:, 96:, 0].reshape(-1).astype(jnp.int32)

    table = jnp.pad(stiffness.reshape(-1, 27), ((0, 128 - stiffness.shape[0]), (0, 128 - 27)))
    own, q, sten, send1, send2 = pl.pallas_call(
        turn_kernel,
        out_shape=(
            shape(YT, XT, 192),
            shape(YT, XT, 192),
            shape(NZ, 128),
            shape(4, XT, 384),
            shape(4, XT, 384),
        ),
        in_specs=[VMEM, VMEM],
        out_specs=(VMEM,) * 5,
        scratch_shapes=[pltpu.VMEM((8, XT, 384), F32), pltpu.VMEM((8, XT, 384), F32)],
        compiler_params=params(),
        name="turn",
    )(got, table)
    lines = pl.pallas_call(
        lines_kernel,
        out_shape=(shape(192, 192), shape(192, 192), shape(96, 96), shape(96, 96)),
        in_specs=[SMEM, SMEM],
        out_specs=(VMEM,) * 4,
        compiler_params=params(),
        name="lines",
    )(mats, line_factors.reshape(-1))
    fine, coarse = pl.pallas_call(
        setup_kernel,
        out_shape=(shape(2, 192, 1024, dtype=BF16), shape(2, 96, 1024, dtype=BF16)),
        in_specs=[VMEM] * 5,
        out_specs=(VMEM, VMEM),
        scratch_shapes=[pltpu.VMEM((192, 192), F32), pltpu.VMEM((96, 96), F32)],
        compiler_params=params(),
        name="setup",
    )(*lines, sten)
    count_x, count_y, count_z = (lax.axis_size(axis) for axis in ("gx", "gy", "gz"))
    y1 = lax.ppermute(send1, "gy", swaps(range(count_y), 0))
    y2 = lax.ppermute(send2, "gy", swaps(range(count_y), 1))
    resid, edge, send1, send2 = pl.pallas_call(
        sides_kernel,
        out_shape=(
            shape(RW, XT, 192),
            shape(RW, XH, 192),
            shape(RW // 2, XH, 384),
            shape(RW // 2, XH, 384),
        ),
        in_specs=[VMEM, VMEM, VMEM, VMEM, pl.BlockSpec(memory_space=pl.ANY)],
        out_specs=(VMEM,) * 4,
        scratch_shapes=[pltpu.VMEM((RW, XH, 384), F32)],
        compiler_params=params(),
        name="sides",
    )(own, q, y1, y2, fine)
    along = [
        (count_z - 1 - i if x % 2 else i) * count_x + x
        for x in range(count_x)
        for i in range(count_z)
    ]
    x1 = lax.ppermute(send1, ("gz", "gx"), swaps(along, 0))
    x2 = lax.ppermute(send2, ("gz", "gx"), swaps(along, 1))

    sides = tuple(shape(YW, XT, 96 if i in (2, 4, 5) else 192) for i in range(7))
    middle = pl.pallas_call(
        middle_kernel,
        out_shape=(*sides, shape(YT, 16, 192), shape(YT, 16, 192)),
        in_specs=[VMEM] * 3,
        out_specs=(VMEM,) * 9,
        scratch_shapes=cycle_scratch(),
        compiler_params=params(),
        name="middle",
    )(resid, fine, coarse)
    out = pl.pallas_call(
        strips_kernel,
        out_shape=shape(8, 96, 128),
        in_specs=[VMEM] * 15,
        out_specs=VMEM,
        scratch_shapes=[
            pltpu.VMEM((YW, XT, 192), F32),
            pltpu.VMEM((YW, XT, 96), F32),
            *cycle_scratch(),
        ],
        compiler_params=params(),
        name="strips",
    )(resid, edge, x1, x2, fine, coarse, *middle)
    back = lax.all_to_all(out, "gz", 0, 0, tiled=True)
    return pl.pallas_call(
        unpack_kernel,
        out_shape=(shape(8, 3, 8, 256), shape(8, 3, 8, 256)),
        in_specs=[VMEM, VMEM],
        out_specs=(HBM, HBM),
        scratch_shapes=[pltpu.VMEM((2, 8, 3, 8, 256), F32), pltpu.SemaphoreType.DMA((2,))],
        compiler_params=params(),
        name="unpack",
    )(back.reshape(768, 128), start_field)


def solution(mesh):
    return jax.shard_map(
        on_device,
        mesh=mesh,
        in_specs=(P("gz", None, "gy", "gx"), P("gz", None, "gy", "gx"), P("gz"), P(), P()),
        out_specs=(P("gz", None, "gy", "gx"), P("gz", None, "gy", "gx")),
        check_vma=False,
    )
```
